32 devices in a mesh: lat: 8 (over z, y), wall: 4 (over x, core).
Axes of the slice: x: 2, y: 2, z: 4, core: 2. Of those that a mesh axis runs over, the one named last changes fastest.
Arguments:
- populations: float32 [19, 128, 32, 128], P(None, 'wall', 'lat'), may hold values from 0.0138 to 0.5, as said below
- concentration: float32 [128, 4, 32, 128], P('wall', None, 'lat'), may hold values from 0.2 to 2
- cell_flags: int32 [128, 32, 128], P('wall', 'lat'), may hold values from 0 to 2, as said below
- valence: int32 [4], replicated, may hold values from -2 to 2, as said below
- diffusivity: float32 [4], replicated, may hold values from 1000 to 4000
- applied_field: float32 [3], replicated, may hold values from -1 to 1
Outputs:
- new_populations: float32 [19, 128, 32, 128], P(None, 'wall', 'lat')
- new_concentration: float32 [128, 4, 32, 128], P('wall', None, 'lat')
The draws below stay inside these ranges and needn't reach their ends.
Inputs may be any that keep to these rules, and one draw needn't show every extreme that they name: `populations`: each population is its lattice weight times a factor between 0.5 and 1.5. `cell_flags`: cells at the first and last wall-normal index and at the first and last index of the split lateral dimension are 1; every wall-normal index z with z % 16 == 8 is 2 away from those; other cells are 0 or 1. `valence`: each entry is -2, -1, 1 or 2; two species are positive and two negative, and one species of each sign has magnitude 2.
All inputs are finite; a program needn't handle non-finite values.
Results may differ from the reference program's by a relative error of at most 0.0003.
Values sent between devices are 32-bit elements; how exact they have to be, the bound alone decides.
No kernel may reach another device: no remote copies, remote signals or barrier semaphores. Data moves between devices by JAX's collectives and lax.ppermute only.
A program may use at most 64 MiB of HBM per device.

```python
import math
import jax
import jax.numpy as jnp
from jax import lax

SPECIES = 4
NY = 128
NZ = 128
NX = 32


lattice_wts = tuple([1.0 / 3.0] + [1.0 / 18.0] * 6 + [1.0 / 36.0] * 12)


def draw_populations(key, part):
    weights = jnp.array(lattice_wts, dtype=jnp.float32)[:, None, None, None]
    factor = 1.0 + 0.25 * jnp.clip(jax.random.normal(key, (19, NZ, NX, NY), jnp.float32), -2.0, 2.0)
    return (weights * factor).astype(jnp.float32)


def draw_cell_flags(key, part):
    depth_idx = jnp.arange(NZ, dtype=jnp.int32)[:, None, None]
    across = jnp.arange(NX, dtype=jnp.int32)[None, :, None]
    obstacles = jax.random.randint(key, (NZ, NX, NY), 0, 40) == 0
    boundary = (depth_idx == 0) | (depth_idx == NZ - 1) | (across == 0) | (across == NX - 1)
    planes = depth_idx % 16 == 8
    return jnp.where(boundary, 1, jnp.where(planes, 2, jnp.where(obstacles, 1, 0))).astype(jnp.int32)


def draw_valence(key, part):
    first_key, second_key = jax.random.split(key)
    position = jnp.arange(SPECIES, dtype=jnp.int32)
    magnitude = jax.random.randint(first_key, (SPECIES,), 1, 3)
    magnitude = jnp.where(position < 2, 2, magnitude)
    signs = jnp.where(position % 2 == 0, 1, -1)
    order = jax.random.permutation(second_key, SPECIES)
    return (magnitude * signs)[order].astype(jnp.int32)


def shard_levels(key, shape, cuts, low, high):
    level = 1.0
    for dim, shards_of in cuts:
        heights = jax.random.uniform(jax.random.fold_in(jax.random.fold_in(key, 6), dim), (shards_of,), jnp.float32, low / len(cuts), high / len(cuts))
        level = level * jnp.repeat(jnp.exp(heights), shape[dim] // shards_of).reshape((-1,) + (1,) * (len(shape) - 1 - dim))
    return level


def setup_inputs(seed: int = 0) -> dict:
    key_of = jax.random.split(jax.random.key(seed), 7)
    populations = draw_populations(jax.random.fold_in(key_of[6], 71), 0)
    concentration = jnp.clip(jnp.exp(math.log(2.0) - 2.3025851 * jax.random.uniform(key_of[1], (NZ, SPECIES, NX, NY), jnp.float32) ** shard_levels(key_of[1], (NZ, SPECIES, NX, NY), ((0, 4), (2, 8)), -0.2, 0.2)), 0.2, 2.0)
    cell_flags = draw_cell_flags(jax.random.fold_in(key_of[6], 71), 0)
    valence = draw_valence(jax.random.fold_in(key_of[6], 71), 0)
    diffusivity = jnp.clip(jnp.exp(jax.random.uniform(key_of[4], (SPECIES,), jnp.float32, math.log(1000.0), math.log(4000.0))), 1000.0, 4000.0)
    applied_field = jnp.clip(jax.random.uniform(key_of[5], (3,), jnp.float32, -1.0, 1.0), -1.0, 1.0)
    return dict(populations=populations, concentration=concentration, cell_flags=cell_flags, valence=valence, diffusivity=diffusivity, applied_field=applied_field)


lattice_dirs = ((0, 0, 0), (1, 0, 0), (-1, 0, 0), (0, 1, 0), (0, -1, 0), (0, 0, 1), (0, 0, -1),
                (1, 1, 0), (-1, -1, 0), (1, -1, 0), (-1, 1, 0), (1, 0, 1), (-1, 0, -1), (1, 0, -1),
                (-1, 0, 1), (0, 1, 1), (0, -1, -1), (0, 1, -1), (0, -1, 1))
lattice_wts = tuple([1.0 / 3.0] + [1.0 / 18.0] * 6 + [1.0 / 36.0] * 12)
opposite = (0, 2, 1, 4, 3, 6, 5, 8, 7, 10, 9, 12, 11, 14, 13, 16, 15, 18, 17)
relax_time = 0.8
force_gain = 0.02


def collide(populations, concentration, cell_flags, valence, applied_field):
    density = jnp.sum(populations, axis=0)
    charge = jnp.sum(valence.astype(jnp.float32)[None, :, None, None] * concentration, axis=1)
    body_force = [force_gain * charge * applied_field[axis_num] for axis_num in range(3)]
    momentum = [sum(populations[dir_idx] * lattice_dirs[dir_idx][axis_num] for dir_idx in range(19) if lattice_dirs[dir_idx][axis_num] != 0) for axis_num in range(3)]
    velocity = [(momentum[axis_num] + 0.5 * body_force[axis_num]) / density for axis_num in range(3)]
    speed_sq = velocity[0] * velocity[0] + velocity[1] * velocity[1] + velocity[2] * velocity[2]
    is_solid = cell_flags != 0
    outputs = []
    for dir_idx in range(19):
        lattice_vec = lattice_dirs[dir_idx]
        weight = lattice_wts[dir_idx]
        projected = lattice_vec[0] * velocity[0] + lattice_vec[1] * velocity[1] + lattice_vec[2] * velocity[2]
        force_along = lattice_vec[0] * body_force[0] + lattice_vec[1] * body_force[1] + lattice_vec[2] * body_force[2]
        force_rel = sum((lattice_vec[axis_num] - velocity[axis_num]) * body_force[axis_num] for axis_num in range(3))
        forcing = 3.0 * force_rel + 9.0 * projected * force_along
        equilibrium = weight * density * (1.0 + 3.0 * projected + 4.5 * projected * projected - 1.5 * speed_sq)
        relaxed = populations[dir_idx] - (populations[dir_idx] - equilibrium) / relax_time + (1.0 - 0.5 / relax_time) * weight * forcing
        outputs.append(jnp.where(is_solid, populations[opposite[dir_idx]], relaxed))
    return jnp.stack(outputs), velocity[2]


def ion_coefficients(concentration, padded_conc, cell_flags, valence, diffusivity, applied_field, vel_z, first_row, last_row):
    charge_num = valence.astype(jnp.float32)[None, :, None, None]
    membrane = jnp.where(charge_num > 0, 0.5, 0.02)
    flag_cells = cell_flags[:, None, :, :]
    factor = jnp.where(flag_cells == 0, 1.0, jnp.where(flag_cells == 1, 0.01, membrane))
    spread = diffusivity[None, :, None, None] * factor
    drift_vel = spread * jnp.tanh(2.0 * vel_z[:, None, :, :] + charge_num * applied_field[2])
    lower_w = spread + 0.5 * drift_vel
    upper_w = spread - 0.5 * drift_vel
    explicit = concentration + 0.5 * (lower_w * padded_conc[:-2] - 2.0 * spread * concentration + upper_w * padded_conc[2:])
    sub_diag = jnp.where(first_row[:, None, None, None], 0.0, -0.5 * lower_w)
    sup_diag = jnp.where(last_row[:, None, None, None], 0.0, -0.5 * upper_w)
    main_diag = 1.0 + spread
    return sub_diag, main_diag, sup_diag, explicit


def forward_sweep(sub_diag, main_diag, sup_diag, right_side, prev_c, prev_d):
    def advance(carry_in, row_vals):
        carry_c, carry_d = carry_in
        sub_val, middle, sup_val, rhs_val = row_vals
        pivot_val = middle - sub_val * carry_c
        next_c = sup_val / pivot_val
        next_d = (rhs_val - sub_val * carry_d) / pivot_val
        return (next_c, next_d), (next_c, next_d)
    _, (sweep_c, sweep_d) = lax.scan(advance, (prev_c, prev_d), (sub_diag, main_diag, sup_diag, right_side))
    return sweep_c, sweep_d


def backward_sweep(sweep_c, sweep_d, last_x):
    def retreat(next_x, row_vals):
        ratio_val, rhs_val = row_vals
        this_x = rhs_val - ratio_val * next_x
        return this_x, this_x
    _, solved = lax.scan(retreat, last_x, (sweep_c, sweep_d), reverse=True)
    return solved


def thomas(sub_diag, main_diag, sup_diag, right_side):
    zero_line = jnp.zeros_like(right_side[0])
    sweep_c, sweep_d = forward_sweep(sub_diag, main_diag, sup_diag, right_side, zero_line, zero_line)
    return backward_sweep(sweep_c, sweep_d, zero_line)


def propagate(collided):
    padded = jnp.pad(collided, ((0, 0), (1, 1), (1, 1), (0, 0)))
    moved = []
    for dir_idx in range(19):
        step_x, step_y, step_z = lattice_dirs[dir_idx]
        piece_view = padded[dir_idx, 1 - step_z:1 - step_z + NZ, 1 - step_x:1 - step_x + NX, :]
        moved.append(jnp.roll(piece_view, step_y, axis=-1))
    return jnp.stack(moved)


def reference(populations, concentration, cell_flags, valence, diffusivity, applied_field):
    collided, vel_z = collide(populations, concentration, cell_flags, valence, applied_field)
    new_populations = propagate(collided)
    depth_rows = jnp.arange(NZ, dtype=jnp.int32)
    padded_conc = jnp.pad(concentration, ((1, 1), (0, 0), (0, 0), (0, 0)))
    sub_diag, main_diag, sup_diag, explicit = ion_coefficients(concentration, padded_conc, cell_flags, valence, diffusivity, applied_field, vel_z, depth_rows == 0, depth_rows == NZ - 1)
    new_concentration = thomas(sub_diag, main_diag, sup_diag, explicit)
    return new_populations, new_concentration
```

```python
import functools

import jax
import jax.numpy as jnp
from jax import lax
from jax.experimental import pallas as pl
from jax.experimental.pallas import tpu as pltpu
from jax.sharding import PartitionSpec as P

lattice_dirs = (
    (0, 0, 0),
    (1, 0, 0),
    (-1, 0, 0),
    (0, 1, 0),
    (0, -1, 0),
    (0, 0, 1),
    (0, 0, -1),
    (1, 1, 0),
    (-1, -1, 0),
    (1, -1, 0),
    (-1, 1, 0),
    (1, 0, 1),
    (-1, 0, -1),
    (1, 0, -1),
    (-1, 0, 1),
    (0, 1, 1),
    (0, -1, -1),
    (0, 1, -1),
    (0, -1, 1),
)
DIRS = len(lattice_dirs)
FORCE_GAIN = 0.02
X_CELLS = 4
SPECIES = 4
LANES = 128
F32 = jnp.float32

x_plus = tuple(q for q in range(DIRS) if lattice_dirs[q][0] == 1)
x_minus = tuple(q for q in range(DIRS) if lattice_dirs[q][0] == -1)
z_plus = tuple(q for q in range(DIRS) if lattice_dirs[q][2] == 1)
z_minus = tuple(q for q in range(DIRS) if lattice_dirs[q][2] == -1)
FACE_ROWS = 24

VMEM_SPEC = pl.BlockSpec(memory_space=pltpu.VMEM)
SMEM_SPEC = pl.BlockSpec(memory_space=pltpu.SMEM)
ANY_SPEC = pl.BlockSpec(memory_space=pl.ANY)


def on_chip(*shape, dtype=F32):
    return pltpu.VMEM(shape, dtype)


def params():
    return pltpu.CompilerParams(vmem_limit_bytes=24 * 1024 * 1024)


def cost(flops, nbytes):
    return pl.CostEstimate(flops=flops, bytes_accessed=nbytes, transcendentals=0)


def pin(*arrays):
    return [pltpu.with_memory_space_constraint(a, pltpu.VMEM) for a in arrays]


def out_even(q):
    step_x, _, step_z = lattice_dirs[q]
    return {0: 12, 1: 16, -1: 8}[step_z] + (0 if step_x > 0 else 3)


def out_odd(q):
    step_x, _, step_z = lattice_dirs[q]
    return {0: 8, 1: 12, -1: 4}[step_z] + (0 if step_x > 0 else 3)


def low_rows():
    return lax.broadcasted_iota(jnp.int32, (8, LANES), 0) < 4


def collide_kernel(
    pops_hbm,
    conc_hbm,
    flags_hbm,
    valence,
    field,
    moved,
    even_msg,
    odd_msg,
    vel_z,
    conc,
    flags,
    pops,
    sems,
    *,
    tiles,
    chunks,
):
    per = tiles // chunks * 8
    copies = []
    flag_copy = pltpu.make_async_copy(flags_hbm, flags, sems.at[0])
    flag_copy.start()
    for c in range(chunks):
        rows = pl.ds(c * per, per)
        crows = pl.ds(c * per * SPECIES, per * SPECIES)
        pair = (
            pltpu.make_async_copy(conc_hbm.at[crows], conc.at[crows], sems.at[1 + 2 * c]),
            pltpu.make_async_copy(pops_hbm.at[:, rows], pops.at[:, rows], sems.at[2 + 2 * c]),
        )
        for copy in pair:
            copy.start()
        copies.append(pair)
    low = low_rows()
    val_pair = [
        jnp.where(low, valence[2 * h].astype(F32), valence[2 * h + 1].astype(F32))
        for h in range(2)
    ]
    field_xyz = [FORCE_GAIN * field[axis] for axis in range(3)]
    zero = jnp.zeros((8, LANES), F32)
    held = {q: zero for q in z_plus + z_minus}
    flag_copy.wait()
    for k in range(tiles):
        if k % (tiles // chunks) == 0:
            for copy in copies[k // (tiles // chunks)]:
                copy.wait()
        p = [pops[q, pl.ds(8 * k, 8)] for q in range(DIRS)]
        solid = flags[pl.ds(8 * k, 8)] != 0
        sums = []
        for z in range(2):
            part = val_pair[0] * conc[pl.ds(32 * k + 16 * z, 8)]
            part = part + val_pair[1] * conc[pl.ds(32 * k + 16 * z + 8, 8)]
            sums.append(part + pltpu.roll(part, 4, axis=0))
        charge = jnp.where(low, sums[0], sums[1])
        force = [charge * f for f in field_xyz]
        diff = {q: p[q] - p[q + 1] for q in range(1, DIRS, 2)}
        total = {q: p[q] + p[q + 1] for q in range(1, DIRS, 2)}
        density = (
            (p[0] + total[1])
            + (total[3] + total[5])
            + (total[7] + total[9])
            + (total[11] + total[13])
            + (total[15] + total[17])
        )
        momentum = [
            (diff[1] + diff[7]) + (diff[9] + diff[11]) + diff[13],
            (diff[3] + diff[7]) - (diff[9] - diff[15]) + diff[17],
            (diff[5] + diff[11]) - (diff[13] - diff[15]) - diff[17],
        ]
        inverse = 1.0 / density
        vel = [(momentum[a] + 0.5 * force[a]) * inverse for a in range(3)]
        vel_z[pl.ds(8 * k, 8)] = vel[2]
        speed_sq = vel[0] * vel[0] + vel[1] * vel[1] + vel[2] * vel[2]
        work = vel[0] * force[0] + vel[1] * force[1] + vel[2] * force[2]
        base = (1.25 * density) * (1.0 - 1.5 * speed_sq) - 1.125 * work
        odd36 = [(3.75 / 36.0) * density * vel[a] + (1.125 / 36.0) * force[a] for a in range(3)]
        even36 = [(5.625 / 36.0) * density * vel[a] + (3.375 / 36.0) * force[a] for a in range(3)]
        base36 = base * (1.0 / 36.0)
        base18 = base * (1.0 / 18.0)
        for q in range(DIRS):
            if q == 0:
                results = [(0, -0.25 * p[0] + base * (1.0 / 3.0), p[0])]
            elif q % 2 == 1:
                axes = [(a, lattice_dirs[q][a]) for a in range(3) if lattice_dirs[q][a]]

                def along(v):
                    out = v[axes[0][0]]
                    for a, sign in axes[1:]:
                        out = out + v[a] if sign > 0 else out - v[a]
                    return out

                cu, odd, even = along(vel), along(odd36), along(even36)
                if len(axes) == 1:
                    shared = base18 + 2.0 * (cu * even)
                    odd = 2.0 * odd
                else:
                    shared = base36 + cu * even
                results = [
                    (q, (shared + odd) - 0.25 * p[q], p[q + 1]),
                    (q + 1, (shared - odd) - 0.25 * p[q + 1], p[q]),
                ]
            else:
                continue
            for d, relaxed, bounced in results:
                step_x, step_y, step_z = lattice_dirs[d]
                value = jnp.where(solid, bounced, relaxed)
                if step_y:
                    value = pltpu.roll(value, step_y % LANES, axis=1)
                shift = (step_x + 4 * step_z) % 8
                if shift:
                    value = pltpu.roll(value, shift, axis=0)
                if step_z == 0:
                    moved[d, pl.ds(8 + 8 * k, 8)] = value
                else:
                    at = 8 + 8 * k if step_z > 0 else 8 * k
                    moved[d, pl.ds(at, 8)] = jnp.where(low, held[d], value)
                    held[d] = value
    for d in z_plus + z_minus:
        at = 8 + 8 * tiles if lattice_dirs[d][2] > 0 else 8 * tiles
        moved[d, pl.ds(at, 8)] = jnp.where(low, held[d], zero)

    def pack(target, dirs):
        for j, q in enumerate(dirs):
            target[pl.ds(2 * tiles * j, tiles)] = moved[q, pl.ds(out_even(q), tiles, stride=8)]
            target[pl.ds(2 * tiles * j + tiles, tiles)] = moved[
                q, pl.ds(out_odd(q), tiles, stride=8)
            ]

    is_odd = lax.rem(lax.axis_index("lat"), 2) == 1

    @pl.when(jnp.logical_not(is_odd))
    def _():
        pack(even_msg, x_plus)
        pack(odd_msg, x_minus)

    @pl.when(is_odd)
    def _():
        pack(even_msg, x_minus)
        pack(odd_msg, x_plus)


def reciprocal(x):
    return 1.0 / x


def eliminate_kernel(
    vel_z, conc, flags, valence, diffusivity, field, offset, edge, link, ends, *, rows
):
    low = low_rows()
    half = rows // 2
    for h in range(2):
        val = jnp.where(low, valence[2 * h].astype(F32), valence[2 * h + 1].astype(F32))
        diff = jnp.where(low, diffusivity[2 * h], diffusivity[2 * h + 1])
        slow = diff * 0.01
        membrane = diff * jnp.where(val > 0, 0.5, 0.02)
        pull = val * field[2]

        def coefficients(z):
            tile = pl.ds(8 * (z // 2), 8)
            vz, flag = vel_z[tile], flags[tile]
            mine = low if z % 2 == 0 else jnp.logical_not(low)
            vz = jnp.where(mine, vz, pltpu.roll(vz, 4, axis=0))
            flag = jnp.where(mine, flag, pltpu.roll(flag, 4, axis=0))
            spread = jnp.where(flag == 0, diff, jnp.where(flag == 1, slow, membrane))
            drift = spread * jnp.tanh(2.0 * vz + pull)
            lower = 0.5 * spread + 0.25 * drift
            upper = 0.5 * spread - 0.25 * drift
            here = conc[pl.ds(16 * z + 8 * h, 8)]
            rhs = here - spread * here
            if z > 0:
                rhs = rhs + lower * conc[pl.ds(16 * (z - 1) + 8 * h, 8)]
            if z < rows - 1:
                rhs = rhs + upper * conc[pl.ds(16 * (z + 1) + 8 * h, 8)]
            return 1.0 + spread, lower, upper, rhs

        state = {}
        for z_up in range(half):
            for side in range(2):
                z = z_up if side == 0 else rows - 1 - z_up
                main, lower, upper, rhs = coefficients(z)
                back, ahead = (lower, upper) if side == 0 else (upper, lower)
                if z_up == 0:
                    r = reciprocal(main)
                    d, e, k = rhs * r, back * r, ahead * r
                    first = (d, e, k)
                else:
                    d, e, k, first = state[side]
                    r = reciprocal(main - back * k)
                    d, e, k = (rhs + back * d) * r, (back * e) * r, ahead * r
                    first = (first[0] + first[2] * d, first[1] + first[2] * e, first[2] * k)
                state[side] = (d, e, k, first)
                at = pl.ds(16 * z + 8 * h, 8)
                offset[at] = d
                edge[at] = e
                link[at] = k
        (d0, e0, k0, first), (d1, e1, k1, last) = state[0], state[1]
        r = reciprocal(1.0 - k0 * k1)
        high = ((d1 + k1 * d0) * r, (k1 * e0) * r, e1 * r)
        below = ((d0 + k0 * d1) * r, e0 * r, (k0 * e1) * r)
        values = (
            conc[pl.ds(8 * h, 8)] + first[0] + first[2] * high[0],
            first[1] + first[2] * high[1],
            first[2] * high[2],
            conc[pl.ds(16 * (rows - 1) + 8 * h, 8)] + last[0] + last[2] * below[0],
            last[2] * below[1],
            last[1] + last[2] * below[2],
        )
        for j, value in enumerate(values):
            ends[pl.ds(16 * j + 8 * h, 8)] = value


def bit(wall, r):
    return lax.rem(lax.div(wall, 2**r), 2)


def read_ends(ref, h, n=6):
    return [ref[pl.ds(16 * j + 8 * h, 8)] for j in range(n)]


def ordered(own, got, is_upper):
    return (
        [jnp.where(is_upper, g, o) for o, g in zip(own, got)],
        [jnp.where(is_upper, o, g) for o, g in zip(own, got)],
    )


def merge(a, b):
    r = reciprocal(1.0 - a[5] * b[1])
    top_a = ((a[3] + a[5] * b[0]) * r, a[4] * r, (a[5] * b[2]) * r)
    low_b = ((b[0] + b[1] * a[3]) * r, (b[1] * a[4]) * r, b[2] * r)
    merged = (
        a[0] + a[2] * low_b[0],
        a[1] + a[2] * low_b[1],
        a[2] * low_b[2],
        b[3] + b[4] * top_a[0],
        b[4] * top_a[1],
        b[5] + b[4] * top_a[2],
    )
    return top_a, low_b, merged


def relay_kernel(*refs, tiles, level, last):
    own, got, moved, even_got, odd_got = refs[:5]
    up_msg = refs[5]
    pair_msg = refs[6] if level == 0 else None
    wall, lat = lax.axis_index("wall"), lax.axis_index("lat")
    lats = lax.axis_size("lat")
    is_upper = bit(wall, level) == 1
    next_upper = bit(wall, level + 1) == 1
    for h in range(2):
        a, b = ordered(read_ends(own, h), read_ends(got, h), is_upper)
        merged = merge(a, b)[2]
        if last:
            send = [
                jnp.where(next_upper, merged[0], merged[3]),
                jnp.where(next_upper, merged[1], merged[5]),
            ]
        else:
            send = merged
        for j, value in enumerate(send):
            up_msg[pl.ds(16 * j + 8 * h, 8)] = value
    base = 32 if last else 96
    odd_lat = lax.rem(lat, 2) == 1
    part = 2 * tiles

    def from_lat(q, odd_z, index):
        dirs = x_plus if q in x_plus else x_minus
        j = dirs.index(q)
        at = pl.ds(part * j + (tiles if odd_z else 0) + index, 1)
        use_even = odd_lat if q in x_plus else jnp.logical_not(odd_lat)
        exists = lat > 0 if q in x_plus else lat < lats - 1
        row = jnp.where(use_even, even_got[at], odd_got[at])
        return jnp.where(exists, row, 0.0)

    def faces(target, start, dirs):
        for j, q in enumerate(dirs):
            up = lattice_dirs[q][2] > 0
            rows = pl.ds(8 * tiles + 8, 4) if up else pl.ds(4, 4)
            target[pl.ds(start + 4 * j, 4)] = moved[q, rows]
            step_x = lattice_dirs[q][0]
            if step_x:
                at = start + 4 * j + (0 if step_x > 0 else 3)
                target[pl.ds(at, 1)] = from_lat(q, up, tiles - 1 if up else 0)
        target[pl.ds(start + 20, 4)] = jnp.zeros((4, LANES), F32)

    for target, start, flag in (
        ((up_msg, base, next_upper), (pair_msg, 0, is_upper))
        if level == 0
        else ((up_msg, base, next_upper),)
    ):

        @pl.when(jnp.logical_not(flag))
        def _(target=target, start=start):
            faces(target, start, z_plus)

        @pl.when(flag)
        def _(target=target, start=start):
            faces(target, start, z_minus)


def spread_kernel(moved, even_got, odd_got, after, out_hbm, tops, patched, sems, *, tiles):
    del after
    lat, lats = lax.axis_index("lat"), lax.axis_size("lat")
    odd_lat = lax.rem(lat, 2) == 1
    body = pl.ds(8, 8 * tiles)
    copies = []
    for q in range(DIRS):
        if lattice_dirs[q][0] == 0:
            copies.append(pltpu.make_async_copy(moved.at[q, body], out_hbm.at[q], sems.at[q]))
            copies[-1].start()
    order = {q: j for j, q in enumerate(x_plus + x_minus)}

    def fill(dirs, got, keep):
        for j, q in enumerate(dirs):
            for k in range(tiles + 2):
                patched[order[q], pl.ds(8 * k, 8)] = moved[q, pl.ds(8 * k, 8)]
            even_z = got[pl.ds(2 * tiles * j, tiles)]
            odd_z = got[pl.ds(2 * tiles * j + tiles, tiles)]
            patched[order[q], pl.ds(out_odd(q), tiles, stride=8)] = jnp.where(keep, even_z, 0.0)
            patched[order[q], pl.ds(out_even(q), tiles, stride=8)] = jnp.where(keep, odd_z, 0.0)

    @pl.when(odd_lat)
    def _():
        fill(x_plus, even_got, lat > 0)
        fill(x_minus, odd_got, lat < lats - 1)

    @pl.when(jnp.logical_not(odd_lat))
    def _():
        fill(x_plus, odd_got, lat > 0)
        fill(x_minus, even_got, lat < lats - 1)

    for q in x_plus + x_minus:
        copies.append(
            pltpu.make_async_copy(patched.at[order[q], body], out_hbm.at[q], sems.at[q])
        )
        copies[-1].start()
    for j, q in enumerate(z_plus + z_minus):
        rows = pl.ds(8, 8) if lattice_dirs[q][2] > 0 else pl.ds(8 * tiles, 8)
        tops[pl.ds(8 * j, 8)] = patched[order[q], rows] if q in order else moved[q, rows]
    for copy in copies:
        copy.wait()


def finish_kernel(*refs, rows, tiles, levels):
    it = iter(refs)
    owns = [next(it) for _ in range(levels)]
    gots = [next(it) for _ in range(levels)]
    pair_got, offset, edge, link, tops, pops_in = [next(it) for _ in range(6)]
    pops_out, conc_out, solved, tiles_out, sems = [next(it) for _ in range(5)]
    del pops_in
    wall = lax.axis_index("wall")
    copies = []
    for j in range(len(z_plus) + len(z_minus)):
        tiles_out[pl.ds(8 * j, 8)] = tops[pl.ds(8 * j, 8)]

    def put(got, base, lower):
        for j in range(5):
            row = 8 * j if lower else 8 * (5 + j) + 4
            tiles_out[pl.ds(row, 4)] = got[pl.ds(base + 4 * j, 4)]

    pl.when(bit(wall, 0) == 1)(lambda: put(pair_got, 0, True))
    pl.when(bit(wall, 0) == 0)(lambda: put(pair_got, 0, False))
    for r in range(1, levels):
        base = 32 if r == levels - 1 else 96
        rest = lax.rem(wall, 2 ** (r + 1))
        pl.when(rest == 2**r)(functools.partial(put, gots[r], base, True))
        pl.when(rest == 2**r - 1)(functools.partial(put, gots[r], base, False))
    for j, q in enumerate(z_plus + z_minus):
        at = pl.ds(0, 8) if lattice_dirs[q][2] > 0 else pl.ds(8 * tiles - 8, 8)
        copies.append(
            pltpu.make_async_copy(tiles_out.at[pl.ds(8 * j, 8)], pops_out.at[q, at], sems.at[j])
        )
        copies[-1].start()
    half = rows // 2
    inner = []
    for h in range(2):
        top = levels - 1
        go, xo = read_ends(owns[top], h, 2)
        gr, xr = read_ends(gots[top], h, 2)
        w = (gr + xr * go) * reciprocal(1.0 - xo * xr)
        is_upper = bit(wall, top) == 1
        w_low, w_high = jnp.where(is_upper, w, 0.0), jnp.where(is_upper, 0.0, w)
        for r in range(top - 1, -1, -1):
            is_upper = bit(wall, r) == 1
            a, b = ordered(read_ends(owns[r], h), read_ends(gots[r], h), is_upper)
            top_a, low_b, _ = merge(a, b)
            new_low = top_a[0] + top_a[1] * w_low + top_a[2] * w_high
            new_high = low_b[0] + low_b[1] * w_low + low_b[2] * w_high
            w_low, w_high = (
                jnp.where(is_upper, new_low, w_low),
                jnp.where(is_upper, w_high, new_high),
            )
        at0, at1 = pl.ds(16 * (half - 1) + 8 * h, 8), pl.ds(16 * half + 8 * h, 8)
        a0 = offset[at0] + edge[at0] * w_low
        a1 = offset[at1] + edge[at1] * w_high
        k0, k1 = link[at0], link[at1]
        r = reciprocal(1.0 - k0 * k1)
        u0, u1 = (a0 + k0 * a1) * r, (a1 + k1 * a0) * r
        solved[at0] = u0
        solved[at1] = u1
        inner.append([u0, u1, w_low, w_high])
    parts = 2
    step = half // parts
    for part in range(parts):
        for i in range(part * step, (part + 1) * step):
            if i == 0:
                continue
            for h in range(2):
                u0, u1, w_low, w_high = inner[h]
                at0 = pl.ds(16 * (half - 1 - i) + 8 * h, 8)
                at1 = pl.ds(16 * (half + i) + 8 * h, 8)
                u0 = (offset[at0] + edge[at0] * w_low) + link[at0] * u0
                u1 = (offset[at1] + edge[at1] * w_high) + link[at1] * u1
                solved[at0] = u0
                solved[at1] = u1
                inner[h] = [u0, u1, w_low, w_high]
        for side in range(2):
            begin = half - (part + 1) * step if side == 0 else half + part * step
            span = pl.ds(16 * begin, 16 * step)
            copies.append(
                pltpu.make_async_copy(
                    solved.at[span], conc_out.at[span], sems.at[10 + 2 * part + side]
                )
            )
            copies[-1].start()
    for copy in copies:
        copy.wait()


def swaps(lats, walls):
    def pairs(partner):
        table = []
        for lat in range(lats):
            for wall in range(walls):
                to_lat, to_wall = partner(lat, wall)
                table.append((lat * walls + wall, to_lat * walls + to_wall))
        return table

    def odd_partner(lat, wall):
        if lat == 0 or lat == lats - 1:
            return lat, wall ^ 1
        return ((lat + 1) ^ 1) - 1, wall

    even = pairs(lambda lat, wall: (lat ^ 1, wall))
    odd = pairs(odd_partner)
    levels = []
    while 2 ** len(levels) < walls:
        flip = 2 ** (len(levels) + 1) - 1
        levels.append(pairs(lambda lat, wall: (lat, wall ^ flip)))
    return even, odd, levels


def per_device(
    populations, concentration, cell_flags, valence, diffusivity, applied_field, *, lats, walls
):
    rows, cells = populations.shape[1], populations.shape[1] * populations.shape[2]
    tiles = cells // 8
    chunks = 4
    assert populations.shape[2] == X_CELLS and lats % 2 == 0 and walls >= 4
    even, odd, levels = swaps(lats, walls)
    assert 2 ** len(levels) == walls

    def move(x, table):
        return lax.ppermute(x, ("lat", "wall"), table)

    msg_rows = 2 * tiles * 5
    moved, even_msg, odd_msg, vel_z, conc, flags = pl.pallas_call(
        functools.partial(collide_kernel, tiles=tiles, chunks=chunks),
        out_shape=(
            on_chip(DIRS, cells + 16, LANES),
            on_chip(msg_rows, LANES),
            on_chip(msg_rows, LANES),
            on_chip(cells, LANES),
            on_chip(cells * SPECIES, LANES),
            on_chip(cells, LANES, dtype=jnp.int32),
        ),
        in_specs=[ANY_SPEC] * 3 + [SMEM_SPEC] * 2,
        out_specs=(VMEM_SPEC,) * 6,
        scratch_shapes=[
            pltpu.VMEM((DIRS, cells, LANES), F32),
            pltpu.SemaphoreType.DMA((1 + 2 * chunks,)),
        ],
        compiler_params=params(),
        cost_estimate=cost(5_000_000, 3_000_000),
        name="collide",
    )(
        populations.reshape(DIRS, cells, LANES),
        concentration.reshape(cells * SPECIES, LANES),
        cell_flags.reshape(cells, LANES),
        valence,
        applied_field,
    )
    even_got, odd_got = move(even_msg, even), move(odd_msg, odd)

    offset, edge, link, ends = pl.pallas_call(
        functools.partial(eliminate_kernel, rows=rows),
        out_shape=(on_chip(cells * SPECIES, LANES),) * 3 + (on_chip(96, LANES),),
        in_specs=[VMEM_SPEC] * 3 + [SMEM_SPEC] * 3,
        out_specs=(VMEM_SPEC,) * 4,
        compiler_params=params(),
        cost_estimate=cost(5_000_000, 3_000_000),
        name="eliminate",
    )(*pin(vel_z, conc, flags), valence, diffusivity, applied_field)

    owns, gots = [ends], [move(ends, levels[0])]
    pair_got = None
    for level in range(len(levels) - 1):
        last = level == len(levels) - 2
        shapes = (on_chip((32 if last else 96) + FACE_ROWS, LANES),)
        if level == 0:
            shapes += (on_chip(FACE_ROWS, LANES),)
        sent = pl.pallas_call(
            functools.partial(relay_kernel, tiles=tiles, level=level, last=last),
            out_shape=shapes,
            in_specs=[VMEM_SPEC] * 5,
            out_specs=(VMEM_SPEC,) * len(shapes),
            compiler_params=params(),
            cost_estimate=cost(100_000, 200_000),
            name=f"relay{level}",
        )(*pin(owns[-1], gots[-1], moved, even_got, odd_got))
        owns.append(sent[0])
        gots.append(move(sent[0], levels[level + 1]))
        if level == 0:
            pair_got = move(sent[1], levels[0])

    pops_out, tops = pl.pallas_call(
        functools.partial(spread_kernel, tiles=tiles),
        out_shape=(
            jax.ShapeDtypeStruct((DIRS, cells, LANES), F32),
            on_chip(80, LANES),
        ),
        in_specs=[VMEM_SPEC] * 4,
        out_specs=(ANY_SPEC, VMEM_SPEC),
        scratch_shapes=[
            pltpu.VMEM((10, cells + 16, LANES), F32),
            pltpu.SemaphoreType.DMA((DIRS,)),
        ],
        compiler_params=params(),
        cost_estimate=cost(1_000_000, 2_500_000),
        name="spread",
    )(*pin(moved, even_got, odd_got, owns[-1]))

    n_in = 2 * len(levels) + 5
    new_pops, new_conc = pl.pallas_call(
        functools.partial(finish_kernel, rows=rows, tiles=tiles, levels=len(levels)),
        out_shape=(
            jax.ShapeDtypeStruct((DIRS, cells, LANES), F32),
            jax.ShapeDtypeStruct((cells * SPECIES, LANES), F32),
        ),
        in_specs=[VMEM_SPEC] * n_in + [ANY_SPEC],
        out_specs=(ANY_SPEC, ANY_SPEC),
        input_output_aliases={n_in: 0},
        scratch_shapes=[
            pltpu.VMEM((cells * SPECIES, LANES), F32),
            pltpu.VMEM((80, LANES), F32),
            pltpu.SemaphoreType.DMA((14,)),
        ],
        compiler_params=params(),
        cost_estimate=cost(1_000_000, 2_000_000),
        name="finish",
    )(*pin(*owns, *gots, pair_got, offset, edge, link, tops), pops_out)
    return new_pops.reshape(populations.shape), new_conc.reshape(concentration.shape)


def solution(mesh):
    in_specs = (
        P(None, "wall", "lat", None),
        P("wall", None, "lat", None),
        P("wall", "lat", None),
        P(),
        P(),
        P(),
    )
    out_specs = (P(None, "wall", "lat", None), P("wall", None, "lat", None))
    return jax.shard_map(
        functools.partial(per_device, lats=mesh.shape["lat"], walls=mesh.shape["wall"]),
        mesh=mesh,
        in_specs=in_specs,
        out_specs=out_specs,
        check_vma=False,
    )
```

```python
import functools

import jax
import jax.numpy as jnp
from jax import lax
from jax.experimental import pallas as pl
from jax.experimental.pallas import tpu as pltpu
from jax.sharding import PartitionSpec as P

lattice_dirs = (
    (0, 0, 0),
    (1, 0, 0),
    (-1, 0, 0),
    (0, 1, 0),
    (0, -1, 0),
    (0, 0, 1),
    (0, 0, -1),
    (1, 1, 0),
    (-1, -1, 0),
    (1, -1, 0),
    (-1, 1, 0),
    (1, 0, 1),
    (-1, 0, -1),
    (1, 0, -1),
    (-1, 0, 1),
    (0, 1, 1),
    (0, -1, -1),
    (0, 1, -1),
    (0, -1, 1),
)
DIRS = len(lattice_dirs)
FORCE_GAIN = 0.02
X_CELLS = 4
SPECIES = 4
LANES = 128
F32 = jnp.float32

x_plus = tuple(q for q in range(DIRS) if lattice_dirs[q][0] == 1)
x_minus = tuple(q for q in range(DIRS) if lattice_dirs[q][0] == -1)
z_plus = tuple(q for q in range(DIRS) if lattice_dirs[q][2] == 1)
z_minus = tuple(q for q in range(DIRS) if lattice_dirs[q][2] == -1)
FACE_ROWS = 24

VMEM_SPEC = pl.BlockSpec(memory_space=pltpu.VMEM)
ANY_SPEC = pl.BlockSpec(memory_space=pl.ANY)


def on_chip(*shape, dtype=F32):
    return pltpu.VMEM(shape, dtype)


def params():
    return pltpu.CompilerParams(vmem_limit_bytes=24 * 1024 * 1024)


def cost(flops, nbytes):
    return pl.CostEstimate(flops=flops, bytes_accessed=nbytes, transcendentals=0)


def in_hbm(*arrays):
    return [pltpu.with_memory_space_constraint(a, pltpu.HBM) for a in arrays]


def pin(*arrays):
    return [pltpu.with_memory_space_constraint(a, pltpu.VMEM) for a in arrays]


def out_even(q):
    step_x, _, step_z = lattice_dirs[q]
    return {0: 12, 1: 16, -1: 8}[step_z] + (0 if step_x > 0 else 3)


def out_odd(q):
    step_x, _, step_z = lattice_dirs[q]
    return {0: 8, 1: 12, -1: 4}[step_z] + (0 if step_x > 0 else 3)


def low_rows():
    return lax.broadcasted_iota(jnp.int32, (8, LANES), 0) < 4


def collide_kernel(
    pops_hbm,
    conc_hbm,
    flags_hbm,
    valence_hbm,
    diffusivity_hbm,
    field_hbm,
    moved,
    even_msg,
    odd_msg,
    vel_z,
    conc,
    flags,
    table,
    pops,
    valence,
    diffusivity,
    field,
    sems,
    *,
    chunks,
):
    tiles = sum(chunks)
    small = [
        pltpu.make_async_copy(source, target, sems.at[i])
        for i, (source, target) in enumerate(
            (
                (flags_hbm, flags),
                (valence_hbm, valence),
                (field_hbm, field),
                (diffusivity_hbm, diffusivity),
            )
        )
    ]
    for copy in small:
        copy.start()
    copies = {}
    at = 0
    for c, count in enumerate(chunks):
        rows = pl.ds(8 * at, 8 * count)
        crows = pl.ds(8 * SPECIES * at, 8 * SPECIES * count)
        copies[at] = (
            pltpu.make_async_copy(conc_hbm.at[crows], conc.at[crows], sems.at[4 + 2 * c]),
            pltpu.make_async_copy(pops_hbm.at[:, rows], pops.at[:, rows], sems.at[5 + 2 * c]),
        )
        for copy in copies[at]:
            copy.start()
        at += count
    low = low_rows()
    for copy in small:
        copy.wait()
    val_pair = [
        jnp.where(low, valence[2 * h].astype(F32), valence[2 * h + 1].astype(F32))
        for h in range(2)
    ]
    field_xyz = [FORCE_GAIN * field[axis] for axis in range(3)]
    zero = jnp.zeros((8, LANES), F32)
    held = {q: zero for q in z_plus + z_minus}
    for k in range(tiles):
        for copy in copies.get(k, ()):
            copy.wait()
        p = [pops[q, pl.ds(8 * k, 8)] for q in range(DIRS)]
        solid = flags[pl.ds(8 * k, 8)] != 0
        sums = []
        for z in range(2):
            part = val_pair[0] * conc[pl.ds(32 * k + 16 * z, 8)]
            part = part + val_pair[1] * conc[pl.ds(32 * k + 16 * z + 8, 8)]
            sums.append(part + pltpu.roll(part, 4, axis=0))
        charge = jnp.where(low, sums[0], sums[1])
        force = [charge * f for f in field_xyz]
        diff = {q: p[q] - p[q + 1] for q in range(1, DIRS, 2)}
        total = {q: p[q] + p[q + 1] for q in range(1, DIRS, 2)}
        density = (
            (p[0] + total[1])
            + (total[3] + total[5])
            + (total[7] + total[9])
            + (total[11] + total[13])
            + (total[15] + total[17])
        )
        momentum = [
            (diff[1] + diff[7]) + (diff[9] + diff[11]) + diff[13],
            (diff[3] + diff[7]) - (diff[9] - diff[15]) + diff[17],
            (diff[5] + diff[11]) - (diff[13] - diff[15]) - diff[17],
        ]
        inverse = 1.0 / density
        vel = [(momentum[a] + 0.5 * force[a]) * inverse for a in range(3)]
        vel_z[pl.ds(8 * k, 8)] = vel[2]
        speed_sq = vel[0] * vel[0] + vel[1] * vel[1] + vel[2] * vel[2]
        work = vel[0] * force[0] + vel[1] * force[1] + vel[2] * force[2]
        base = (1.25 * density) * (1.0 - 1.5 * speed_sq) - 1.125 * work
        odd36 = [(3.75 / 36.0) * density * vel[a] + (1.125 / 36.0) * force[a] for a in range(3)]
        even36 = [(5.625 / 36.0) * density * vel[a] + (3.375 / 36.0) * force[a] for a in range(3)]
        base36 = base * (1.0 / 36.0)
        base18 = base * (1.0 / 18.0)
        for q in range(DIRS):
            if q == 0:
                results = [(0, -0.25 * p[0] + base * (1.0 / 3.0), p[0])]
            elif q % 2 == 1:
                axes = [(a, lattice_dirs[q][a]) for a in range(3) if lattice_dirs[q][a]]

                def along(v):
                    out = v[axes[0][0]]
                    for a, sign in axes[1:]:
                        out = out + v[a] if sign > 0 else out - v[a]
                    return out

                cu, odd, even = along(vel), along(odd36), along(even36)
                if len(axes) == 1:
                    shared = base18 + 2.0 * (cu * even)
                    odd = 2.0 * odd
                else:
                    shared = base36 + cu * even
                results = [
                    (q, (shared + odd) - 0.25 * p[q], p[q + 1]),
                    (q + 1, (shared - odd) - 0.25 * p[q + 1], p[q]),
                ]
            else:
                continue
            for d, relaxed, bounced in results:
                step_x, step_y, step_z = lattice_dirs[d]
                value = jnp.where(solid, bounced, relaxed)
                if step_y:
                    value = pltpu.roll(value, step_y % LANES, axis=1)
                shift = (step_x + 4 * step_z) % 8
                if shift:
                    value = pltpu.roll(value, shift, axis=0)
                if step_z == 0:
                    moved[d, pl.ds(8 + 8 * k, 8)] = value
                else:
                    at = 8 + 8 * k if step_z > 0 else 8 * k
                    moved[d, pl.ds(at, 8)] = jnp.where(low, held[d], value)
                    held[d] = value
    for d in z_plus + z_minus:
        at = 8 + 8 * tiles if lattice_dirs[d][2] > 0 else 8 * tiles
        moved[d, pl.ds(at, 8)] = jnp.where(low, held[d], zero)

    def pack(target, dirs):
        for j, q in enumerate(dirs):
            target[pl.ds(2 * tiles * j, tiles)] = moved[q, pl.ds(out_even(q), tiles, stride=8)]
            target[pl.ds(2 * tiles * j + tiles, tiles)] = moved[
                q, pl.ds(out_odd(q), tiles, stride=8)
            ]

    is_odd = lax.rem(lax.axis_index("lat"), 2) == 1

    @pl.when(jnp.logical_not(is_odd))
    def _():
        pack(even_msg, x_plus)
        pack(odd_msg, x_minus)

    @pl.when(is_odd)
    def _():
        pack(even_msg, x_minus)
        pack(odd_msg, x_plus)

    for h in range(2):
        diff = jnp.where(low, diffusivity[2 * h], diffusivity[2 * h + 1])
        values = (
            diff,
            diff * 0.01,
            diff * jnp.where(val_pair[h] > 0, 0.5, 0.02),
            val_pair[h] * field[2],
        )
        for j, value in enumerate(values):
            table[pl.ds(8 * (4 * h + j), 8)] = value


def reciprocal(x):
    return 1.0 / x


def eliminate_kernel(
    vel_z, conc, flags, table, offset, edge, link, ends, *, rows
):
    low = low_rows()
    half = rows // 2
    for h in range(2):
        diff, slow, membrane, pull = [table[pl.ds(8 * (4 * h + j), 8)] for j in range(4)]

        def coefficients(z):
            tile = pl.ds(8 * (z // 2), 8)
            vz, flag = vel_z[tile], flags[tile]
            mine = low if z % 2 == 0 else jnp.logical_not(low)
            vz = jnp.where(mine, vz, pltpu.roll(vz, 4, axis=0))
            flag = jnp.where(mine, flag, pltpu.roll(flag, 4, axis=0))
            spread = jnp.where(flag == 0, diff, jnp.where(flag == 1, slow, membrane))
            drift = spread * jnp.tanh(2.0 * vz + pull)
            lower = 0.5 * spread + 0.25 * drift
            upper = 0.5 * spread - 0.25 * drift
            here = conc[pl.ds(16 * z + 8 * h, 8)]
            rhs = here - spread * here
            if z > 0:
                rhs = rhs + lower * conc[pl.ds(16 * (z - 1) + 8 * h, 8)]
            if z < rows - 1:
                rhs = rhs + upper * conc[pl.ds(16 * (z + 1) + 8 * h, 8)]
            return 1.0 + spread, lower, upper, rhs

        state = {}
        for z_up in range(half):
            for side in range(2):
                z = z_up if side == 0 else rows - 1 - z_up
                main, lower, upper, rhs = coefficients(z)
                back, ahead = (lower, upper) if side == 0 else (upper, lower)
                if z_up == 0:
                    r = reciprocal(main)
                    d, e, k = rhs * r, back * r, ahead * r
                    first = (d, e, k)
                else:
                    d, e, k, first = state[side]
                    r = reciprocal(main - back * k)
                    d, e, k = (rhs + back * d) * r, (back * e) * r, ahead * r
                    first = (first[0] + first[2] * d, first[1] + first[2] * e, first[2] * k)
                state[side] = (d, e, k, first)
                at = pl.ds(16 * z + 8 * h, 8)
                offset[at] = d
                edge[at] = e
                link[at] = k
        (d0, e0, k0, first), (d1, e1, k1, last) = state[0], state[1]
        r = reciprocal(1.0 - k0 * k1)
        high = ((d1 + k1 * d0) * r, (k1 * e0) * r, e1 * r)
        below = ((d0 + k0 * d1) * r, e0 * r, (k0 * e1) * r)
        values = (
            conc[pl.ds(8 * h, 8)] + first[0] + first[2] * high[0],
            first[1] + first[2] * high[1],
            first[2] * high[2],
            conc[pl.ds(16 * (rows - 1) + 8 * h, 8)] + last[0] + last[2] * below[0],
            last[2] * below[1],
            last[1] + last[2] * below[2],
        )
        for j, value in enumerate(values):
            ends[pl.ds(16 * j + 8 * h, 8)] = value


def bit(wall, r):
    return lax.rem(lax.div(wall, 2**r), 2)


def read_ends(ref, h, n=6):
    return [ref[pl.ds(16 * j + 8 * h, 8)] for j in range(n)]


def ordered(own, got, is_upper):
    return (
        [jnp.where(is_upper, g, o) for o, g in zip(own, got)],
        [jnp.where(is_upper, o, g) for o, g in zip(own, got)],
    )


def merge(a, b):
    r = reciprocal(1.0 - a[5] * b[1])
    top_a = ((a[3] + a[5] * b[0]) * r, a[4] * r, (a[5] * b[2]) * r)
    low_b = ((b[0] + b[1] * a[3]) * r, (b[1] * a[4]) * r, b[2] * r)
    merged = (
        a[0] + a[2] * low_b[0],
        a[1] + a[2] * low_b[1],
        a[2] * low_b[2],
        b[3] + b[4] * top_a[0],
        b[4] * top_a[1],
        b[5] + b[4] * top_a[2],
    )
    return top_a, low_b, merged


def relay_kernel(*refs, tiles, level, last):
    own, got, moved, even_got, odd_got = refs[:5]
    up_msg = refs[5]
    pair_msg = refs[6] if level == 0 else None
    wall, lat = lax.axis_index("wall"), lax.axis_index("lat")
    lats = lax.axis_size("lat")
    is_upper = bit(wall, level) == 1
    next_upper = bit(wall, level + 1) == 1
    for h in range(2):
        a, b = ordered(read_ends(own, h), read_ends(got, h), is_upper)
        merged = merge(a, b)[2]
        if last:
            send = [
                jnp.where(next_upper, merged[0], merged[3]),
                jnp.where(next_upper, merged[1], merged[5]),
            ]
        else:
            send = merged
        for j, value in enumerate(send):
            up_msg[pl.ds(16 * j + 8 * h, 8)] = value
    base = 32 if last else 96
    odd_lat = lax.rem(lat, 2) == 1
    part = 2 * tiles

    def from_lat(q, odd_z, index):
        dirs = x_plus if q in x_plus else x_minus
        j = dirs.index(q)
        at = pl.ds(part * j + (tiles if odd_z else 0) + index, 1)
        use_even = odd_lat if q in x_plus else jnp.logical_not(odd_lat)
        exists = lat > 0 if q in x_plus else lat < lats - 1
        row = jnp.where(use_even, even_got[at], odd_got[at])
        return jnp.where(exists, row, 0.0)

    def faces(target, start, dirs):
        for j, q in enumerate(dirs):
            up = lattice_dirs[q][2] > 0
            rows = pl.ds(8 * tiles + 8, 4) if up else pl.ds(4, 4)
            target[pl.ds(start + 4 * j, 4)] = moved[q, rows]
            step_x = lattice_dirs[q][0]
            if step_x:
                at = start + 4 * j + (0 if step_x > 0 else 3)
                target[pl.ds(at, 1)] = from_lat(q, up, tiles - 1 if up else 0)
        target[pl.ds(start + 20, 4)] = jnp.zeros((4, LANES), F32)

    for target, start, flag in (
        ((up_msg, base, next_upper), (pair_msg, 0, is_upper))
        if level == 0
        else ((up_msg, base, next_upper),)
    ):

        @pl.when(jnp.logical_not(flag))
        def _(target=target, start=start):
            faces(target, start, z_plus)

        @pl.when(flag)
        def _(target=target, start=start):
            faces(target, start, z_minus)


def spread_kernel(moved, even_got, odd_got, after, out_hbm, tops, patched, sems, *, tiles):
    del after
    lat, lats = lax.axis_index("lat"), lax.axis_size("lat")
    odd_lat = lax.rem(lat, 2) == 1
    body = pl.ds(8, 8 * tiles)
    copies = []
    for q in range(DIRS):
        if lattice_dirs[q][0] == 0:
            copies.append(pltpu.make_async_copy(moved.at[q, body], out_hbm.at[q], sems.at[q]))
            copies[-1].start()
    order = {q: j for j, q in enumerate(x_plus + x_minus)}

    def fill(dirs, got, keep):
        for j, q in enumerate(dirs):
            for k in range(tiles + 2):
                patched[order[q], pl.ds(8 * k, 8)] = moved[q, pl.ds(8 * k, 8)]
            even_z = got[pl.ds(2 * tiles * j, tiles)]
            odd_z = got[pl.ds(2 * tiles * j + tiles, tiles)]
            patched[order[q], pl.ds(out_odd(q), tiles, stride=8)] = jnp.where(keep, even_z, 0.0)
            patched[order[q], pl.ds(out_even(q), tiles, stride=8)] = jnp.where(keep, odd_z, 0.0)

    @pl.when(odd_lat)
    def _():
        fill(x_plus, even_got, lat > 0)
        fill(x_minus, odd_got, lat < lats - 1)

    @pl.when(jnp.logical_not(odd_lat))
    def _():
        fill(x_plus, odd_got, lat > 0)
        fill(x_minus, even_got, lat < lats - 1)

    for q in x_plus + x_minus:
        copies.append(
            pltpu.make_async_copy(patched.at[order[q], body], out_hbm.at[q], sems.at[q])
        )
        copies[-1].start()
    for j, q in enumerate(z_plus + z_minus):
        rows = pl.ds(8, 8) if lattice_dirs[q][2] > 0 else pl.ds(8 * tiles, 8)
        tops[pl.ds(8 * j, 8)] = patched[order[q], rows] if q in order else moved[q, rows]
    for copy in copies:
        copy.wait()


def finish_kernel(*refs, rows, tiles, levels):
    it = iter(refs)
    owns = [next(it) for _ in range(levels)]
    gots = [next(it) for _ in range(levels)]
    pair_got, offset, edge, link, tops, pops_in = [next(it) for _ in range(6)]
    pops_out, conc_out, solved, tiles_out, sems = [next(it) for _ in range(5)]
    del pops_in
    wall = lax.axis_index("wall")
    copies = []
    for j in range(len(z_plus) + len(z_minus)):
        tiles_out[pl.ds(8 * j, 8)] = tops[pl.ds(8 * j, 8)]

    def put(got, base, lower):
        for j in range(5):
            row = 8 * j if lower else 8 * (5 + j) + 4
            tiles_out[pl.ds(row, 4)] = got[pl.ds(base + 4 * j, 4)]

    pl.when(bit(wall, 0) == 1)(lambda: put(pair_got, 0, True))
    pl.when(bit(wall, 0) == 0)(lambda: put(pair_got, 0, False))
    for r in range(1, levels):
        base = 32 if r == levels - 1 else 96
        rest = lax.rem(wall, 2 ** (r + 1))
        pl.when(rest == 2**r)(functools.partial(put, gots[r], base, True))
        pl.when(rest == 2**r - 1)(functools.partial(put, gots[r], base, False))
    for j, q in enumerate(z_plus + z_minus):
        at = pl.ds(0, 8) if lattice_dirs[q][2] > 0 else pl.ds(8 * tiles - 8, 8)
        copies.append(
            pltpu.make_async_copy(tiles_out.at[pl.ds(8 * j, 8)], pops_out.at[q, at], sems.at[j])
        )
        copies[-1].start()
    half = rows // 2
    inner = []
    for h in range(2):
        top = levels - 1
        go, xo = read_ends(owns[top], h, 2)
        gr, xr = read_ends(gots[top], h, 2)
        w = (gr + xr * go) * reciprocal(1.0 - xo * xr)
        is_upper = bit(wall, top) == 1
        w_low, w_high = jnp.where(is_upper, w, 0.0), jnp.where(is_upper, 0.0, w)
        for r in range(top - 1, -1, -1):
            is_upper = bit(wall, r) == 1
            a, b = ordered(read_ends(owns[r], h), read_ends(gots[r], h), is_upper)
            top_a, low_b, _ = merge(a, b)
            new_low = top_a[0] + top_a[1] * w_low + top_a[2] * w_high
            new_high = low_b[0] + low_b[1] * w_low + low_b[2] * w_high
            w_low, w_high = (
                jnp.where(is_upper, new_low, w_low),
                jnp.where(is_upper, w_high, new_high),
            )
        at0, at1 = pl.ds(16 * (half - 1) + 8 * h, 8), pl.ds(16 * half + 8 * h, 8)
        a0 = offset[at0] + edge[at0] * w_low
        a1 = offset[at1] + edge[at1] * w_high
        k0, k1 = link[at0], link[at1]
        r = reciprocal(1.0 - k0 * k1)
        u0, u1 = (a0 + k0 * a1) * r, (a1 + k1 * a0) * r
        solved[at0] = u0
        solved[at1] = u1
        inner.append([u0, u1, w_low, w_high])
    parts = 2
    step = half // parts
    for part in range(parts):
        for i in range(part * step, (part + 1) * step):
            if i == 0:
                continue
            for h in range(2):
                u0, u1, w_low, w_high = inner[h]
                at0 = pl.ds(16 * (half - 1 - i) + 8 * h, 8)
                at1 = pl.ds(16 * (half + i) + 8 * h, 8)
                u0 = (offset[at0] + edge[at0] * w_low) + link[at0] * u0
                u1 = (offset[at1] + edge[at1] * w_high) + link[at1] * u1
                solved[at0] = u0
                solved[at1] = u1
                inner[h] = [u0, u1, w_low, w_high]
        for side in range(2):
            begin = half - (part + 1) * step if side == 0 else half + part * step
            span = pl.ds(16 * begin, 16 * step)
            copies.append(
                pltpu.make_async_copy(
                    solved.at[span], conc_out.at[span], sems.at[10 + 2 * part + side]
                )
            )
            copies[-1].start()
    for copy in copies:
        copy.wait()


def swaps(lats, walls):
    def pairs(partner):
        table = []
        for lat in range(lats):
            for wall in range(walls):
                to_lat, to_wall = partner(lat, wall)
                table.append((lat * walls + wall, to_lat * walls + to_wall))
        return table

    def odd_partner(lat, wall):
        if lat == 0 or lat == lats - 1:
            return lat, wall ^ 1
        return ((lat + 1) ^ 1) - 1, wall

    even = pairs(lambda lat, wall: (lat ^ 1, wall))
    odd = pairs(odd_partner)
    levels = []
    while 2 ** len(levels) < walls:
        flip = 2 ** (len(levels) + 1) - 1
        levels.append(pairs(lambda lat, wall: (lat, wall ^ flip)))
    return even, odd, levels


def per_device(
    populations, concentration, cell_flags, valence, diffusivity, applied_field, *, lats, walls
):
    rows, cells = populations.shape[1], populations.shape[1] * populations.shape[2]
    tiles = cells // 8
    chunks = [tiles // 8, tiles // 4]
    chunks += [(tiles - sum(chunks)) // 2, (tiles - sum(chunks) + 1) // 2]
    assert populations.shape[2] == X_CELLS and lats % 2 == 0 and walls >= 4
    even, odd, levels = swaps(lats, walls)
    assert 2 ** len(levels) == walls

    def move(x, table):
        return lax.ppermute(x, ("lat", "wall"), table)

    msg_rows = 2 * tiles * 5
    moved, even_msg, odd_msg, vel_z, conc, flags, table = pl.pallas_call(
        functools.partial(collide_kernel, chunks=chunks),
        out_shape=(
            on_chip(DIRS, cells + 16, LANES),
            on_chip(msg_rows, LANES),
            on_chip(msg_rows, LANES),
            on_chip(cells, LANES),
            on_chip(cells * SPECIES, LANES),
            on_chip(cells, LANES, dtype=jnp.int32),
            on_chip(64, LANES),
        ),
        in_specs=[ANY_SPEC] * 6,
        out_specs=(VMEM_SPEC,) * 7,
        scratch_shapes=[
            pltpu.VMEM((DIRS, cells, LANES), F32),
            pltpu.SMEM((SPECIES,), jnp.int32),
            pltpu.SMEM((SPECIES,), F32),
            pltpu.SMEM((3,), F32),
            pltpu.SemaphoreType.DMA((4 + 2 * len(chunks),)),
        ],
        compiler_params=params(),
        cost_estimate=cost(5_000_000, 3_000_000),
        name="collide",
    )(
        *in_hbm(
            populations.reshape(DIRS, cells, LANES),
            concentration.reshape(cells * SPECIES, LANES),
            cell_flags.reshape(cells, LANES),
            valence,
            diffusivity,
            applied_field,
        )
    )
    even_got, odd_got = move(even_msg, even), move(odd_msg, odd)

    offset, edge, link, ends = pl.pallas_call(
        functools.partial(eliminate_kernel, rows=rows),
        out_shape=(on_chip(cells * SPECIES, LANES),) * 3 + (on_chip(96, LANES),),
        in_specs=[VMEM_SPEC] * 4,
        out_specs=(VMEM_SPEC,) * 4,
        compiler_params=params(),
        cost_estimate=cost(5_000_000, 3_000_000),
        name="eliminate",
    )(*pin(vel_z, conc, flags, table))

    owns, gots = [ends], [move(ends, levels[0])]
    pair_got = None
    for level in range(len(levels) - 1):
        last = level == len(levels) - 2
        shapes = (on_chip((32 if last else 96) + FACE_ROWS, LANES),)
        if level == 0:
            shapes += (on_chip(FACE_ROWS, LANES),)
        sent = pl.pallas_call(
            functools.partial(relay_kernel, tiles=tiles, level=level, last=last),
            out_shape=shapes,
            in_specs=[VMEM_SPEC] * 5,
            out_specs=(VMEM_SPEC,) * len(shapes),
            compiler_params=params(),
            cost_estimate=cost(100_000, 200_000),
            name=f"relay{level}",
        )(*pin(owns[-1], gots[-1], moved, even_got, odd_got))
        owns.append(sent[0])
        gots.append(move(sent[0], levels[level + 1]))
        if level == 0:
            pair_got = move(sent[1], levels[0])

    pops_out, tops = pl.pallas_call(
        functools.partial(spread_kernel, tiles=tiles),
        out_shape=(
            jax.ShapeDtypeStruct((DIRS, cells, LANES), F32),
            on_chip(80, LANES),
        ),
        in_specs=[VMEM_SPEC] * 4,
        out_specs=(ANY_SPEC, VMEM_SPEC),
        scratch_shapes=[
            pltpu.VMEM((10, cells + 16, LANES), F32),
            pltpu.SemaphoreType.DMA((DIRS,)),
        ],
        compiler_params=params(),
        cost_estimate=cost(1_000_000, 2_500_000),
        name="spread",
    )(*pin(moved, even_got, odd_got, owns[-1]))

    n_in = 2 * len(levels) + 5
    new_pops, new_conc = pl.pallas_call(
        functools.partial(finish_kernel, rows=rows, tiles=tiles, levels=len(levels)),
        out_shape=(
            jax.ShapeDtypeStruct((DIRS, cells, LANES), F32),
            jax.ShapeDtypeStruct((cells * SPECIES, LANES), F32),
        ),
        in_specs=[VMEM_SPEC] * n_in + [ANY_SPEC],
        out_specs=(ANY_SPEC, ANY_SPEC),
        input_output_aliases={n_in: 0},
        scratch_shapes=[
            pltpu.VMEM((cells * SPECIES, LANES), F32),
            pltpu.VMEM((80, LANES), F32),
            pltpu.SemaphoreType.DMA((14,)),
        ],
        compiler_params=params(),
        cost_estimate=cost(1_000_000, 2_000_000),
        name="finish",
    )(*pin(*owns, *gots, pair_got, offset, edge, link, tops), pops_out)
    return new_pops.reshape(populations.shape), new_conc.reshape(concentration.shape)


def solution(mesh):
    in_specs = (
        P(None, "wall", "lat", None),
        P("wall", None, "lat", None),
        P("wall", "lat", None),
        P(),
        P(),
        P(),
    )
    out_specs = (P(None, "wall", "lat", None), P("wall", None, "lat", None))
    return jax.shard_map(
        functools.partial(per_device, lats=mesh.shape["lat"], walls=mesh.shape["wall"]),
        mesh=mesh,
        in_specs=in_specs,
        out_specs=out_specs,
        check_vma=False,
    )
```

```python
import functools

import jax
import jax.numpy as jnp
from jax import lax
from jax.experimental import pallas as pl
from jax.experimental.pallas import tpu as pltpu
from jax.sharding import PartitionSpec as P

lattice_dirs = (
    (0, 0, 0),
    (1, 0, 0),
    (-1, 0, 0),
    (0, 1, 0),
    (0, -1, 0),
    (0, 0, 1),
    (0, 0, -1),
    (1, 1, 0),
    (-1, -1, 0),
    (1, -1, 0),
    (-1, 1, 0),
    (1, 0, 1),
    (-1, 0, -1),
    (1, 0, -1),
    (-1, 0, 1),
    (0, 1, 1),
    (0, -1, -1),
    (0, 1, -1),
    (0, -1, 1),
)
DIRS = len(lattice_dirs)
FORCE_GAIN = 0.02
X_CELLS = 4
SPECIES = 4
LANES = 128
F32 = jnp.float32

x_plus = tuple(q for q in range(DIRS) if lattice_dirs[q][0] == 1)
x_minus = tuple(q for q in range(DIRS) if lattice_dirs[q][0] == -1)
z_plus = tuple(q for q in range(DIRS) if lattice_dirs[q][2] == 1)
z_minus = tuple(q for q in range(DIRS) if lattice_dirs[q][2] == -1)
FACE_ROWS = 24

VMEM_SPEC = pl.BlockSpec(memory_space=pltpu.VMEM)
ANY_SPEC = pl.BlockSpec(memory_space=pl.ANY)


def on_chip(*shape, dtype=F32):
    return pltpu.VMEM(shape, dtype)


def params():
    return pltpu.CompilerParams(vmem_limit_bytes=24 * 1024 * 1024)


def cost(flops, nbytes):
    return pl.CostEstimate(flops=flops, bytes_accessed=nbytes, transcendentals=0)


def in_hbm(*arrays):
    return [pltpu.with_memory_space_constraint(a, pltpu.HBM) for a in arrays]


def pin(*arrays):
    return [pltpu.with_memory_space_constraint(a, pltpu.VMEM) for a in arrays]


def out_even(q):
    step_x, _, step_z = lattice_dirs[q]
    return {0: 12, 1: 16, -1: 8}[step_z] + (0 if step_x > 0 else 3)


def out_odd(q):
    step_x, _, step_z = lattice_dirs[q]
    return {0: 8, 1: 12, -1: 4}[step_z] + (0 if step_x > 0 else 3)


def low_rows():
    return lax.broadcasted_iota(jnp.int32, (8, LANES), 0) < 4


def collide_kernel(
    pops_hbm,
    conc_hbm,
    flags_hbm,
    valence_hbm,
    diffusivity_hbm,
    field_hbm,
    moved,
    even_msg,
    odd_msg,
    vel_z,
    conc,
    flags,
    table,
    pops,
    mid,
    valence,
    diffusivity,
    field,
    sems,
    *,
    chunks,
):
    tiles = sum(chunks)
    small = [
        pltpu.make_async_copy(source, target, sems.at[i])
        for i, (source, target) in enumerate(
            (
                (flags_hbm, flags),
                (valence_hbm, valence),
                (field_hbm, field),
                (diffusivity_hbm, diffusivity),
            )
        )
    ]
    for copy in small:
        copy.start()
    copies = {}
    at = 0
    for c, count in enumerate(chunks):
        rows = pl.ds(8 * at, 8 * count)
        crows = pl.ds(8 * SPECIES * at, 8 * SPECIES * count)
        copies[at] = (
            pltpu.make_async_copy(conc_hbm.at[crows], conc.at[crows], sems.at[4 + c]),
            pltpu.make_async_copy(
                pops_hbm.at[:, rows], pops.at[pl.ds(0, DIRS), rows], sems.at[4 + c]
            ),
        )
        for copy in copies[at]:
            copy.start()
        both = pops.at[:, rows]
        copies[at] = pltpu.make_async_copy(both, both, sems.at[4 + c])
        at += count
    low = low_rows()
    for copy in small:
        copy.wait()
    val_pair = [
        jnp.where(low, valence[2 * h].astype(F32), valence[2 * h + 1].astype(F32))
        for h in range(2)
    ]
    field_xyz = [FORCE_GAIN * field[axis] for axis in range(3)]

    def moments(at):
        p = [pops[q, pl.ds(at, 8)] for q in range(DIRS)]
        sums = []
        for z in range(2):
            part = val_pair[0] * conc[pl.ds(4 * at + 16 * z, 8)]
            part = part + val_pair[1] * conc[pl.ds(4 * at + 16 * z + 8, 8)]
            sums.append(part + pltpu.roll(part, 4, axis=0))
        charge = jnp.where(low, sums[0], sums[1])
        diff = {q: p[q] - p[q + 1] for q in range(1, DIRS, 2)}
        total = {q: p[q] + p[q + 1] for q in range(1, DIRS, 2)}
        density = (
            ((p[0] + total[1]) + (total[3] + total[5]))
            + ((total[7] + total[9]) + (total[11] + total[13]))
            + (total[15] + total[17])
        )
        momentum = [
            (diff[1] + diff[7]) + (diff[9] + diff[11]) + diff[13],
            (diff[3] + diff[7]) - (diff[9] - diff[15]) + diff[17],
            (diff[5] + diff[11]) - (diff[13] - diff[15]) - diff[17],
        ]
        force = [charge * f for f in field_xyz]
        inverse = 1.0 / density
        vel = [(momentum[a] + 0.5 * force[a]) * inverse for a in range(3)]
        vel_z[pl.ds(at, 8)] = vel[2]
        speed_sq = vel[0] * vel[0] + vel[1] * vel[1] + vel[2] * vel[2]
        work = vel[0] * force[0] + vel[1] * force[1] + vel[2] * force[2]
        base = (1.25 / 36.0 * density) * (1.0 - 1.5 * speed_sq) - (1.125 / 36.0) * work
        odd = [(3.75 / 36.0) * momentum[a] + (3.0 / 36.0) * force[a] for a in range(3)]
        even = [(5.625 / 36.0) * momentum[a] + (6.1875 / 36.0) * force[a] for a in range(3)]
        for j, value in enumerate((base, *vel, *odd, *even)):
            mid[j, pl.ds(at, 8)] = value

    def scatter(at):
        solid = flags[pl.ds(at, 8)] != 0
        base36, *rest = [mid[j, pl.ds(at, 8)] for j in range(10)]
        vel, odd36, even36 = rest[:3], rest[3:6], rest[6:]
        base18 = base36 + base36
        p0 = pops[0, pl.ds(at, 8)]
        moved[0, pl.ds(8 + at, 8)] = jnp.where(solid, p0, 12.0 * base36 - 0.25 * p0)
        for q in range(1, DIRS, 2):
            axes = [(a, lattice_dirs[q][a]) for a in range(3) if lattice_dirs[q][a]]

            def along(v):
                out = v[axes[0][0]]
                for a, sign in axes[1:]:
                    out = out + v[a] if sign > 0 else out - v[a]
                return out

            cu, odd, even = along(vel), along(odd36), along(even36)
            if len(axes) == 1:
                shared = base18 + 2.0 * (cu * even)
                odd = odd + odd
            else:
                shared = base36 + cu * even
            ahead, behind = pops[q, pl.ds(at, 8)], pops[q + 1, pl.ds(at, 8)]
            for d, relaxed, bounced in (
                (q, (shared + odd) - 0.25 * ahead, behind),
                (q + 1, (shared - odd) - 0.25 * behind, ahead),
            ):
                step_x, step_y, step_z = lattice_dirs[d]
                value = jnp.where(solid, bounced, relaxed)
                if step_y:
                    value = pltpu.roll(value, step_y % LANES, axis=1)
                if step_x:
                    value = pltpu.roll(value, step_x % 8, axis=0)
                moved[d, pl.ds(8 + at + 4 * step_z, 8)] = value

    at = 0
    for count in chunks:
        copies[at].wait()
        for k in range(at, at + count):
            moments(8 * k)
        for k in range(at, at + count):
            scatter(8 * k)
        at += count
    for d in z_plus + z_minus:
        at = 8 if lattice_dirs[d][2] > 0 else 8 * tiles + 4
        moved[d, pl.ds(at, 4)] = jnp.zeros((4, LANES), F32)

    def pack(target, dirs):
        for j, q in enumerate(dirs):
            target[pl.ds(2 * tiles * j, tiles)] = moved[q, pl.ds(out_even(q), tiles, stride=8)]
            target[pl.ds(2 * tiles * j + tiles, tiles)] = moved[
                q, pl.ds(out_odd(q), tiles, stride=8)
            ]

    is_odd = lax.rem(lax.axis_index("lat"), 2) == 1

    @pl.when(jnp.logical_not(is_odd))
    def _():
        pack(even_msg, x_plus)
        pack(odd_msg, x_minus)

    @pl.when(is_odd)
    def _():
        pack(even_msg, x_minus)
        pack(odd_msg, x_plus)

    for h in range(2):
        diff = jnp.where(low, diffusivity[2 * h], diffusivity[2 * h + 1])
        values = (
            diff,
            diff * 0.01,
            diff * jnp.where(val_pair[h] > 0, 0.5, 0.02),
            val_pair[h] * field[2],
        )
        for j, value in enumerate(values):
            table[pl.ds(8 * (4 * h + j), 8)] = value


def reciprocal(x):
    return 1.0 / x


def eliminate_kernel(
    vel_z, conc, flags, table, offset, edge, link, ends, *, rows
):
    low = low_rows()
    half = rows // 2
    for h in range(2):
        diff, slow, membrane, pull = [table[pl.ds(8 * (4 * h + j), 8)] for j in range(4)]

        def coefficients(z):
            tile = pl.ds(8 * (z // 2), 8)
            vz, flag = vel_z[tile], flags[tile]
            mine = low if z % 2 == 0 else jnp.logical_not(low)
            vz = jnp.where(mine, vz, pltpu.roll(vz, 4, axis=0))
            flag = jnp.where(mine, flag, pltpu.roll(flag, 4, axis=0))
            spread = jnp.where(flag == 0, diff, jnp.where(flag == 1, slow, membrane))
            drift = spread * jnp.tanh(2.0 * vz + pull)
            lower = 0.5 * spread + 0.25 * drift
            upper = 0.5 * spread - 0.25 * drift
            here = conc[pl.ds(16 * z + 8 * h, 8)]
            rhs = here - spread * here
            if z > 0:
                rhs = rhs + lower * conc[pl.ds(16 * (z - 1) + 8 * h, 8)]
            if z < rows - 1:
                rhs = rhs + upper * conc[pl.ds(16 * (z + 1) + 8 * h, 8)]
            return 1.0 + spread, lower, upper, rhs

        state = {}
        for z_up in range(half):
            for side in range(2):
                z = z_up if side == 0 else rows - 1 - z_up
                main, lower, upper, rhs = coefficients(z)
                back, ahead = (lower, upper) if side == 0 else (upper, lower)
                if z_up == 0:
                    r = reciprocal(main)
                    d, e, k = rhs * r, back * r, ahead * r
                    first = (d, e, k)
                else:
                    d, e, k, first = state[side]
                    r = reciprocal(main - back * k)
                    d, e, k = (rhs + back * d) * r, (back * e) * r, ahead * r
                    first = (first[0] + first[2] * d, first[1] + first[2] * e, first[2] * k)
                state[side] = (d, e, k, first)
                at = pl.ds(16 * z + 8 * h, 8)
                offset[at] = d
                edge[at] = e
                link[at] = k
        (d0, e0, k0, first), (d1, e1, k1, last) = state[0], state[1]
        r = reciprocal(1.0 - k0 * k1)
        high = ((d1 + k1 * d0) * r, (k1 * e0) * r, e1 * r)
        below = ((d0 + k0 * d1) * r, e0 * r, (k0 * e1) * r)
        values = (
            conc[pl.ds(8 * h, 8)] + first[0] + first[2] * high[0],
            first[1] + first[2] * high[1],
            first[2] * high[2],
            conc[pl.ds(16 * (rows - 1) + 8 * h, 8)] + last[0] + last[2] * below[0],
            last[2] * below[1],
            last[1] + last[2] * below[2],
        )
        for j, value in enumerate(values):
            ends[pl.ds(16 * j + 8 * h, 8)] = value


def bit(wall, r):
    return lax.rem(lax.div(wall, 2**r), 2)


def read_ends(ref, h, n=6):
    return [ref[pl.ds(16 * j + 8 * h, 8)] for j in range(n)]


def ordered(own, got, is_upper):
    return (
        [jnp.where(is_upper, g, o) for o, g in zip(own, got)],
        [jnp.where(is_upper, o, g) for o, g in zip(own, got)],
    )


def merge(a, b):
    r = reciprocal(1.0 - a[5] * b[1])
    top_a = ((a[3] + a[5] * b[0]) * r, a[4] * r, (a[5] * b[2]) * r)
    low_b = ((b[0] + b[1] * a[3]) * r, (b[1] * a[4]) * r, b[2] * r)
    merged = (
        a[0] + a[2] * low_b[0],
        a[1] + a[2] * low_b[1],
        a[2] * low_b[2],
        b[3] + b[4] * top_a[0],
        b[4] * top_a[1],
        b[5] + b[4] * top_a[2],
    )
    return top_a, low_b, merged


def relay_kernel(own, got, send, *, level, last):
    wall = lax.axis_index("wall")
    is_upper = bit(wall, level) == 1
    next_upper = bit(wall, level + 1) == 1
    for h in range(2):
        a, b = ordered(read_ends(own, h), read_ends(got, h), is_upper)
        values = merge(a, b)[2]
        if last:
            values = [
                jnp.where(next_upper, values[0], values[3]),
                jnp.where(next_upper, values[1], values[5]),
            ]
        for j, value in enumerate(values):
            send[pl.ds(16 * j + 8 * h, 8)] = value


def faces_kernel(moved, even_got, odd_got, *targets, tiles):
    wall, lat = lax.axis_index("wall"), lax.axis_index("lat")
    lats = lax.axis_size("lat")
    odd_lat = lax.rem(lat, 2) == 1

    def from_lat(q, odd_z, index):
        dirs = x_plus if q in x_plus else x_minus
        at = pl.ds(2 * tiles * dirs.index(q) + (tiles if odd_z else 0) + index, 1)
        use_even = odd_lat if q in x_plus else jnp.logical_not(odd_lat)
        exists = lat > 0 if q in x_plus else lat < lats - 1
        row = jnp.where(use_even, even_got[at], odd_got[at])
        return jnp.where(exists, row, 0.0)

    def fill(target, dirs):
        for j, q in enumerate(dirs):
            up = lattice_dirs[q][2] > 0
            target[pl.ds(4 * j, 4)] = moved[q, pl.ds(8 * tiles + 8, 4) if up else pl.ds(4, 4)]
            step_x = lattice_dirs[q][0]
            if step_x:
                at = 4 * j + (0 if step_x > 0 else 3)
                target[pl.ds(at, 1)] = from_lat(q, up, tiles - 1 if up else 0)
        target[pl.ds(20, 4)] = jnp.zeros((4, LANES), F32)

    for r, target in enumerate(targets):
        pl.when(bit(wall, r) == 0)(functools.partial(fill, target, z_plus))
        pl.when(bit(wall, r) == 1)(functools.partial(fill, target, z_minus))


def solve_ions(owns, gots, offset, edge, link, solved, write, *, rows):
    levels = len(owns)
    wall = lax.axis_index("wall")
    half = rows // 2
    inner = []
    for h in range(2):
        top = levels - 1
        go, xo = read_ends(owns[top], h, 2)
        gr, xr = read_ends(gots[top], h, 2)
        w = (gr + xr * go) * reciprocal(1.0 - xo * xr)
        is_upper = bit(wall, top) == 1
        w_low, w_high = jnp.where(is_upper, w, 0.0), jnp.where(is_upper, 0.0, w)
        for r in range(top - 1, -1, -1):
            is_upper = bit(wall, r) == 1
            a, b = ordered(read_ends(owns[r], h), read_ends(gots[r], h), is_upper)
            top_a, low_b, _ = merge(a, b)
            new_low = top_a[0] + top_a[1] * w_low + top_a[2] * w_high
            new_high = low_b[0] + low_b[1] * w_low + low_b[2] * w_high
            w_low, w_high = (
                jnp.where(is_upper, new_low, w_low),
                jnp.where(is_upper, w_high, new_high),
            )
        at0, at1 = pl.ds(16 * (half - 1) + 8 * h, 8), pl.ds(16 * half + 8 * h, 8)
        a0 = offset[at0] + edge[at0] * w_low
        a1 = offset[at1] + edge[at1] * w_high
        k0, k1 = link[at0], link[at1]
        r = reciprocal(1.0 - k0 * k1)
        u0, u1 = (a0 + k0 * a1) * r, (a1 + k1 * a0) * r
        solved[at0] = u0
        solved[at1] = u1
        inner.append([u0, u1, w_low, w_high])
    for i in range(1, half):
        for h in range(2):
            u0, u1, w_low, w_high = inner[h]
            at0 = pl.ds(16 * (half - 1 - i) + 8 * h, 8)
            at1 = pl.ds(16 * (half + i) + 8 * h, 8)
            u0 = (offset[at0] + edge[at0] * w_low) + link[at0] * u0
            u1 = (offset[at1] + edge[at1] * w_high) + link[at1] * u1
            solved[at0] = u0
            solved[at1] = u1
            inner[h] = [u0, u1, w_low, w_high]
        if i == half // 2 - 1:
            write(0, half - half // 2, 2 * (half // 2))
    write(1, 0, half - half // 2)
    write(2, half + half // 2, half - half // 2)


def outputs_kernel(*refs, rows, tiles, levels):
    it = iter(refs)
    owns = [next(it) for _ in range(levels)]
    gots = [next(it) for _ in range(levels)]
    offset, edge, link, moved, even_got, odd_got, _ = [next(it) for _ in range(7)]
    pops_out, conc_out, tops, patched, solved, sems = [next(it) for _ in range(6)]
    lat, lats = lax.axis_index("lat"), lax.axis_size("lat")
    odd_lat = lax.rem(lat, 2) == 1
    body = pl.ds(8, 8 * tiles)
    copies = []

    def start(source, target):
        copies.append(pltpu.make_async_copy(source, target, sems.at[len(copies)]))
        copies[-1].start()

    for q in range(DIRS):
        if lattice_dirs[q][0] == 0:
            start(moved.at[q, body], pops_out.at[q])
    order = {q: j for j, q in enumerate(x_plus + x_minus)}

    def fill(dirs, got, keep):
        for j, q in enumerate(dirs):
            for k in range(tiles + 2):
                patched[order[q], pl.ds(8 * k, 8)] = moved[q, pl.ds(8 * k, 8)]
            even_z = got[pl.ds(2 * tiles * j, tiles)]
            odd_z = got[pl.ds(2 * tiles * j + tiles, tiles)]
            patched[order[q], pl.ds(out_odd(q), tiles, stride=8)] = jnp.where(keep, even_z, 0.0)
            patched[order[q], pl.ds(out_even(q), tiles, stride=8)] = jnp.where(keep, odd_z, 0.0)

    @pl.when(odd_lat)
    def _():
        fill(x_plus, even_got, lat > 0)
        fill(x_minus, odd_got, lat < lats - 1)

    @pl.when(jnp.logical_not(odd_lat))
    def _():
        fill(x_plus, odd_got, lat > 0)
        fill(x_minus, even_got, lat < lats - 1)

    for q in x_plus + x_minus:
        start(patched.at[order[q], body], pops_out.at[q])
    for j, q in enumerate(z_plus + z_minus):
        at = pl.ds(8, 8) if lattice_dirs[q][2] > 0 else pl.ds(8 * tiles, 8)
        tops[pl.ds(8 * j, 8)] = patched[order[q], at] if q in order else moved[q, at]

    def write(_, begin, count):
        span = pl.ds(16 * begin, 16 * count)
        start(solved.at[span], conc_out.at[span])

    solve_ions(owns, gots, offset, edge, link, solved, write, rows=rows)
    for copy in copies:
        copy.wait()


def patch_kernel(*refs, tiles, levels):
    gots = refs[:levels]
    tops, _, pops_out, fixed, sems = refs[levels:]
    wall = lax.axis_index("wall")
    for j in range(len(z_plus) + len(z_minus)):
        fixed[pl.ds(8 * j, 8)] = tops[pl.ds(8 * j, 8)]

    def put(got, lower):
        for j in range(5):
            row = 8 * j if lower else 8 * (5 + j) + 4
            fixed[pl.ds(row, 4)] = got[pl.ds(4 * j, 4)]

    for r in range(levels):
        rest = lax.rem(wall, 2 ** (r + 1))
        pl.when(rest == 2**r)(functools.partial(put, gots[r], True))
        pl.when(rest == 2**r - 1)(functools.partial(put, gots[r], False))
    copies = []
    for j, q in enumerate(z_plus + z_minus):
        at = pl.ds(0, 8) if lattice_dirs[q][2] > 0 else pl.ds(8 * tiles - 8, 8)
        copies.append(
            pltpu.make_async_copy(fixed.at[pl.ds(8 * j, 8)], pops_out.at[q, at], sems.at[j])
        )
        copies[-1].start()
    for copy in copies:
        copy.wait()


def swaps(lats, walls):
    def pairs(partner):
        table = []
        for lat in range(lats):
            for wall in range(walls):
                to_lat, to_wall = partner(lat, wall)
                table.append((lat * walls + wall, to_lat * walls + to_wall))
        return table

    def odd_partner(lat, wall):
        if lat == 0 or lat == lats - 1:
            return lat, wall ^ 1
        return ((lat + 1) ^ 1) - 1, wall

    even = pairs(lambda lat, wall: (lat ^ 1, wall))
    odd = pairs(odd_partner)
    levels = []
    while 2 ** len(levels) < walls:
        flip = 2 ** (len(levels) + 1) - 1
        levels.append(pairs(lambda lat, wall: (lat, wall ^ flip)))
    return even, odd, levels


def per_device(
    populations, concentration, cell_flags, valence, diffusivity, applied_field, *, lats, walls
):
    rows, cells = populations.shape[1], populations.shape[1] * populations.shape[2]
    tiles = cells // 8
    chunks = [tiles // 8, tiles // 4]
    chunks += [(tiles - sum(chunks)) // 2, (tiles - sum(chunks) + 1) // 2]
    assert populations.shape[2] == X_CELLS and lats % 2 == 0 and walls >= 4
    even, odd, levels = swaps(lats, walls)
    assert 2 ** len(levels) == walls

    def move(x, table):
        return lax.ppermute(x, ("lat", "wall"), table)

    msg_rows = 2 * tiles * 5
    moved, even_msg, odd_msg, vel_z, conc, flags, table = pl.pallas_call(
        functools.partial(collide_kernel, chunks=chunks),
        out_shape=(
            on_chip(DIRS, cells + 16, LANES),
            on_chip(msg_rows, LANES),
            on_chip(msg_rows, LANES),
            on_chip(cells, LANES),
            on_chip(cells * SPECIES, LANES),
            on_chip(cells, LANES, dtype=jnp.int32),
            on_chip(64, LANES),
        ),
        in_specs=[ANY_SPEC] * 6,
        out_specs=(VMEM_SPEC,) * 7,
        scratch_shapes=[
            pltpu.VMEM((DIRS + SPECIES, cells, LANES), F32),
            pltpu.VMEM((10, cells, LANES), F32),
            pltpu.SMEM((SPECIES,), jnp.int32),
            pltpu.SMEM((SPECIES,), F32),
            pltpu.SMEM((3,), F32),
            pltpu.SemaphoreType.DMA((4 + len(chunks),)),
        ],
        compiler_params=params(),
        cost_estimate=cost(5_000_000, 3_000_000),
        name="collide",
    )(
        *in_hbm(
            populations.reshape(DIRS, cells, LANES),
            concentration.reshape(cells * SPECIES, LANES),
            cell_flags.reshape(cells, LANES),
            valence,
            diffusivity,
            applied_field,
        )
    )
    odd_got = move(odd_msg, odd)
    even_got = move(even_msg, even)

    offset, edge, link, ends = pl.pallas_call(
        functools.partial(eliminate_kernel, rows=rows),
        out_shape=(on_chip(cells * SPECIES, LANES),) * 3 + (on_chip(96, LANES),),
        in_specs=[VMEM_SPEC] * 4,
        out_specs=(VMEM_SPEC,) * 4,
        compiler_params=params(),
        cost_estimate=cost(5_000_000, 3_000_000),
        name="eliminate",
    )(*pin(vel_z, conc, flags, table))

    depth = len(levels)
    owns, gots = [ends], [move(ends, levels[0])]
    for level in range(depth - 1):
        last = level == depth - 2
        sent = pl.pallas_call(
            functools.partial(relay_kernel, level=level, last=last),
            out_shape=on_chip(32 if last else 96, LANES),
            in_specs=[VMEM_SPEC] * 2,
            out_specs=VMEM_SPEC,
            compiler_params=params(),
            cost_estimate=cost(100_000, 200_000),
            name=f"relay{level}",
        )(*pin(owns[-1], gots[-1]))
        owns.append(sent)
        gots.append(move(sent, levels[level + 1]))

    faces = pl.pallas_call(
        functools.partial(faces_kernel, tiles=tiles),
        out_shape=(on_chip(FACE_ROWS, LANES),) * depth,
        in_specs=[VMEM_SPEC] * 3,
        out_specs=(VMEM_SPEC,) * depth,
        compiler_params=params(),
        cost_estimate=cost(100_000, 200_000),
        name="faces",
    )(*pin(moved, even_got, odd_got))
    face_gots = [move(face, table) for face, table in zip(faces, levels)]

    operands = pin(*owns, *gots, offset, edge, link, moved, even_got, odd_got, faces[-1])
    pops_out, new_conc, tops = pl.pallas_call(
        functools.partial(outputs_kernel, rows=rows, tiles=tiles, levels=depth),
        out_shape=(
            jax.ShapeDtypeStruct((DIRS, cells, LANES), F32),
            jax.ShapeDtypeStruct((cells * SPECIES, LANES), F32),
            on_chip(80, LANES),
        ),
        in_specs=[VMEM_SPEC] * len(operands),
        out_specs=(ANY_SPEC, ANY_SPEC, VMEM_SPEC),
        scratch_shapes=[
            pltpu.VMEM((10, cells + 16, LANES), F32),
            pltpu.VMEM((cells * SPECIES, LANES), F32),
            pltpu.SemaphoreType.DMA((DIRS + 3,)),
        ],
        compiler_params=params(),
        cost_estimate=cost(1_000_000, 2_500_000),
        name="outputs",
    )(*operands)

    new_pops = pl.pallas_call(
        functools.partial(patch_kernel, tiles=tiles, levels=depth),
        out_shape=jax.ShapeDtypeStruct((DIRS, cells, LANES), F32),
        in_specs=[VMEM_SPEC] * (depth + 1) + [ANY_SPEC],
        out_specs=ANY_SPEC,
        input_output_aliases={depth + 1: 0},
        scratch_shapes=[
            pltpu.VMEM((80, LANES), F32),
            pltpu.SemaphoreType.DMA((10,)),
        ],
        compiler_params=params(),
        cost_estimate=cost(10_000, 100_000),
        name="patch",
    )(*pin(*face_gots, tops), pops_out)
    return new_pops.reshape(populations.shape), new_conc.reshape(concentration.shape)


def solution(mesh):
    in_specs = (
        P(None, "wall", "lat", None),
        P("wall", None, "lat", None),
        P("wall", "lat", None),
        P(),
        P(),
        P(),
    )
    out_specs = (P(None, "wall", "lat", None), P("wall", None, "lat", None))
    return jax.shard_map(
        functools.partial(per_device, lats=mesh.shape["lat"], walls=mesh.shape["wall"]),
        mesh=mesh,
        in_specs=in_specs,
        out_specs=out_specs,
        check_vma=False,
    )
```

```python
import functools

import jax
import jax.numpy as jnp
from jax import lax
from jax.experimental import pallas as pl
from jax.experimental.pallas import tpu as pltpu
from jax.sharding import PartitionSpec as P

lattice_dirs = (
    (0, 0, 0),
    (1, 0, 0),
    (-1, 0, 0),
    (0, 1, 0),
    (0, -1, 0),
    (0, 0, 1),
    (0, 0, -1),
    (1, 1, 0),
    (-1, -1, 0),
    (1, -1, 0),
    (-1, 1, 0),
    (1, 0, 1),
    (-1, 0, -1),
    (1, 0, -1),
    (-1, 0, 1),
    (0, 1, 1),
    (0, -1, -1),
    (0, 1, -1),
    (0, -1, 1),
)
DIRS = len(lattice_dirs)
FORCE_GAIN = 0.02
X_CELLS = 4
SPECIES = 4
LANES = 128
F32 = jnp.float32

x_plus = tuple(q for q in range(DIRS) if lattice_dirs[q][0] == 1)
x_minus = tuple(q for q in range(DIRS) if lattice_dirs[q][0] == -1)
z_plus = tuple(q for q in range(DIRS) if lattice_dirs[q][2] == 1)
z_minus = tuple(q for q in range(DIRS) if lattice_dirs[q][2] == -1)
FACE_ROWS = 24

VMEM_SPEC = pl.BlockSpec(memory_space=pltpu.VMEM)
ANY_SPEC = pl.BlockSpec(memory_space=pl.ANY)


def on_chip(*shape, dtype=F32):
    return pltpu.VMEM(shape, dtype)


def params():
    return pltpu.CompilerParams(vmem_limit_bytes=24 * 1024 * 1024)


def cost(flops, nbytes):
    return pl.CostEstimate(flops=flops, bytes_accessed=nbytes, transcendentals=0)


def in_hbm(*arrays):
    return [pltpu.with_memory_space_constraint(a, pltpu.HBM) for a in arrays]


def pin(*arrays):
    return [pltpu.with_memory_space_constraint(a, pltpu.VMEM) for a in arrays]


def out_even(q):
    step_x, _, step_z = lattice_dirs[q]
    return {0: 12, 1: 16, -1: 8}[step_z] + (0 if step_x > 0 else 3)


def out_odd(q):
    step_x, _, step_z = lattice_dirs[q]
    return {0: 8, 1: 12, -1: 4}[step_z] + (0 if step_x > 0 else 3)


def low_rows():
    return lax.broadcasted_iota(jnp.int32, (8, LANES), 0) < 4


def density_and_momentum(p):
    diff = {q: p[q] - p[q + 1] for q in range(1, DIRS, 2)}
    total = {q: p[q] + p[q + 1] for q in range(1, DIRS, 2)}
    density = (
        ((p[0] + total[1]) + (total[3] + total[5]))
        + ((total[7] + total[9]) + (total[11] + total[13]))
        + (total[15] + total[17])
    )
    momentum = [
        (diff[1] + diff[7]) + (diff[9] + diff[11]) + diff[13],
        (diff[3] + diff[7]) - (diff[9] - diff[15]) + diff[17],
        (diff[5] + diff[11]) - (diff[13] - diff[15]) - diff[17],
    ]
    return density, momentum


def moments(p, charge, field_xyz):
    density, momentum = density_and_momentum(p)
    force = [charge * f for f in field_xyz]
    inverse = 1.0 / density
    vel = [(momentum[a] + 0.5 * force[a]) * inverse for a in range(3)]
    speed_sq = vel[0] * vel[0] + vel[1] * vel[1] + vel[2] * vel[2]
    work = vel[0] * force[0] + vel[1] * force[1] + vel[2] * force[2]
    base = (1.25 / 36.0 * density) * (1.0 - 1.5 * speed_sq) - (1.125 / 36.0) * work
    odd = [(3.75 / 36.0) * momentum[a] + (3.0 / 36.0) * force[a] for a in range(3)]
    even = [(5.625 / 36.0) * momentum[a] + (6.1875 / 36.0) * force[a] for a in range(3)]
    return base, vel, odd, even


def parts_of(q, base, vel, odd, even):
    axes = [(a, lattice_dirs[q][a]) for a in range(3) if lattice_dirs[q][a]]

    def along(v):
        out = v[axes[0][0]]
        for a, sign in axes[1:]:
            out = out + v[a] if sign > 0 else out - v[a]
        return out

    cu, odd_q, even_q = along(vel), along(odd), along(even)
    if len(axes) == 1:
        return (base + base) + 2.0 * (cu * even_q), odd_q + odd_q
    return base + cu * even_q, odd_q


def edges_kernel(
    pops_hbm,
    conc_hbm,
    flags_hbm,
    valence_hbm,
    diffusivity_hbm,
    field_hbm,
    even_msg,
    odd_msg,
    pops,
    conc,
    flags,
    table,
    valence,
    diffusivity,
    field,
    sems,
    *,
    chunks,
):
    small = [
        pltpu.make_async_copy(source, target, sems.at[i])
        for i, (source, target) in enumerate(
            (
                (flags_hbm, flags),
                (valence_hbm, valence),
                (field_hbm, field),
                (diffusivity_hbm, diffusivity),
            )
        )
    ]
    for copy in small:
        copy.start()
    arrived = {}
    at = 0
    for c, count in enumerate(chunks):
        rows = pl.ds(32 * at, 32 * count)
        crows = pl.ds(128 * at, 128 * count)
        sem = sems.at[4 + c]
        pltpu.make_async_copy(conc_hbm.at[crows], conc.at[crows], sem).start()
        pltpu.make_async_copy(pops_hbm.at[:, rows], pops.at[pl.ds(0, DIRS), rows], sem).start()
        both = pops.at[:, rows]
        arrived[at] = pltpu.make_async_copy(both, both, sem)
        at += count
    low = low_rows()
    for copy in small:
        copy.wait()
    val = [valence[s].astype(F32) for s in range(SPECIES)]
    field_xyz = [FORCE_GAIN * field[axis] for axis in range(3)]
    values = [jnp.full((8, LANES), f, F32) for f in field_xyz]
    for h in range(2):
        diff = jnp.where(low, diffusivity[2 * h], diffusivity[2 * h + 1])
        val_pair = jnp.where(low, val[2 * h], val[2 * h + 1])
        values += [
            val_pair,
            diff,
            diff * 0.01,
            diff * jnp.where(val_pair > 0, 0.5, 0.02),
            val_pair * field[2],
        ]
    for j, value in enumerate(values):
        table[pl.ds(8 * j, 8)] = value
    is_odd = lax.rem(lax.axis_index("lat"), 2) == 1
    for g in range(sum(chunks)):
        if g in arrived:
            arrived[g].wait()
        sent = {}
        for x, dirs in ((X_CELLS - 1, x_plus), (0, x_minus)):
            at = pl.ds(32 * g + x, 8, stride=4)
            p = [pops[q, at] for q in range(DIRS)]
            solid = flags[at] != 0
            terms = [
                val[s] * conc[pl.ds(128 * g + 4 * s + x, 8, stride=16)] for s in range(SPECIES)
            ]
            charge = (terms[0] + terms[1]) + (terms[2] + terms[3])
            found = moments(p, charge, field_xyz)
            for j, q in enumerate(dirs):
                first = q if q % 2 else q - 1
                shared, odd = parts_of(first, *found)
                relaxed = (shared + odd if q % 2 else shared - odd) - 0.25 * p[q]
                value = jnp.where(solid, p[q + 1 if q % 2 else q - 1], relaxed)
                step_y = lattice_dirs[q][1]
                if step_y:
                    value = pltpu.roll(value, step_y % LANES, axis=1)
                sent[x, j] = value
        for j in range(5):
            plus, minus = sent[X_CELLS - 1, j], sent[0, j]
            at = pl.ds(8 * sum(chunks) * j + 8 * g, 8)
            even_msg[at] = jnp.where(is_odd, minus, plus)
            odd_msg[at] = jnp.where(is_odd, plus, minus)


def collide_kernel(pops, flags, mid, moved, *, tiles):
    def scatter(at):
        solid = flags[pl.ds(at, 8)] != 0
        base, *rest = [mid[j, pl.ds(at, 8)] for j in range(10)]
        p0 = pops[0, pl.ds(at, 8)]
        moved[0, pl.ds(8 + at, 8)] = jnp.where(solid, p0, 12.0 * base - 0.25 * p0)
        for q in range(1, DIRS, 2):
            shared, odd = parts_of(q, base, rest[:3], rest[3:6], rest[6:])
            ahead, behind = pops[q, pl.ds(at, 8)], pops[q + 1, pl.ds(at, 8)]
            for d, relaxed, bounced in (
                (q, (shared + odd) - 0.25 * ahead, behind),
                (q + 1, (shared - odd) - 0.25 * behind, ahead),
            ):
                step_x, step_y, step_z = lattice_dirs[d]
                value = jnp.where(solid, bounced, relaxed)
                if step_y:
                    value = pltpu.roll(value, step_y % LANES, axis=1)
                if step_x:
                    value = pltpu.roll(value, step_x % 8, axis=0)
                moved[d, pl.ds(8 + at + 4 * step_z, 8)] = value

    for k in range(tiles):
        scatter(8 * k)
    for d in z_plus + z_minus:
        at = 8 if lattice_dirs[d][2] > 0 else 8 * tiles + 4
        moved[d, pl.ds(at, 4)] = jnp.zeros((4, LANES), F32)


def reciprocal(x):
    return 1.0 / x


def eliminate_kernel(
    pops, conc, flags, table, mid, offset, edge, link, ends, *, rows
):
    low = low_rows()
    half = rows // 2
    field_xyz = [table[pl.ds(8 * a, 8)] for a in range(3)]
    val_pair = [table[pl.ds(8 * (3 + 5 * h), 8)] for h in range(2)]
    for k in range(half):
        at = 8 * k
        sums = []
        for z in range(2):
            part = val_pair[0] * conc[pl.ds(4 * at + 16 * z, 8)]
            part = part + val_pair[1] * conc[pl.ds(4 * at + 16 * z + 8, 8)]
            sums.append(part + pltpu.roll(part, 4, axis=0))
        charge = jnp.where(low, sums[0], sums[1])
        base, vel, odd, even = moments(
            [pops[q, pl.ds(at, 8)] for q in range(DIRS)], charge, field_xyz
        )
        for j, value in enumerate((base, *vel, *odd, *even)):
            mid[j, pl.ds(at, 8)] = value
    for h in range(2):
        diff, slow, membrane, pull = [table[pl.ds(8 * (4 + 5 * h + j), 8)] for j in range(4)]

        def coefficients(z):
            tile = pl.ds(8 * (z // 2), 8)
            vz, flag = mid[3, tile], flags[tile]
            mine = low if z % 2 == 0 else jnp.logical_not(low)
            vz = jnp.where(mine, vz, pltpu.roll(vz, 4, axis=0))
            flag = jnp.where(mine, flag, pltpu.roll(flag, 4, axis=0))
            spread = jnp.where(flag == 0, diff, jnp.where(flag == 1, slow, membrane))
            drift = spread * jnp.tanh(2.0 * vz + pull)
            lower = 0.5 * spread + 0.25 * drift
            upper = 0.5 * spread - 0.25 * drift
            here = conc[pl.ds(16 * z + 8 * h, 8)]
            rhs = here - spread * here
            if z > 0:
                rhs = rhs + lower * conc[pl.ds(16 * (z - 1) + 8 * h, 8)]
            if z < rows - 1:
                rhs = rhs + upper * conc[pl.ds(16 * (z + 1) + 8 * h, 8)]
            return 1.0 + spread, lower, upper, rhs

        state = {}
        for z_up in range(half):
            for side in range(2):
                z = z_up if side == 0 else rows - 1 - z_up
                main, lower, upper, rhs = coefficients(z)
                back, ahead = (lower, upper) if side == 0 else (upper, lower)
                if z_up == 0:
                    r = reciprocal(main)
                    d, e, k = rhs * r, back * r, ahead * r
                    first = (d, e, k)
                else:
                    d, e, k, first = state[side]
                    r = reciprocal(main - back * k)
                    d, e, k = (rhs + back * d) * r, (back * e) * r, ahead * r
                    first = (first[0] + first[2] * d, first[1] + first[2] * e, first[2] * k)
                state[side] = (d, e, k, first)
                at = pl.ds(16 * z + 8 * h, 8)
                offset[at] = d
                edge[at] = e
                link[at] = k
        (d0, e0, k0, first), (d1, e1, k1, last) = state[0], state[1]
        r = reciprocal(1.0 - k0 * k1)
        high = ((d1 + k1 * d0) * r, (k1 * e0) * r, e1 * r)
        below = ((d0 + k0 * d1) * r, e0 * r, (k0 * e1) * r)
        values = (
            conc[pl.ds(8 * h, 8)] + first[0] + first[2] * high[0],
            first[1] + first[2] * high[1],
            first[2] * high[2],
            conc[pl.ds(16 * (rows - 1) + 8 * h, 8)] + last[0] + last[2] * below[0],
            last[2] * below[1],
            last[1] + last[2] * below[2],
        )
        for j, value in enumerate(values):
            ends[pl.ds(16 * j + 8 * h, 8)] = value


def bit(wall, r):
    return lax.rem(lax.div(wall, 2**r), 2)


def read_ends(ref, h, n=6):
    return [ref[pl.ds(16 * j + 8 * h, 8)] for j in range(n)]


def ordered(own, got, is_upper):
    return (
        [jnp.where(is_upper, g, o) for o, g in zip(own, got)],
        [jnp.where(is_upper, o, g) for o, g in zip(own, got)],
    )


def merge(a, b):
    r = reciprocal(1.0 - a[5] * b[1])
    top_a = ((a[3] + a[5] * b[0]) * r, a[4] * r, (a[5] * b[2]) * r)
    low_b = ((b[0] + b[1] * a[3]) * r, (b[1] * a[4]) * r, b[2] * r)
    merged = (
        a[0] + a[2] * low_b[0],
        a[1] + a[2] * low_b[1],
        a[2] * low_b[2],
        b[3] + b[4] * top_a[0],
        b[4] * top_a[1],
        b[5] + b[4] * top_a[2],
    )
    return top_a, low_b, merged


def relay_kernel(own, got, _, send, *, level, last):
    wall = lax.axis_index("wall")
    is_upper = bit(wall, level) == 1
    next_upper = bit(wall, level + 1) == 1
    for h in range(2):
        a, b = ordered(read_ends(own, h), read_ends(got, h), is_upper)
        values = merge(a, b)[2]
        if last:
            values = [
                jnp.where(next_upper, values[0], values[3]),
                jnp.where(next_upper, values[1], values[5]),
            ]
        for j, value in enumerate(values):
            send[pl.ds(16 * j + 8 * h, 8)] = value


def faces_kernel(moved, even_got, odd_got, *targets, tiles):
    wall, lat = lax.axis_index("wall"), lax.axis_index("lat")
    lats = lax.axis_size("lat")
    odd_lat = lax.rem(lat, 2) == 1

    def from_lat(q, odd_z, index):
        dirs = x_plus if q in x_plus else x_minus
        at = pl.ds(2 * tiles * dirs.index(q) + 2 * index + (1 if odd_z else 0), 1)
        use_even = odd_lat if q in x_plus else jnp.logical_not(odd_lat)
        exists = lat > 0 if q in x_plus else lat < lats - 1
        row = jnp.where(use_even, even_got[at], odd_got[at])
        return jnp.where(exists, row, 0.0)

    def fill(target, dirs):
        for j, q in enumerate(dirs):
            up = lattice_dirs[q][2] > 0
            target[pl.ds(4 * j, 4)] = moved[q, pl.ds(8 * tiles + 8, 4) if up else pl.ds(4, 4)]
            step_x = lattice_dirs[q][0]
            if step_x:
                at = 4 * j + (0 if step_x > 0 else 3)
                target[pl.ds(at, 1)] = from_lat(q, up, tiles - 1 if up else 0)
        target[pl.ds(20, 4)] = jnp.zeros((4, LANES), F32)

    for r, target in enumerate(targets):
        pl.when(bit(wall, r) == 0)(functools.partial(fill, target, z_plus))
        pl.when(bit(wall, r) == 1)(functools.partial(fill, target, z_minus))


def solve_ions(owns, gots, offset, edge, link, solved, write, *, rows):
    levels = len(owns)
    wall = lax.axis_index("wall")
    half = rows // 2
    inner = []
    for h in range(2):
        top = levels - 1
        go, xo = read_ends(owns[top], h, 2)
        gr, xr = read_ends(gots[top], h, 2)
        w = (gr + xr * go) * reciprocal(1.0 - xo * xr)
        is_upper = bit(wall, top) == 1
        w_low, w_high = jnp.where(is_upper, w, 0.0), jnp.where(is_upper, 0.0, w)
        for r in range(top - 1, -1, -1):
            is_upper = bit(wall, r) == 1
            a, b = ordered(read_ends(owns[r], h), read_ends(gots[r], h), is_upper)
            top_a, low_b, _ = merge(a, b)
            new_low = top_a[0] + top_a[1] * w_low + top_a[2] * w_high
            new_high = low_b[0] + low_b[1] * w_low + low_b[2] * w_high
            w_low, w_high = (
                jnp.where(is_upper, new_low, w_low),
                jnp.where(is_upper, w_high, new_high),
            )
        at0, at1 = pl.ds(16 * (half - 1) + 8 * h, 8), pl.ds(16 * half + 8 * h, 8)
        a0 = offset[at0] + edge[at0] * w_low
        a1 = offset[at1] + edge[at1] * w_high
        k0, k1 = link[at0], link[at1]
        r = reciprocal(1.0 - k0 * k1)
        u0, u1 = (a0 + k0 * a1) * r, (a1 + k1 * a0) * r
        solved[at0] = u0
        solved[at1] = u1
        inner.append([u0, u1, w_low, w_high])
    for i in range(1, half):
        for h in range(2):
            u0, u1, w_low, w_high = inner[h]
            at0 = pl.ds(16 * (half - 1 - i) + 8 * h, 8)
            at1 = pl.ds(16 * (half + i) + 8 * h, 8)
            u0 = (offset[at0] + edge[at0] * w_low) + link[at0] * u0
            u1 = (offset[at1] + edge[at1] * w_high) + link[at1] * u1
            solved[at0] = u0
            solved[at1] = u1
            inner[h] = [u0, u1, w_low, w_high]
        if i == half // 2 - 1:
            write(0, half - half // 2, 2 * (half // 2))
    write(1, 0, half - half // 2)
    write(2, half + half // 2, half - half // 2)


def outputs_kernel(*refs, rows, tiles, levels):
    it = iter(refs)
    owns = [next(it) for _ in range(levels)]
    gots = [next(it) for _ in range(levels)]
    offset, edge, link, moved, even_got, odd_got, _ = [next(it) for _ in range(7)]
    pops_out, conc_out, tops, patched, solved, sems = [next(it) for _ in range(6)]
    lat, lats = lax.axis_index("lat"), lax.axis_size("lat")
    odd_lat = lax.rem(lat, 2) == 1
    body = pl.ds(8, 8 * tiles)
    copies = []

    def start(source, target):
        copies.append(pltpu.make_async_copy(source, target, sems.at[len(copies)]))
        copies[-1].start()

    for q in range(DIRS):
        if lattice_dirs[q][0] == 0:
            start(moved.at[q, body], pops_out.at[q])
    order = {q: j for j, q in enumerate(x_plus + x_minus)}

    def fill(dirs, got, keep):
        for j, q in enumerate(dirs):
            for k in range(tiles + 2):
                patched[order[q], pl.ds(8 * k, 8)] = moved[q, pl.ds(8 * k, 8)]
            even_z = got[pl.ds(2 * tiles * j, tiles, stride=2)]
            odd_z = got[pl.ds(2 * tiles * j + 1, tiles, stride=2)]
            patched[order[q], pl.ds(out_odd(q), tiles, stride=8)] = jnp.where(keep, even_z, 0.0)
            patched[order[q], pl.ds(out_even(q), tiles, stride=8)] = jnp.where(keep, odd_z, 0.0)

    @pl.when(odd_lat)
    def _():
        fill(x_plus, even_got, lat > 0)
        fill(x_minus, odd_got, lat < lats - 1)

    @pl.when(jnp.logical_not(odd_lat))
    def _():
        fill(x_plus, odd_got, lat > 0)
        fill(x_minus, even_got, lat < lats - 1)

    for q in x_plus + x_minus:
        start(patched.at[order[q], body], pops_out.at[q])
    for j, q in enumerate(z_plus + z_minus):
        at = pl.ds(8, 8) if lattice_dirs[q][2] > 0 else pl.ds(8 * tiles, 8)
        tops[pl.ds(8 * j, 8)] = patched[order[q], at] if q in order else moved[q, at]

    def write(_, begin, count):
        span = pl.ds(16 * begin, 16 * count)
        start(solved.at[span], conc_out.at[span])

    solve_ions(owns, gots, offset, edge, link, solved, write, rows=rows)
    for copy in copies:
        copy.wait()


def patch_kernel(*refs, tiles, levels):
    gots = refs[:levels]
    tops, _, pops_out, fixed, sem = refs[levels:]
    wall = lax.axis_index("wall")
    for j in range(len(z_plus) + len(z_minus)):
        fixed[pl.ds(8 * j, 8)] = tops[pl.ds(8 * j, 8)]

    def put(got, lower):
        for j in range(5):
            row = 8 * j if lower else 8 * (5 + j) + 4
            fixed[pl.ds(row, 4)] = got[pl.ds(4 * j, 4)]

    for r in range(levels):
        rest = lax.rem(wall, 2 ** (r + 1))
        pl.when(rest == 2**r)(functools.partial(put, gots[r], True))
        pl.when(rest == 2**r - 1)(functools.partial(put, gots[r], False))
    for j, q in enumerate(z_plus + z_minus):
        at = pl.ds(0, 8) if lattice_dirs[q][2] > 0 else pl.ds(8 * tiles - 8, 8)
        pltpu.make_async_copy(fixed.at[pl.ds(8 * j, 8)], pops_out.at[q, at], sem).start()
    pltpu.make_async_copy(fixed, fixed, sem).wait()


def swaps(lats, walls):
    def pairs(partner):
        table = []
        for lat in range(lats):
            for wall in range(walls):
                to_lat, to_wall = partner(lat, wall)
                table.append((lat * walls + wall, to_lat * walls + to_wall))
        return table

    def odd_partner(lat, wall):
        if lat == 0 or lat == lats - 1:
            return lat, wall ^ 1
        return ((lat + 1) ^ 1) - 1, wall

    even = pairs(lambda lat, wall: (lat ^ 1, wall))
    odd = pairs(odd_partner)
    levels = []
    while 2 ** len(levels) < walls:
        flip = 2 ** (len(levels) + 1) - 1
        levels.append(pairs(lambda lat, wall: (lat, wall ^ flip)))
    return even, odd, levels


def per_device(
    populations, concentration, cell_flags, valence, diffusivity, applied_field, *, lats, walls
):
    rows, cells = populations.shape[1], populations.shape[1] * populations.shape[2]
    tiles = cells // 8
    chunks = [1] * (rows // 8)
    assert populations.shape[2] == X_CELLS and lats % 2 == 0 and walls >= 4
    even, odd, levels = swaps(lats, walls)
    assert 2 ** len(levels) == walls

    def move(x, table):
        return lax.ppermute(x, ("lat", "wall"), table)

    msg_rows = 2 * tiles * 5
    even_msg, odd_msg, pops, conc, flags, table = pl.pallas_call(
        functools.partial(edges_kernel, chunks=chunks),
        out_shape=(
            on_chip(msg_rows, LANES),
            on_chip(msg_rows, LANES),
            on_chip(DIRS + SPECIES, cells, LANES),
            on_chip(cells * SPECIES, LANES),
            on_chip(cells, LANES, dtype=jnp.int32),
            on_chip(104, LANES),
        ),
        in_specs=[ANY_SPEC] * 6,
        out_specs=(VMEM_SPEC,) * 6,
        scratch_shapes=[
            pltpu.SMEM((SPECIES,), jnp.int32),
            pltpu.SMEM((SPECIES,), F32),
            pltpu.SMEM((3,), F32),
            pltpu.SemaphoreType.DMA((4 + len(chunks),)),
        ],
        compiler_params=params(),
        cost_estimate=cost(2_000_000, 3_000_000),
        name="edges",
    )(
        *in_hbm(
            populations.reshape(DIRS, cells, LANES),
            concentration.reshape(cells * SPECIES, LANES),
            cell_flags.reshape(cells, LANES),
            valence,
            diffusivity,
            applied_field,
        )
    )
    odd_got = move(odd_msg, odd)
    even_got = move(even_msg, even)

    mid, offset, edge, link, ends = pl.pallas_call(
        functools.partial(eliminate_kernel, rows=rows),
        out_shape=(on_chip(10, cells, LANES),)
        + (on_chip(cells * SPECIES, LANES),) * 3
        + (on_chip(96, LANES),),
        in_specs=[VMEM_SPEC] * 4,
        out_specs=(VMEM_SPEC,) * 5,
        compiler_params=params(),
        cost_estimate=cost(5_000_000, 3_000_000),
        name="eliminate",
    )(*pin(pops, conc, flags, table))

    moved = pl.pallas_call(
        functools.partial(collide_kernel, tiles=tiles),
        out_shape=on_chip(DIRS, cells + 16, LANES),
        in_specs=[VMEM_SPEC] * 3,
        out_specs=VMEM_SPEC,
        compiler_params=params(),
        cost_estimate=cost(5_000_000, 3_000_000),
        name="collide",
    )(*pin(pops, flags, mid))

    depth = len(levels)
    owns, gots = [ends], [move(ends, levels[0])]
    for level in range(depth - 1):
        last = level == depth - 2
        sent = pl.pallas_call(
            functools.partial(relay_kernel, level=level, last=last),
            out_shape=on_chip(32 if last else 96, LANES),
            in_specs=[VMEM_SPEC] * 3,
            out_specs=VMEM_SPEC,
            compiler_params=params(),
            cost_estimate=cost(100_000, 200_000),
            name=f"relay{level}",
        )(*pin(owns[-1], gots[-1], moved))
        owns.append(sent)
        gots.append(move(sent, levels[level + 1]))

    faces = pl.pallas_call(
        functools.partial(faces_kernel, tiles=tiles),
        out_shape=(on_chip(FACE_ROWS, LANES),) + (on_chip(FACE_ROWS + 8, LANES),) * (depth - 1),
        in_specs=[VMEM_SPEC] * 3,
        out_specs=(VMEM_SPEC,) * depth,
        compiler_params=params(),
        cost_estimate=cost(100_000, 200_000),
        name="faces",
    )(*pin(moved, even_got, odd_got))
    face_gots = [move(face, table) for face, table in zip(faces, levels)]

    operands = pin(*owns, *gots, offset, edge, link, moved, even_got, odd_got, faces[-1])
    pops_out, new_conc, tops = pl.pallas_call(
        functools.partial(outputs_kernel, rows=rows, tiles=tiles, levels=depth),
        out_shape=(
            jax.ShapeDtypeStruct((DIRS, cells, LANES), F32),
            jax.ShapeDtypeStruct((cells * SPECIES, LANES), F32),
            on_chip(80, LANES),
        ),
        in_specs=[VMEM_SPEC] * len(operands),
        out_specs=(ANY_SPEC, ANY_SPEC, VMEM_SPEC),
        scratch_shapes=[
            pltpu.VMEM((10, cells + 16, LANES), F32),
            pltpu.VMEM((cells * SPECIES, LANES), F32),
            pltpu.SemaphoreType.DMA((DIRS + 3,)),
        ],
        compiler_params=params(),
        cost_estimate=cost(1_000_000, 2_500_000),
        name="outputs",
    )(*operands)

    new_pops = pl.pallas_call(
        functools.partial(patch_kernel, tiles=tiles, levels=depth),
        out_shape=jax.ShapeDtypeStruct((DIRS, cells, LANES), F32),
        in_specs=[VMEM_SPEC] * (depth + 1) + [ANY_SPEC],
        out_specs=ANY_SPEC,
        input_output_aliases={depth + 1: 0},
        scratch_shapes=[
            pltpu.VMEM((80, LANES), F32),
            pltpu.SemaphoreType.DMA,
        ],
        compiler_params=params(),
        cost_estimate=cost(10_000, 100_000),
        name="patch",
    )(*pin(*face_gots, tops), pops_out)
    return new_pops.reshape(populations.shape), new_conc.reshape(concentration.shape)


def solution(mesh):
    in_specs = (
        P(None, "wall", "lat", None),
        P("wall", None, "lat", None),
        P("wall", "lat", None),
        P(),
        P(),
        P(),
    )
    out_specs = (P(None, "wall", "lat", None), P("wall", None, "lat", None))
    return jax.shard_map(
        functools.partial(per_device, lats=mesh.shape["lat"], walls=mesh.shape["wall"]),
        mesh=mesh,
        in_specs=in_specs,
        out_specs=out_specs,
        check_vma=False,
    )
```

```python
import functools

import jax
import jax.numpy as jnp
from jax import lax
from jax.experimental import pallas as pl
from jax.experimental.pallas import tpu as pltpu
from jax.sharding import PartitionSpec as P

lattice_dirs = (
    (0, 0, 0),
    (1, 0, 0),
    (-1, 0, 0),
    (0, 1, 0),
    (0, -1, 0),
    (0, 0, 1),
    (0, 0, -1),
    (1, 1, 0),
    (-1, -1, 0),
    (1, -1, 0),
    (-1, 1, 0),
    (1, 0, 1),
    (-1, 0, -1),
    (1, 0, -1),
    (-1, 0, 1),
    (0, 1, 1),
    (0, -1, -1),
    (0, 1, -1),
    (0, -1, 1),
)
DIRS = len(lattice_dirs)
FORCE_GAIN = 0.02
X_CELLS = 4
SPECIES = 4
LANES = 128
F32 = jnp.float32

x_plus = tuple(q for q in range(DIRS) if lattice_dirs[q][0] == 1)
x_minus = tuple(q for q in range(DIRS) if lattice_dirs[q][0] == -1)
z_plus = tuple(q for q in range(DIRS) if lattice_dirs[q][2] == 1)
z_minus = tuple(q for q in range(DIRS) if lattice_dirs[q][2] == -1)
FACE_ROWS = 24

VMEM_SPEC = pl.BlockSpec(memory_space=pltpu.VMEM)
ANY_SPEC = pl.BlockSpec(memory_space=pl.ANY)


def on_chip(*shape, dtype=F32):
    return pltpu.VMEM(shape, dtype)


def params():
    return pltpu.CompilerParams(vmem_limit_bytes=24 * 1024 * 1024)


def cost(flops, nbytes):
    return pl.CostEstimate(flops=flops, bytes_accessed=nbytes, transcendentals=0)


def in_hbm(*arrays):
    return [pltpu.with_memory_space_constraint(a, pltpu.HBM) for a in arrays]


def pin(*arrays):
    return [pltpu.with_memory_space_constraint(a, pltpu.VMEM) for a in arrays]


def out_even(q):
    step_x, _, step_z = lattice_dirs[q]
    return {0: 12, 1: 16, -1: 8}[step_z] + (0 if step_x > 0 else 3)


def out_odd(q):
    step_x, _, step_z = lattice_dirs[q]
    return {0: 8, 1: 12, -1: 4}[step_z] + (0 if step_x > 0 else 3)


def low_rows():
    return lax.broadcasted_iota(jnp.int32, (8, LANES), 0) < 4


def density_and_momentum(p):
    diff = {q: p[q] - p[q + 1] for q in range(1, DIRS, 2)}
    total = {q: p[q] + p[q + 1] for q in range(1, DIRS, 2)}
    density = (
        ((p[0] + total[1]) + (total[3] + total[5]))
        + ((total[7] + total[9]) + (total[11] + total[13]))
        + (total[15] + total[17])
    )
    momentum = [
        (diff[1] + diff[7]) + (diff[9] + diff[11]) + diff[13],
        (diff[3] + diff[7]) - (diff[9] - diff[15]) + diff[17],
        (diff[5] + diff[11]) - (diff[13] - diff[15]) - diff[17],
    ]
    return density, momentum


def moments(p, charge, field_xyz):
    density, momentum = density_and_momentum(p)
    force = [charge * f for f in field_xyz]
    inverse = 1.0 / density
    vel = [(momentum[a] + 0.5 * force[a]) * inverse for a in range(3)]
    speed_sq = vel[0] * vel[0] + vel[1] * vel[1] + vel[2] * vel[2]
    work = vel[0] * force[0] + vel[1] * force[1] + vel[2] * force[2]
    base = (1.25 / 36.0 * density) * (1.0 - 1.5 * speed_sq) - (1.125 / 36.0) * work
    odd = [(3.75 / 36.0) * momentum[a] + (3.0 / 36.0) * force[a] for a in range(3)]
    even = [(5.625 / 36.0) * momentum[a] + (6.1875 / 36.0) * force[a] for a in range(3)]
    return base, vel, odd, even


def parts_of(q, base, vel, odd, even):
    axes = [(a, lattice_dirs[q][a]) for a in range(3) if lattice_dirs[q][a]]

    def along(v):
        out = v[axes[0][0]]
        for a, sign in axes[1:]:
            out = out + v[a] if sign > 0 else out - v[a]
        return out

    cu, odd_q, even_q = along(vel), along(odd), along(even)
    if len(axes) == 1:
        return (base + base) + 2.0 * (cu * even_q), odd_q + odd_q
    return base + cu * even_q, odd_q


def edges_kernel(
    pops_hbm,
    conc_hbm,
    flags_hbm,
    valence_hbm,
    diffusivity_hbm,
    field_hbm,
    even_msg,
    odd_msg,
    pops,
    conc,
    flags,
    table,
    valence,
    diffusivity,
    field,
    sems,
    *,
    chunks,
):
    small = [
        pltpu.make_async_copy(source, target, sems.at[i])
        for i, (source, target) in enumerate(
            (
                (flags_hbm, flags),
                (valence_hbm, valence),
                (field_hbm, field),
                (diffusivity_hbm, diffusivity),
            )
        )
    ]
    arrived = {}
    at = 0
    for c, count in enumerate(chunks):
        rows = pl.ds(32 * at, 32 * count)
        crows = pl.ds(128 * at, 128 * count)
        sem = sems.at[4 + c]
        pltpu.make_async_copy(conc_hbm.at[crows], conc.at[crows], sem).start()
        pltpu.make_async_copy(pops_hbm.at[:, rows], pops.at[pl.ds(0, DIRS), rows], sem).start()
        both = pops.at[:, rows]
        arrived[at] = pltpu.make_async_copy(both, both, sem)
        at += count
        if c == 0:
            for copy in small:
                copy.start()
    low = low_rows()
    for copy in small:
        copy.wait()
    val = [valence[s].astype(F32) for s in range(SPECIES)]
    field_xyz = [FORCE_GAIN * field[axis] for axis in range(3)]
    values = [jnp.full((8, LANES), f, F32) for f in field_xyz]
    for h in range(2):
        diff = jnp.where(low, diffusivity[2 * h], diffusivity[2 * h + 1])
        val_pair = jnp.where(low, val[2 * h], val[2 * h + 1])
        values += [
            val_pair,
            diff,
            diff * 0.01,
            diff * jnp.where(val_pair > 0, 0.5, 0.02),
            val_pair * field[2],
        ]
    for j, value in enumerate(values):
        table[pl.ds(8 * j, 8)] = value
    is_odd = lax.rem(lax.axis_index("lat"), 2) == 1
    for g in range(sum(chunks)):
        if g in arrived:
            arrived[g].wait()
        sent = {}
        for x, dirs in ((X_CELLS - 1, x_plus), (0, x_minus)):
            at = pl.ds(32 * g + x, 8, stride=4)
            p = [pops[q, at] for q in range(DIRS)]
            solid = flags[at] != 0
            terms = [
                val[s] * conc[pl.ds(128 * g + 4 * s + x, 8, stride=16)] for s in range(SPECIES)
            ]
            charge = (terms[0] + terms[1]) + (terms[2] + terms[3])
            found = moments(p, charge, field_xyz)
            for j, q in enumerate(dirs):
                first = q if q % 2 else q - 1
                shared, odd = parts_of(first, *found)
                relaxed = (shared + odd if q % 2 else shared - odd) - 0.25 * p[q]
                value = jnp.where(solid, p[q + 1 if q % 2 else q - 1], relaxed)
                step_y = lattice_dirs[q][1]
                if step_y:
                    value = pltpu.roll(value, step_y % LANES, axis=1)
                sent[x, j] = value
        for j in range(5):
            plus, minus = sent[X_CELLS - 1, j], sent[0, j]
            at = pl.ds(8 * sum(chunks) * j + 8 * g, 8)
            even_msg[at] = jnp.where(is_odd, minus, plus)
            odd_msg[at] = jnp.where(is_odd, plus, minus)


def write_faces(target, start, moved, level, tiles):
    def fill(dirs):
        for j, q in enumerate(dirs):
            rows = pl.ds(8 * tiles + 8, 4) if lattice_dirs[q][2] > 0 else pl.ds(4, 4)
            target[pl.ds(start + 4 * j, 4)] = moved[q, rows]
        target[pl.ds(start + 20, 4)] = jnp.zeros((4, LANES), F32)

    is_upper = bit(lax.axis_index("wall"), level) == 1
    pl.when(jnp.logical_not(is_upper))(functools.partial(fill, z_plus))
    pl.when(is_upper)(functools.partial(fill, z_minus))


def collide_kernel(pops, flags, mid, moved, pair_faces, *, tiles):
    def scatter(at):
        solid = flags[pl.ds(at, 8)] != 0
        base, *rest = [mid[j, pl.ds(at, 8)] for j in range(10)]
        p0 = pops[0, pl.ds(at, 8)]
        moved[0, pl.ds(8 + at, 8)] = jnp.where(solid, p0, 12.0 * base - 0.25 * p0)
        for q in range(1, DIRS, 2):
            shared, odd = parts_of(q, base, rest[:3], rest[3:6], rest[6:])
            ahead, behind = pops[q, pl.ds(at, 8)], pops[q + 1, pl.ds(at, 8)]
            for d, relaxed, bounced in (
                (q, (shared + odd) - 0.25 * ahead, behind),
                (q + 1, (shared - odd) - 0.25 * behind, ahead),
            ):
                step_x, step_y, step_z = lattice_dirs[d]
                value = jnp.where(solid, bounced, relaxed)
                if step_y:
                    value = pltpu.roll(value, step_y % LANES, axis=1)
                if step_x:
                    value = pltpu.roll(value, step_x % 8, axis=0)
                moved[d, pl.ds(8 + at + 4 * step_z, 8)] = value

    for k in range(tiles):
        scatter(8 * k)
    for d in z_plus + z_minus:
        at = 8 if lattice_dirs[d][2] > 0 else 8 * tiles + 4
        moved[d, pl.ds(at, 4)] = jnp.zeros((4, LANES), F32)
    write_faces(pair_faces, 0, moved, 0, tiles)


def reciprocal(x):
    return 1.0 / x


def eliminate_kernel(
    pops, conc, flags, table, mid, offset, edge, link, ends, *, rows
):
    low = low_rows()
    half = rows // 2
    field_xyz = [table[pl.ds(8 * a, 8)] for a in range(3)]
    val_pair = [table[pl.ds(8 * (3 + 5 * h), 8)] for h in range(2)]
    for k in range(half):
        at = 8 * k
        sums = []
        for z in range(2):
            part = val_pair[0] * conc[pl.ds(4 * at + 16 * z, 8)]
            part = part + val_pair[1] * conc[pl.ds(4 * at + 16 * z + 8, 8)]
            sums.append(part + pltpu.roll(part, 4, axis=0))
        charge = jnp.where(low, sums[0], sums[1])
        base, vel, odd, even = moments(
            [pops[q, pl.ds(at, 8)] for q in range(DIRS)], charge, field_xyz
        )
        for j, value in enumerate((base, *vel, *odd, *even)):
            mid[j, pl.ds(at, 8)] = value
    for h in range(2):
        diff, slow, membrane, pull = [table[pl.ds(8 * (4 + 5 * h + j), 8)] for j in range(4)]

        def coefficients(z):
            tile = pl.ds(8 * (z // 2), 8)
            vz, flag = mid[3, tile], flags[tile]
            mine = low if z % 2 == 0 else jnp.logical_not(low)
            vz = jnp.where(mine, vz, pltpu.roll(vz, 4, axis=0))
            flag = jnp.where(mine, flag, pltpu.roll(flag, 4, axis=0))
            spread = jnp.where(flag == 0, diff, jnp.where(flag == 1, slow, membrane))
            drift = spread * jnp.tanh(2.0 * vz + pull)
            lower = 0.5 * spread + 0.25 * drift
            upper = 0.5 * spread - 0.25 * drift
            here = conc[pl.ds(16 * z + 8 * h, 8)]
            rhs = here - spread * here
            if z > 0:
                rhs = rhs + lower * conc[pl.ds(16 * (z - 1) + 8 * h, 8)]
            if z < rows - 1:
                rhs = rhs + upper * conc[pl.ds(16 * (z + 1) + 8 * h, 8)]
            return 1.0 + spread, lower, upper, rhs

        state = {}
        for z_up in range(half):
            for side in range(2):
                z = z_up if side == 0 else rows - 1 - z_up
                main, lower, upper, rhs = coefficients(z)
                back, ahead = (lower, upper) if side == 0 else (upper, lower)
                if z_up == 0:
                    r = reciprocal(main)
                    d, e, k = rhs * r, back * r, ahead * r
                    first = (d, e, k)
                else:
                    d, e, k, first = state[side]
                    r = reciprocal(main - back * k)
                    d, e, k = (rhs + back * d) * r, (back * e) * r, ahead * r
                    first = (first[0] + first[2] * d, first[1] + first[2] * e, first[2] * k)
                state[side] = (d, e, k, first)
                at = pl.ds(16 * z + 8 * h, 8)
                offset[at] = d
                edge[at] = e
                link[at] = k
        (d0, e0, k0, first), (d1, e1, k1, last) = state[0], state[1]
        r = reciprocal(1.0 - k0 * k1)
        high = ((d1 + k1 * d0) * r, (k1 * e0) * r, e1 * r)
        below = ((d0 + k0 * d1) * r, e0 * r, (k0 * e1) * r)
        values = (
            conc[pl.ds(8 * h, 8)] + first[0] + first[2] * high[0],
            first[1] + first[2] * high[1],
            first[2] * high[2],
            conc[pl.ds(16 * (rows - 1) + 8 * h, 8)] + last[0] + last[2] * below[0],
            last[2] * below[1],
            last[1] + last[2] * below[2],
        )
        for j, value in enumerate(values):
            ends[pl.ds(16 * j + 8 * h, 8)] = value


def bit(wall, r):
    return lax.rem(lax.div(wall, 2**r), 2)


def read_ends(ref, h, n=6):
    return [ref[pl.ds(16 * j + 8 * h, 8)] for j in range(n)]


def ordered(own, got, is_upper):
    return (
        [jnp.where(is_upper, g, o) for o, g in zip(own, got)],
        [jnp.where(is_upper, o, g) for o, g in zip(own, got)],
    )


def merge(a, b):
    r = reciprocal(1.0 - a[5] * b[1])
    top_a = ((a[3] + a[5] * b[0]) * r, a[4] * r, (a[5] * b[2]) * r)
    low_b = ((b[0] + b[1] * a[3]) * r, (b[1] * a[4]) * r, b[2] * r)
    merged = (
        a[0] + a[2] * low_b[0],
        a[1] + a[2] * low_b[1],
        a[2] * low_b[2],
        b[3] + b[4] * top_a[0],
        b[4] * top_a[1],
        b[5] + b[4] * top_a[2],
    )
    return top_a, low_b, merged


def relay_kernel(own, got, moved, send, *, level, last, tiles):
    wall = lax.axis_index("wall")
    is_upper = bit(wall, level) == 1
    next_upper = bit(wall, level + 1) == 1
    for h in range(2):
        a, b = ordered(read_ends(own, h), read_ends(got, h), is_upper)
        values = merge(a, b)[2]
        if last:
            values = [
                jnp.where(next_upper, values[0], values[3]),
                jnp.where(next_upper, values[1], values[5]),
            ]
        for j, value in enumerate(values):
            send[pl.ds(16 * j + 8 * h, 8)] = value
    write_faces(send, 16 * len(values), moved, level + 1, tiles)


def faces_kernel(even_got, odd_got, *targets, tiles):
    wall, lat = lax.axis_index("wall"), lax.axis_index("lat")
    lats = lax.axis_size("lat")
    odd_lat = lax.rem(lat, 2) == 1

    def from_lat(q, odd_z, index):
        dirs = x_plus if q in x_plus else x_minus
        at = pl.ds(2 * tiles * dirs.index(q) + 2 * index + (1 if odd_z else 0), 1)
        use_even = odd_lat if q in x_plus else jnp.logical_not(odd_lat)
        exists = lat > 0 if q in x_plus else lat < lats - 1
        row = jnp.where(use_even, even_got[at], odd_got[at])
        return jnp.where(exists, row, 0.0)

    def fill(target, dirs):
        target[...] = jnp.zeros(target.shape, F32)
        for j, q in enumerate([q for q in dirs if lattice_dirs[q][0]]):
            up = lattice_dirs[q][2] > 0
            target[pl.ds(j, 1)] = from_lat(q, up, tiles - 1 if up else 0)

    for r, target in enumerate(targets):
        pl.when(bit(wall, r) == 0)(functools.partial(fill, target, z_plus))
        pl.when(bit(wall, r) == 1)(functools.partial(fill, target, z_minus))


def solve_ions(owns, gots, offset, edge, link, solved, write, *, rows):
    levels = len(owns)
    wall = lax.axis_index("wall")
    half = rows // 2
    inner = []
    for h in range(2):
        top = levels - 1
        go, xo = read_ends(owns[top], h, 2)
        gr, xr = read_ends(gots[top], h, 2)
        w = (gr + xr * go) * reciprocal(1.0 - xo * xr)
        is_upper = bit(wall, top) == 1
        w_low, w_high = jnp.where(is_upper, w, 0.0), jnp.where(is_upper, 0.0, w)
        for r in range(top - 1, -1, -1):
            is_upper = bit(wall, r) == 1
            a, b = ordered(read_ends(owns[r], h), read_ends(gots[r], h), is_upper)
            top_a, low_b, _ = merge(a, b)
            new_low = top_a[0] + top_a[1] * w_low + top_a[2] * w_high
            new_high = low_b[0] + low_b[1] * w_low + low_b[2] * w_high
            w_low, w_high = (
                jnp.where(is_upper, new_low, w_low),
                jnp.where(is_upper, w_high, new_high),
            )
        at0, at1 = pl.ds(16 * (half - 1) + 8 * h, 8), pl.ds(16 * half + 8 * h, 8)
        a0 = offset[at0] + edge[at0] * w_low
        a1 = offset[at1] + edge[at1] * w_high
        k0, k1 = link[at0], link[at1]
        r = reciprocal(1.0 - k0 * k1)
        u0, u1 = (a0 + k0 * a1) * r, (a1 + k1 * a0) * r
        solved[at0] = u0
        solved[at1] = u1
        inner.append([u0, u1, w_low, w_high])
    for i in range(1, half):
        for h in range(2):
            u0, u1, w_low, w_high = inner[h]
            at0 = pl.ds(16 * (half - 1 - i) + 8 * h, 8)
            at1 = pl.ds(16 * (half + i) + 8 * h, 8)
            u0 = (offset[at0] + edge[at0] * w_low) + link[at0] * u0
            u1 = (offset[at1] + edge[at1] * w_high) + link[at1] * u1
            solved[at0] = u0
            solved[at1] = u1
            inner[h] = [u0, u1, w_low, w_high]
        if i == half // 2 - 1:
            write(0, half - half // 2, 2 * (half // 2))
    write(1, 0, half - half // 2)
    write(2, half + half // 2, half - half // 2)


def outputs_kernel(*refs, rows, tiles, levels):
    it = iter(refs)
    owns = [next(it) for _ in range(levels)]
    gots = [next(it) for _ in range(levels)]
    offset, edge, link, moved, even_got, odd_got, _ = [next(it) for _ in range(7)]
    pops_out, conc_out, tops, patched, solved, sems = [next(it) for _ in range(6)]
    lat, lats = lax.axis_index("lat"), lax.axis_size("lat")
    odd_lat = lax.rem(lat, 2) == 1
    body = pl.ds(8, 8 * tiles)
    copies = []

    def start(source, target):
        copies.append(pltpu.make_async_copy(source, target, sems.at[len(copies)]))
        copies[-1].start()

    for q in range(DIRS):
        if lattice_dirs[q][0] == 0:
            start(moved.at[q, body], pops_out.at[q])
    order = {q: j for j, q in enumerate(x_plus + x_minus)}

    def fill(dirs, got, keep):
        for j, q in enumerate(dirs):
            for k in range(tiles + 2):
                patched[order[q], pl.ds(8 * k, 8)] = moved[q, pl.ds(8 * k, 8)]
            even_z = got[pl.ds(2 * tiles * j, tiles, stride=2)]
            odd_z = got[pl.ds(2 * tiles * j + 1, tiles, stride=2)]
            patched[order[q], pl.ds(out_odd(q), tiles, stride=8)] = jnp.where(keep, even_z, 0.0)
            patched[order[q], pl.ds(out_even(q), tiles, stride=8)] = jnp.where(keep, odd_z, 0.0)

    @pl.when(odd_lat)
    def _():
        fill(x_plus, even_got, lat > 0)
        fill(x_minus, odd_got, lat < lats - 1)

    @pl.when(jnp.logical_not(odd_lat))
    def _():
        fill(x_plus, odd_got, lat > 0)
        fill(x_minus, even_got, lat < lats - 1)

    for q in x_plus + x_minus:
        start(patched.at[order[q], body], pops_out.at[q])
    for j, q in enumerate(z_plus + z_minus):
        at = pl.ds(8, 8) if lattice_dirs[q][2] > 0 else pl.ds(8 * tiles, 8)
        tops[pl.ds(8 * j, 8)] = patched[order[q], at] if q in order else moved[q, at]

    def write(_, begin, count):
        span = pl.ds(16 * begin, 16 * count)
        start(solved.at[span], conc_out.at[span])

    solve_ions(owns, gots, offset, edge, link, solved, write, rows=rows)
    for copy in copies:
        copy.wait()


def patch_kernel(*refs, tiles, levels):
    gots, faces = refs[:levels], refs[levels : 2 * levels]
    tops, _, pops_out, fixed, sem = refs[2 * levels :]
    wall = lax.axis_index("wall")
    for j in range(len(z_plus) + len(z_minus)):
        fixed[pl.ds(8 * j, 8)] = tops[pl.ds(8 * j, 8)]

    def put(r, lower):
        base = 0 if r == 0 else 32 if r == levels - 1 else 96
        row_of_x = 0
        for j, q in enumerate(z_plus if lower else z_minus):
            row = 8 * j if lower else 8 * (5 + j) + 4
            fixed[pl.ds(row, 4)] = faces[r][pl.ds(base + 4 * j, 4)]
            step_x = lattice_dirs[q][0]
            if step_x:
                row += 0 if step_x > 0 else 3
                fixed[pl.ds(row, 1)] = gots[r][pl.ds(row_of_x, 1)]
                row_of_x += 1

    for r in range(levels):
        rest = lax.rem(wall, 2 ** (r + 1))
        pl.when(rest == 2**r)(functools.partial(put, r, True))
        pl.when(rest == 2**r - 1)(functools.partial(put, r, False))
    for j, q in enumerate(z_plus + z_minus):
        at = pl.ds(0, 8) if lattice_dirs[q][2] > 0 else pl.ds(8 * tiles - 8, 8)
        pltpu.make_async_copy(fixed.at[pl.ds(8 * j, 8)], pops_out.at[q, at], sem).start()
    pltpu.make_async_copy(fixed, fixed, sem).wait()


def swaps(lats, walls):
    def pairs(partner):
        table = []
        for lat in range(lats):
            for wall in range(walls):
                to_lat, to_wall = partner(lat, wall)
                table.append((lat * walls + wall, to_lat * walls + to_wall))
        return table

    def odd_partner(lat, wall):
        if lat == 0 or lat == lats - 1:
            return lat, wall ^ 1
        return ((lat + 1) ^ 1) - 1, wall

    even = pairs(lambda lat, wall: (lat ^ 1, wall))
    odd = pairs(odd_partner)
    levels = []
    while 2 ** len(levels) < walls:
        flip = 2 ** (len(levels) + 1) - 1
        levels.append(pairs(lambda lat, wall: (lat, wall ^ flip)))
    return even, odd, levels


def per_device(
    populations, concentration, cell_flags, valence, diffusivity, applied_field, *, lats, walls
):
    rows, cells = populations.shape[1], populations.shape[1] * populations.shape[2]
    tiles = cells // 8
    chunks = [1] * (rows // 8)
    assert populations.shape[2] == X_CELLS and lats % 2 == 0 and walls >= 4
    even, odd, levels = swaps(lats, walls)
    assert 2 ** len(levels) == walls

    def move(x, table):
        return lax.ppermute(x, ("lat", "wall"), table)

    msg_rows = 2 * tiles * 5
    even_msg, odd_msg, pops, conc, flags, table = pl.pallas_call(
        functools.partial(edges_kernel, chunks=chunks),
        out_shape=(
            on_chip(msg_rows, LANES),
            on_chip(msg_rows, LANES),
            on_chip(DIRS + SPECIES, cells, LANES),
            on_chip(cells * SPECIES, LANES),
            on_chip(cells, LANES, dtype=jnp.int32),
            on_chip(104, LANES),
        ),
        in_specs=[ANY_SPEC] * 6,
        out_specs=(VMEM_SPEC,) * 6,
        scratch_shapes=[
            pltpu.SMEM((SPECIES,), jnp.int32),
            pltpu.SMEM((SPECIES,), F32),
            pltpu.SMEM((3,), F32),
            pltpu.SemaphoreType.DMA((4 + len(chunks),)),
        ],
        compiler_params=params(),
        cost_estimate=cost(2_000_000, 3_000_000),
        name="edges",
    )(
        *in_hbm(
            populations.reshape(DIRS, cells, LANES),
            concentration.reshape(cells * SPECIES, LANES),
            cell_flags.reshape(cells, LANES),
            valence,
            diffusivity,
            applied_field,
        )
    )
    odd_got = move(odd_msg, odd)
    even_got = move(even_msg, even)

    mid, offset, edge, link, ends = pl.pallas_call(
        functools.partial(eliminate_kernel, rows=rows),
        out_shape=(on_chip(10, cells, LANES),)
        + (on_chip(cells * SPECIES, LANES),) * 3
        + (on_chip(96, LANES),),
        in_specs=[VMEM_SPEC] * 4,
        out_specs=(VMEM_SPEC,) * 5,
        compiler_params=params(),
        cost_estimate=cost(5_000_000, 3_000_000),
        name="eliminate",
    )(*pin(pops, conc, flags, table))

    moved, pair_faces = pl.pallas_call(
        functools.partial(collide_kernel, tiles=tiles),
        out_shape=(on_chip(DIRS, cells + 16, LANES), on_chip(FACE_ROWS, LANES)),
        in_specs=[VMEM_SPEC] * 3,
        out_specs=(VMEM_SPEC,) * 2,
        compiler_params=params(),
        cost_estimate=cost(5_000_000, 3_000_000),
        name="collide",
    )(*pin(pops, flags, mid))

    depth = len(levels)
    pair_got = move(pair_faces, levels[0])
    owns, gots = [ends], [move(ends, levels[0])]
    for level in range(depth - 1):
        last = level == depth - 2
        sent = pl.pallas_call(
            functools.partial(relay_kernel, level=level, last=last, tiles=tiles),
            out_shape=on_chip((32 if last else 96) + FACE_ROWS, LANES),
            in_specs=[VMEM_SPEC] * 3,
            out_specs=VMEM_SPEC,
            compiler_params=params(),
            cost_estimate=cost(100_000, 200_000),
            name=f"relay{level}",
        )(*pin(owns[-1], gots[-1], moved))
        owns.append(sent)
        gots.append(move(sent, levels[level + 1]))

    faces = pl.pallas_call(
        functools.partial(faces_kernel, tiles=tiles),
        out_shape=(on_chip(8, LANES),) + (on_chip(16, LANES),) * (depth - 1),
        in_specs=[VMEM_SPEC] * 2,
        out_specs=(VMEM_SPEC,) * depth,
        compiler_params=params(),
        cost_estimate=cost(100_000, 200_000),
        name="faces",
    )(*pin(even_got, odd_got))
    face_gots = [move(face, table) for face, table in zip(faces, levels)]

    operands = pin(*owns, *gots, offset, edge, link, moved, even_got, odd_got, faces[-1])
    pops_out, new_conc, tops = pl.pallas_call(
        functools.partial(outputs_kernel, rows=rows, tiles=tiles, levels=depth),
        out_shape=(
            jax.ShapeDtypeStruct((DIRS, cells, LANES), F32),
            jax.ShapeDtypeStruct((cells * SPECIES, LANES), F32),
            on_chip(80, LANES),
        ),
        in_specs=[VMEM_SPEC] * len(operands),
        out_specs=(ANY_SPEC, ANY_SPEC, VMEM_SPEC),
        scratch_shapes=[
            pltpu.VMEM((10, cells + 16, LANES), F32),
            pltpu.VMEM((cells * SPECIES, LANES), F32),
            pltpu.SemaphoreType.DMA((DIRS + 3,)),
        ],
        compiler_params=params(),
        cost_estimate=cost(1_000_000, 2_500_000),
        name="outputs",
    )(*operands)

    new_pops = pl.pallas_call(
        functools.partial(patch_kernel, tiles=tiles, levels=depth),
        out_shape=jax.ShapeDtypeStruct((DIRS, cells, LANES), F32),
        in_specs=[VMEM_SPEC] * (2 * depth + 1) + [ANY_SPEC],
        out_specs=ANY_SPEC,
        input_output_aliases={2 * depth + 1: 0},
        scratch_shapes=[
            pltpu.VMEM((80, LANES), F32),
            pltpu.SemaphoreType.DMA,
        ],
        compiler_params=params(),
        cost_estimate=cost(10_000, 100_000),
        name="patch",
    )(*pin(*face_gots, pair_got, *gots[1:], tops), pops_out)
    return new_pops.reshape(populations.shape), new_conc.reshape(concentration.shape)


def solution(mesh):
    in_specs = (
        P(None, "wall", "lat", None),
        P("wall", None, "lat", None),
        P("wall", "lat", None),
        P(),
        P(),
        P(),
    )
    out_specs = (P(None, "wall", "lat", None), P("wall", None, "lat", None))
    return jax.shard_map(
        functools.partial(per_device, lats=mesh.shape["lat"], walls=mesh.shape["wall"]),
        mesh=mesh,
        in_specs=in_specs,
        out_specs=out_specs,
        check_vma=False,
    )
```

```python
import functools

import jax
import jax.numpy as jnp
from jax import lax
from jax.experimental import pallas as pl
from jax.experimental.pallas import tpu as pltpu
from jax.sharding import PartitionSpec as P

lattice_dirs = (
    (0, 0, 0),
    (1, 0, 0),
    (-1, 0, 0),
    (0, 1, 0),
    (0, -1, 0),
    (0, 0, 1),
    (0, 0, -1),
    (1, 1, 0),
    (-1, -1, 0),
    (1, -1, 0),
    (-1, 1, 0),
    (1, 0, 1),
    (-1, 0, -1),
    (1, 0, -1),
    (-1, 0, 1),
    (0, 1, 1),
    (0, -1, -1),
    (0, 1, -1),
    (0, -1, 1),
)
DIRS = len(lattice_dirs)
FORCE_GAIN = 0.02
X_CELLS = 4
SPECIES = 4
LANES = 128
F32 = jnp.float32

x_plus = tuple(q for q in range(DIRS) if lattice_dirs[q][0] == 1)
x_minus = tuple(q for q in range(DIRS) if lattice_dirs[q][0] == -1)
z_plus = tuple(q for q in range(DIRS) if lattice_dirs[q][2] == 1)
z_minus = tuple(q for q in range(DIRS) if lattice_dirs[q][2] == -1)
FACE_ROWS = 24

VMEM_SPEC = pl.BlockSpec(memory_space=pltpu.VMEM)
ANY_SPEC = pl.BlockSpec(memory_space=pl.ANY)


def on_chip(*shape, dtype=F32):
    return pltpu.VMEM(shape, dtype)


def params():
    return pltpu.CompilerParams(vmem_limit_bytes=24 * 1024 * 1024)


def cost(flops, nbytes):
    return pl.CostEstimate(flops=flops, bytes_accessed=nbytes, transcendentals=0)


def in_hbm(*arrays):
    return [pltpu.with_memory_space_constraint(a, pltpu.HBM) for a in arrays]


def pin(*arrays):
    return [pltpu.with_memory_space_constraint(a, pltpu.VMEM) for a in arrays]


def out_even(q):
    step_x, _, step_z = lattice_dirs[q]
    return {0: 12, 1: 16, -1: 8}[step_z] + (0 if step_x > 0 else 3)


def out_odd(q):
    step_x, _, step_z = lattice_dirs[q]
    return {0: 8, 1: 12, -1: 4}[step_z] + (0 if step_x > 0 else 3)


def low_rows():
    return lax.broadcasted_iota(jnp.int32, (8, LANES), 0) < 4


def density_and_momentum(p):
    diff = {q: p[q] - p[q + 1] for q in range(1, DIRS, 2)}
    total = {q: p[q] + p[q + 1] for q in range(1, DIRS, 2)}
    density = (
        ((p[0] + total[1]) + (total[3] + total[5]))
        + ((total[7] + total[9]) + (total[11] + total[13]))
        + (total[15] + total[17])
    )
    momentum = [
        (diff[1] + diff[7]) + (diff[9] + diff[11]) + diff[13],
        (diff[3] + diff[7]) - (diff[9] - diff[15]) + diff[17],
        (diff[5] + diff[11]) - (diff[13] - diff[15]) - diff[17],
    ]
    return density, momentum


def moments(p, charge, field_xyz):
    density, momentum = density_and_momentum(p)
    force = [charge * f for f in field_xyz]
    inverse = 1.0 / density
    vel = [(momentum[a] + 0.5 * force[a]) * inverse for a in range(3)]
    speed_sq = vel[0] * vel[0] + vel[1] * vel[1] + vel[2] * vel[2]
    work = vel[0] * force[0] + vel[1] * force[1] + vel[2] * force[2]
    base = (1.25 / 36.0 * density) * (1.0 - 1.5 * speed_sq) - (1.125 / 36.0) * work
    odd = [(3.75 / 36.0) * momentum[a] + (3.0 / 36.0) * force[a] for a in range(3)]
    even = [(5.625 / 36.0) * momentum[a] + (6.1875 / 36.0) * force[a] for a in range(3)]
    return base, vel, odd, even


def parts_of(q, base, vel, odd, even):
    axes = [(a, lattice_dirs[q][a]) for a in range(3) if lattice_dirs[q][a]]

    def along(v):
        out = v[axes[0][0]]
        for a, sign in axes[1:]:
            out = out + v[a] if sign > 0 else out - v[a]
        return out

    cu, odd_q, even_q = along(vel), along(odd), along(even)
    if len(axes) == 1:
        return (base + base) + 2.0 * (cu * even_q), odd_q + odd_q
    return base + cu * even_q, odd_q


def edges_kernel(
    pops_hbm,
    conc_hbm,
    flags_hbm,
    valence_hbm,
    diffusivity_hbm,
    field_hbm,
    even_msg,
    odd_msg,
    pops,
    conc,
    flags,
    table,
    valence,
    diffusivity,
    field,
    sems,
    *,
    chunks,
):
    small = [
        pltpu.make_async_copy(source, target, sems.at[i])
        for i, (source, target) in enumerate(
            (
                (flags_hbm, flags),
                (valence_hbm, valence),
                (field_hbm, field),
                (diffusivity_hbm, diffusivity),
            )
        )
    ]
    arrived = {}
    at = 0
    for c, count in enumerate(chunks):
        rows = pl.ds(32 * at, 32 * count)
        crows = pl.ds(128 * at, 128 * count)
        sem = sems.at[4 + c]
        pltpu.make_async_copy(conc_hbm.at[crows], conc.at[crows], sem).start()
        pltpu.make_async_copy(pops_hbm.at[:, rows], pops.at[pl.ds(0, DIRS), rows], sem).start()
        both = pops.at[:, rows]
        arrived[at] = pltpu.make_async_copy(both, both, sem)
        at += count
        if c == 0:
            for copy in small:
                copy.start()
    low = low_rows()
    for copy in small:
        copy.wait()
    val = [valence[s].astype(F32) for s in range(SPECIES)]
    field_xyz = [FORCE_GAIN * field[axis] for axis in range(3)]
    values = [jnp.full((8, LANES), f, F32) for f in field_xyz]
    for h in range(2):
        diff = jnp.where(low, diffusivity[2 * h], diffusivity[2 * h + 1])
        val_pair = jnp.where(low, val[2 * h], val[2 * h + 1])
        values += [
            val_pair,
            diff,
            diff * 0.01,
            diff * jnp.where(val_pair > 0, 0.5, 0.02),
            val_pair * field[2],
        ]
    for j, value in enumerate(values):
        table[pl.ds(8 * j, 8)] = value
    is_odd = lax.rem(lax.axis_index("lat"), 2) == 1
    for g in range(sum(chunks)):
        if g in arrived:
            arrived[g].wait()
        sent = {}
        for x, dirs in ((X_CELLS - 1, x_plus), (0, x_minus)):
            at = pl.ds(32 * g + x, 8, stride=4)
            p = [pops[q, at] for q in range(DIRS)]
            solid = flags[at] != 0
            terms = [
                val[s] * conc[pl.ds(128 * g + 4 * s + x, 8, stride=16)] for s in range(SPECIES)
            ]
            charge = (terms[0] + terms[1]) + (terms[2] + terms[3])
            found = moments(p, charge, field_xyz)
            for j, q in enumerate(dirs):
                first = q if q % 2 else q - 1
                shared, odd = parts_of(first, *found)
                relaxed = (shared + odd if q % 2 else shared - odd) - 0.25 * p[q]
                value = jnp.where(solid, p[q + 1 if q % 2 else q - 1], relaxed)
                step_y = lattice_dirs[q][1]
                if step_y:
                    value = pltpu.roll(value, step_y % LANES, axis=1)
                sent[x, j] = value
        for j in range(5):
            plus, minus = sent[X_CELLS - 1, j], sent[0, j]
            at = pl.ds(8 * sum(chunks) * j + 8 * g, 8)
            even_msg[at] = jnp.where(is_odd, minus, plus)
            odd_msg[at] = jnp.where(is_odd, plus, minus)


def write_faces(target, start, moved, level, tiles):
    def fill(dirs):
        for j, q in enumerate(dirs):
            rows = pl.ds(8 * tiles + 8, 4) if lattice_dirs[q][2] > 0 else pl.ds(4, 4)
            target[pl.ds(start + 4 * j, 4)] = moved[q, rows]
        target[pl.ds(start + 20, 4)] = jnp.zeros((4, LANES), F32)

    is_upper = bit(lax.axis_index("wall"), level) == 1
    pl.when(jnp.logical_not(is_upper))(functools.partial(fill, z_plus))
    pl.when(is_upper)(functools.partial(fill, z_minus))


def collide_kernel(pops, flags, mid, moved, pair_faces, *, tiles):
    def scatter(at):
        solid = flags[pl.ds(at, 8)] != 0
        base, *rest = [mid[j, pl.ds(at, 8)] for j in range(10)]
        p0 = pops[0, pl.ds(at, 8)]
        moved[0, pl.ds(8 + at, 8)] = jnp.where(solid, p0, 12.0 * base - 0.25 * p0)
        for q in range(1, DIRS, 2):
            shared, odd = parts_of(q, base, rest[:3], rest[3:6], rest[6:])
            ahead, behind = pops[q, pl.ds(at, 8)], pops[q + 1, pl.ds(at, 8)]
            for d, relaxed, bounced in (
                (q, (shared + odd) - 0.25 * ahead, behind),
                (q + 1, (shared - odd) - 0.25 * behind, ahead),
            ):
                step_x, step_y, step_z = lattice_dirs[d]
                value = jnp.where(solid, bounced, relaxed)
                if step_y:
                    value = pltpu.roll(value, step_y % LANES, axis=1)
                if step_x:
                    value = pltpu.roll(value, step_x % 8, axis=0)
                moved[d, pl.ds(8 + at + 4 * step_z, 8)] = value

    for k in range(tiles):
        scatter(8 * k)
    for d in z_plus + z_minus:
        at = 8 if lattice_dirs[d][2] > 0 else 8 * tiles + 4
        moved[d, pl.ds(at, 4)] = jnp.zeros((4, LANES), F32)
    write_faces(pair_faces, 0, moved, 0, tiles)


def reciprocal(x):
    return 1.0 / x


def eliminate_kernel(
    pops, conc, flags, table, mid, offset, edge, link, ends, *, rows
):
    low = low_rows()
    half = rows // 2
    field_xyz = [table[pl.ds(8 * a, 8)] for a in range(3)]
    val_pair = [table[pl.ds(8 * (3 + 5 * h), 8)] for h in range(2)]
    for k in range(half):
        at = 8 * k
        sums = []
        for z in range(2):
            part = val_pair[0] * conc[pl.ds(4 * at + 16 * z, 8)]
            part = part + val_pair[1] * conc[pl.ds(4 * at + 16 * z + 8, 8)]
            sums.append(part + pltpu.roll(part, 4, axis=0))
        charge = jnp.where(low, sums[0], sums[1])
        base, vel, odd, even = moments(
            [pops[q, pl.ds(at, 8)] for q in range(DIRS)], charge, field_xyz
        )
        for j, value in enumerate((base, *vel, *odd, *even)):
            mid[j, pl.ds(at, 8)] = value
    for h in range(2):
        diff, slow, membrane, pull = [table[pl.ds(8 * (4 + 5 * h + j), 8)] for j in range(4)]

        def coefficients(z):
            tile = pl.ds(8 * (z // 2), 8)
            vz, flag = mid[3, tile], flags[tile]
            mine = low if z % 2 == 0 else jnp.logical_not(low)
            vz = jnp.where(mine, vz, pltpu.roll(vz, 4, axis=0))
            flag = jnp.where(mine, flag, pltpu.roll(flag, 4, axis=0))
            spread = jnp.where(flag == 0, diff, jnp.where(flag == 1, slow, membrane))
            drift = spread * jnp.tanh(2.0 * vz + pull)
            lower = 0.5 * spread + 0.25 * drift
            upper = 0.5 * spread - 0.25 * drift
            here = conc[pl.ds(16 * z + 8 * h, 8)]
            rhs = here - spread * here
            if z > 0:
                rhs = rhs + lower * conc[pl.ds(16 * (z - 1) + 8 * h, 8)]
            if z < rows - 1:
                rhs = rhs + upper * conc[pl.ds(16 * (z + 1) + 8 * h, 8)]
            return 1.0 + spread, lower, upper, rhs

        state = {}
        for z_up in range(half):
            for side in range(2):
                z = z_up if side == 0 else rows - 1 - z_up
                main, lower, upper, rhs = coefficients(z)
                back, ahead = (lower, upper) if side == 0 else (upper, lower)
                if z_up == 0:
                    r = reciprocal(main)
                    d, e, k = rhs * r, back * r, ahead * r
                    first = (d, e, k)
                else:
                    d, e, k, first = state[side]
                    r = reciprocal(main - back * k)
                    d, e, k = (rhs + back * d) * r, (back * e) * r, ahead * r
                    first = (first[0] + first[2] * d, first[1] + first[2] * e, first[2] * k)
                state[side] = (d, e, k, first)
                at = pl.ds(16 * z + 8 * h, 8)
                offset[at] = d
                edge[at] = e
                link[at] = k
        (d0, e0, k0, first), (d1, e1, k1, last) = state[0], state[1]
        r = reciprocal(1.0 - k0 * k1)
        high = ((d1 + k1 * d0) * r, (k1 * e0) * r, e1 * r)
        below = ((d0 + k0 * d1) * r, e0 * r, (k0 * e1) * r)
        values = (
            conc[pl.ds(8 * h, 8)] + first[0] + first[2] * high[0],
            first[1] + first[2] * high[1],
            first[2] * high[2],
            conc[pl.ds(16 * (rows - 1) + 8 * h, 8)] + last[0] + last[2] * below[0],
            last[2] * below[1],
            last[1] + last[2] * below[2],
        )
        for j, value in enumerate(values):
            ends[pl.ds(16 * j + 8 * h, 8)] = value


def bit(wall, r):
    return lax.rem(lax.div(wall, 2**r), 2)


def read_ends(ref, h, n=6):
    return [ref[pl.ds(16 * j + 8 * h, 8)] for j in range(n)]


def ordered(own, got, is_upper):
    return (
        [jnp.where(is_upper, g, o) for o, g in zip(own, got)],
        [jnp.where(is_upper, o, g) for o, g in zip(own, got)],
    )


def merge(a, b):
    r = reciprocal(1.0 - a[5] * b[1])
    top_a = ((a[3] + a[5] * b[0]) * r, a[4] * r, (a[5] * b[2]) * r)
    low_b = ((b[0] + b[1] * a[3]) * r, (b[1] * a[4]) * r, b[2] * r)
    merged = (
        a[0] + a[2] * low_b[0],
        a[1] + a[2] * low_b[1],
        a[2] * low_b[2],
        b[3] + b[4] * top_a[0],
        b[4] * top_a[1],
        b[5] + b[4] * top_a[2],
    )
    return top_a, low_b, merged


def relay_kernel(own, got, moved, send, *, level, last, tiles):
    wall = lax.axis_index("wall")
    is_upper = bit(wall, level) == 1
    next_upper = bit(wall, level + 1) == 1
    for h in range(2):
        a, b = ordered(read_ends(own, h), read_ends(got, h), is_upper)
        values = merge(a, b)[2]
        if last:
            values = [
                jnp.where(next_upper, values[0], values[3]),
                jnp.where(next_upper, values[1], values[5]),
            ]
        for j, value in enumerate(values):
            send[pl.ds(16 * j + 8 * h, 8)] = value
    write_faces(send, 16 * len(values), moved, level + 1, tiles)


def faces_kernel(even_got, odd_got, *targets, tiles):
    wall, lat = lax.axis_index("wall"), lax.axis_index("lat")
    lats = lax.axis_size("lat")
    odd_lat = lax.rem(lat, 2) == 1

    def from_lat(q, odd_z, index):
        dirs = x_plus if q in x_plus else x_minus
        at = pl.ds(2 * tiles * dirs.index(q) + 2 * index + (1 if odd_z else 0), 1)
        use_even = odd_lat if q in x_plus else jnp.logical_not(odd_lat)
        exists = lat > 0 if q in x_plus else lat < lats - 1
        row = jnp.where(use_even, even_got[at], odd_got[at])
        return jnp.where(exists, row, 0.0)

    def fill(target, dirs):
        target[...] = jnp.zeros(target.shape, F32)
        for j, q in enumerate([q for q in dirs if lattice_dirs[q][0]]):
            up = lattice_dirs[q][2] > 0
            target[pl.ds(j, 1)] = from_lat(q, up, tiles - 1 if up else 0)

    for r, target in enumerate(targets):
        pl.when(bit(wall, r) == 0)(functools.partial(fill, target, z_plus))
        pl.when(bit(wall, r) == 1)(functools.partial(fill, target, z_minus))


def solve_ions(owns, gots, offset, edge, link, solved, write, *, rows):
    levels = len(owns)
    wall = lax.axis_index("wall")
    half = rows // 2
    inner = []
    for h in range(2):
        top = levels - 1
        go, xo = read_ends(owns[top], h, 2)
        gr, xr = read_ends(gots[top], h, 2)
        w = (gr + xr * go) * reciprocal(1.0 - xo * xr)
        is_upper = bit(wall, top) == 1
        w_low, w_high = jnp.where(is_upper, w, 0.0), jnp.where(is_upper, 0.0, w)
        for r in range(top - 1, -1, -1):
            is_upper = bit(wall, r) == 1
            a, b = ordered(read_ends(owns[r], h), read_ends(gots[r], h), is_upper)
            top_a, low_b, _ = merge(a, b)
            new_low = top_a[0] + top_a[1] * w_low + top_a[2] * w_high
            new_high = low_b[0] + low_b[1] * w_low + low_b[2] * w_high
            w_low, w_high = (
                jnp.where(is_upper, new_low, w_low),
                jnp.where(is_upper, w_high, new_high),
            )
        at0, at1 = pl.ds(16 * (half - 1) + 8 * h, 8), pl.ds(16 * half + 8 * h, 8)
        a0 = offset[at0] + edge[at0] * w_low
        a1 = offset[at1] + edge[at1] * w_high
        k0, k1 = link[at0], link[at1]
        r = reciprocal(1.0 - k0 * k1)
        u0, u1 = (a0 + k0 * a1) * r, (a1 + k1 * a0) * r
        solved[at0] = u0
        solved[at1] = u1
        inner.append([u0, u1, w_low, w_high])
    for i in range(1, half):
        for h in range(2):
            u0, u1, w_low, w_high = inner[h]
            at0 = pl.ds(16 * (half - 1 - i) + 8 * h, 8)
            at1 = pl.ds(16 * (half + i) + 8 * h, 8)
            u0 = (offset[at0] + edge[at0] * w_low) + link[at0] * u0
            u1 = (offset[at1] + edge[at1] * w_high) + link[at1] * u1
            solved[at0] = u0
            solved[at1] = u1
            inner[h] = [u0, u1, w_low, w_high]
        if i == half // 2 - 1:
            write(0, half - half // 2, 2 * (half // 2))
    write(1, 0, half - half // 2)
    write(2, half + half // 2, half - half // 2)


def outputs_kernel(*refs, rows, tiles, levels):
    it = iter(refs)
    owns = [next(it) for _ in range(levels)]
    gots = [next(it) for _ in range(levels)]
    offset, edge, link, moved, even_got, odd_got, _ = [next(it) for _ in range(7)]
    pops_out, conc_out, tops, patched, solved, sems = [next(it) for _ in range(6)]
    lat, lats = lax.axis_index("lat"), lax.axis_size("lat")
    odd_lat = lax.rem(lat, 2) == 1
    body = pl.ds(8, 8 * tiles)

    def start(source, target, sem):
        pltpu.make_async_copy(source, target, sems.at[sem]).start()

    for q in range(DIRS):
        if lattice_dirs[q][0] == 0:
            start(moved.at[q, body], pops_out.at[q], 0)
    order = {q: j for j, q in enumerate(x_plus + x_minus)}

    def fill(dirs, got, keep):
        for j, q in enumerate(dirs):
            for k in range(tiles + 2):
                patched[order[q], pl.ds(8 * k, 8)] = moved[q, pl.ds(8 * k, 8)]
            even_z = got[pl.ds(2 * tiles * j, tiles, stride=2)]
            odd_z = got[pl.ds(2 * tiles * j + 1, tiles, stride=2)]
            patched[order[q], pl.ds(out_odd(q), tiles, stride=8)] = jnp.where(keep, even_z, 0.0)
            patched[order[q], pl.ds(out_even(q), tiles, stride=8)] = jnp.where(keep, odd_z, 0.0)

    @pl.when(odd_lat)
    def _():
        fill(x_plus, even_got, lat > 0)
        fill(x_minus, odd_got, lat < lats - 1)

    @pl.when(jnp.logical_not(odd_lat))
    def _():
        fill(x_plus, odd_got, lat > 0)
        fill(x_minus, even_got, lat < lats - 1)

    for q in x_plus + x_minus:
        start(patched.at[order[q], body], pops_out.at[q], 0)
    for j, q in enumerate(z_plus + z_minus):
        at = pl.ds(8, 8) if lattice_dirs[q][2] > 0 else pl.ds(8 * tiles, 8)
        tops[pl.ds(8 * j, 8)] = patched[order[q], at] if q in order else moved[q, at]

    def write(_, begin, count):
        span = pl.ds(16 * begin, 16 * count)
        start(solved.at[span], conc_out.at[span], 1)

    solve_ions(owns, gots, offset, edge, link, solved, write, rows=rows)
    pltpu.make_async_copy(pops_out, pops_out, sems.at[0]).wait()
    pltpu.make_async_copy(solved, solved, sems.at[1]).wait()


def patch_kernel(*refs, tiles, levels):
    gots, faces = refs[:levels], refs[levels : 2 * levels]
    tops, _, pops_out, fixed, sem = refs[2 * levels :]
    wall = lax.axis_index("wall")
    for j in range(len(z_plus) + len(z_minus)):
        fixed[pl.ds(8 * j, 8)] = tops[pl.ds(8 * j, 8)]

    def put(r, lower):
        base = 0 if r == 0 else 32 if r == levels - 1 else 96
        row_of_x = 0
        for j, q in enumerate(z_plus if lower else z_minus):
            row = 8 * j if lower else 8 * (5 + j) + 4
            fixed[pl.ds(row, 4)] = faces[r][pl.ds(base + 4 * j, 4)]
            step_x = lattice_dirs[q][0]
            if step_x:
                row += 0 if step_x > 0 else 3
                fixed[pl.ds(row, 1)] = gots[r][pl.ds(row_of_x, 1)]
                row_of_x += 1

    for r in range(levels):
        rest = lax.rem(wall, 2 ** (r + 1))
        pl.when(rest == 2**r)(functools.partial(put, r, True))
        pl.when(rest == 2**r - 1)(functools.partial(put, r, False))
    for j, q in enumerate(z_plus + z_minus):
        at = pl.ds(0, 8) if lattice_dirs[q][2] > 0 else pl.ds(8 * tiles - 8, 8)
        pltpu.make_async_copy(fixed.at[pl.ds(8 * j, 8)], pops_out.at[q, at], sem).start()
    pltpu.make_async_copy(fixed, fixed, sem).wait()


def swaps(lats, walls):
    def pairs(partner):
        table = []
        for lat in range(lats):
            for wall in range(walls):
                to_lat, to_wall = partner(lat, wall)
                table.append((lat * walls + wall, to_lat * walls + to_wall))
        return table

    def odd_partner(lat, wall):
        if lat == 0 or lat == lats - 1:
            return lat, wall ^ 1
        return ((lat + 1) ^ 1) - 1, wall

    even = pairs(lambda lat, wall: (lat ^ 1, wall))
    odd = pairs(odd_partner)
    levels = []
    while 2 ** len(levels) < walls:
        flip = 2 ** (len(levels) + 1) - 1
        levels.append(pairs(lambda lat, wall: (lat, wall ^ flip)))
    return even, odd, levels


def per_device(
    populations, concentration, cell_flags, valence, diffusivity, applied_field, *, lats, walls
):
    rows, cells = populations.shape[1], populations.shape[1] * populations.shape[2]
    tiles = cells // 8
    chunks = [1] * (rows // 8)
    assert populations.shape[2] == X_CELLS and lats % 2 == 0 and walls >= 4
    even, odd, levels = swaps(lats, walls)
    assert 2 ** len(levels) == walls

    def move(x, table):
        return lax.ppermute(x, ("lat", "wall"), table)

    msg_rows = 2 * tiles * 5
    even_msg, odd_msg, pops, conc, flags, table = pl.pallas_call(
        functools.partial(edges_kernel, chunks=chunks),
        out_shape=(
            on_chip(msg_rows, LANES),
            on_chip(msg_rows, LANES),
            on_chip(DIRS + SPECIES, cells, LANES),
            on_chip(cells * SPECIES, LANES),
            on_chip(cells, LANES, dtype=jnp.int32),
            on_chip(104, LANES),
        ),
        in_specs=[ANY_SPEC] * 6,
        out_specs=(VMEM_SPEC,) * 6,
        scratch_shapes=[
            pltpu.SMEM((SPECIES,), jnp.int32),
            pltpu.SMEM((SPECIES,), F32),
            pltpu.SMEM((3,), F32),
            pltpu.SemaphoreType.DMA((4 + len(chunks),)),
        ],
        compiler_params=params(),
        cost_estimate=cost(2_000_000, 3_000_000),
        name="edges",
    )(
        *in_hbm(
            populations.reshape(DIRS, cells, LANES),
            concentration.reshape(cells * SPECIES, LANES),
            cell_flags.reshape(cells, LANES),
            valence,
            diffusivity,
            applied_field,
        )
    )
    odd_got = move(odd_msg, odd)
    even_got = move(even_msg, even)

    mid, offset, edge, link, ends = pl.pallas_call(
        functools.partial(eliminate_kernel, rows=rows),
        out_shape=(on_chip(10, cells, LANES),)
        + (on_chip(cells * SPECIES, LANES),) * 3
        + (on_chip(96, LANES),),
        in_specs=[VMEM_SPEC] * 4,
        out_specs=(VMEM_SPEC,) * 5,
        compiler_params=params(),
        cost_estimate=cost(5_000_000, 3_000_000),
        name="eliminate",
    )(*pin(pops, conc, flags, table))

    moved, pair_faces = pl.pallas_call(
        functools.partial(collide_kernel, tiles=tiles),
        out_shape=(on_chip(DIRS, cells + 16, LANES), on_chip(FACE_ROWS, LANES)),
        in_specs=[VMEM_SPEC] * 3,
        out_specs=(VMEM_SPEC,) * 2,
        compiler_params=params(),
        cost_estimate=cost(5_000_000, 3_000_000),
        name="collide",
    )(*pin(pops, flags, mid))

    depth = len(levels)
    pair_got = move(pair_faces, levels[0])
    owns, gots = [ends], [move(ends, levels[0])]
    for level in range(depth - 1):
        last = level == depth - 2
        sent = pl.pallas_call(
            functools.partial(relay_kernel, level=level, last=last, tiles=tiles),
            out_shape=on_chip((32 if last else 96) + FACE_ROWS, LANES),
            in_specs=[VMEM_SPEC] * 3,
            out_specs=VMEM_SPEC,
            compiler_params=params(),
            cost_estimate=cost(100_000, 200_000),
            name=f"relay{level}",
        )(*pin(owns[-1], gots[-1], moved))
        owns.append(sent)
        gots.append(move(sent, levels[level + 1]))

    faces = pl.pallas_call(
        functools.partial(faces_kernel, tiles=tiles),
        out_shape=(on_chip(8, LANES),) + (on_chip(16, LANES),) * (depth - 1),
        in_specs=[VMEM_SPEC] * 2,
        out_specs=(VMEM_SPEC,) * depth,
        compiler_params=params(),
        cost_estimate=cost(100_000, 200_000),
        name="faces",
    )(*pin(even_got, odd_got))
    face_gots = [move(face, table) for face, table in zip(faces, levels)]

    operands = pin(*owns, *gots, offset, edge, link, moved, even_got, odd_got, faces[-1])
    pops_out, new_conc, tops = pl.pallas_call(
        functools.partial(outputs_kernel, rows=rows, tiles=tiles, levels=depth),
        out_shape=(
            jax.ShapeDtypeStruct((DIRS, cells, LANES), F32),
            jax.ShapeDtypeStruct((cells * SPECIES, LANES), F32),
            on_chip(80, LANES),
        ),
        in_specs=[VMEM_SPEC] * len(operands),
        out_specs=(ANY_SPEC, ANY_SPEC, VMEM_SPEC),
        scratch_shapes=[
            pltpu.VMEM((10, cells + 16, LANES), F32),
            pltpu.VMEM((cells * SPECIES, LANES), F32),
            pltpu.SemaphoreType.DMA((2,)),
        ],
        compiler_params=params(),
        cost_estimate=cost(1_000_000, 2_500_000),
        name="outputs",
    )(*operands)

    new_pops = pl.pallas_call(
        functools.partial(patch_kernel, tiles=tiles, levels=depth),
        out_shape=jax.ShapeDtypeStruct((DIRS, cells, LANES), F32),
        in_specs=[VMEM_SPEC] * (2 * depth + 1) + [ANY_SPEC],
        out_specs=ANY_SPEC,
        input_output_aliases={2 * depth + 1: 0},
        scratch_shapes=[
            pltpu.VMEM((80, LANES), F32),
            pltpu.SemaphoreType.DMA,
        ],
        compiler_params=params(),
        cost_estimate=cost(10_000, 100_000),
        name="patch",
    )(*pin(*face_gots, pair_got, *gots[1:], tops), pops_out)
    return new_pops.reshape(populations.shape), new_conc.reshape(concentration.shape)


def solution(mesh):
    in_specs = (
        P(None, "wall", "lat", None),
        P("wall", None, "lat", None),
        P("wall", "lat", None),
        P(),
        P(),
        P(),
    )
    out_specs = (P(None, "wall", "lat", None), P("wall", None, "lat", None))
    return jax.shard_map(
        functools.partial(per_device, lats=mesh.shape["lat"], walls=mesh.shape["wall"]),
        mesh=mesh,
        in_specs=in_specs,
        out_specs=out_specs,
        check_vma=False,
    )
```

```python
import functools

import jax
import jax.numpy as jnp
from jax import lax
from jax.experimental import pallas as pl
from jax.experimental.pallas import tpu as pltpu
from jax.sharding import PartitionSpec as P

lattice_dirs = (
    (0, 0, 0),
    (1, 0, 0),
    (-1, 0, 0),
    (0, 1, 0),
    (0, -1, 0),
    (0, 0, 1),
    (0, 0, -1),
    (1, 1, 0),
    (-1, -1, 0),
    (1, -1, 0),
    (-1, 1, 0),
    (1, 0, 1),
    (-1, 0, -1),
    (1, 0, -1),
    (-1, 0, 1),
    (0, 1, 1),
    (0, -1, -1),
    (0, 1, -1),
    (0, -1, 1),
)
DIRS = len(lattice_dirs)
FORCE_GAIN = 0.02
X_CELLS = 4
SPECIES = 4
LANES = 128
F32 = jnp.float32

x_plus = tuple(q for q in range(DIRS) if lattice_dirs[q][0] == 1)
x_minus = tuple(q for q in range(DIRS) if lattice_dirs[q][0] == -1)
z_plus = tuple(q for q in range(DIRS) if lattice_dirs[q][2] == 1)
z_minus = tuple(q for q in range(DIRS) if lattice_dirs[q][2] == -1)
FACE_ROWS = 24

VMEM_SPEC = pl.BlockSpec(memory_space=pltpu.VMEM)
ANY_SPEC = pl.BlockSpec(memory_space=pl.ANY)


def on_chip(*shape, dtype=F32):
    return pltpu.VMEM(shape, dtype)


def params():
    return pltpu.CompilerParams(vmem_limit_bytes=24 * 1024 * 1024)


def cost(flops, nbytes):
    return pl.CostEstimate(flops=flops, bytes_accessed=nbytes, transcendentals=0)


def in_hbm(*arrays):
    return [pltpu.with_memory_space_constraint(a, pltpu.HBM) for a in arrays]


def pin(*arrays):
    return [pltpu.with_memory_space_constraint(a, pltpu.VMEM) for a in arrays]


def out_even(q):
    step_x, _, step_z = lattice_dirs[q]
    return {0: 12, 1: 16, -1: 8}[step_z] + (0 if step_x > 0 else 3)


def out_odd(q):
    step_x, _, step_z = lattice_dirs[q]
    return {0: 8, 1: 12, -1: 4}[step_z] + (0 if step_x > 0 else 3)


def low_rows():
    return lax.broadcasted_iota(jnp.int32, (8, LANES), 0) < 4


def density_and_momentum(p):
    diff = {q: p[q] - p[q + 1] for q in range(1, DIRS, 2)}
    total = {q: p[q] + p[q + 1] for q in range(1, DIRS, 2)}
    density = (
        ((p[0] + total[1]) + (total[3] + total[5]))
        + ((total[7] + total[9]) + (total[11] + total[13]))
        + (total[15] + total[17])
    )
    momentum = [
        (diff[1] + diff[7]) + (diff[9] + diff[11]) + diff[13],
        (diff[3] + diff[7]) - (diff[9] - diff[15]) + diff[17],
        (diff[5] + diff[11]) - (diff[13] - diff[15]) - diff[17],
    ]
    return density, momentum


def moments(p, charge, field_xyz):
    density, momentum = density_and_momentum(p)
    force = [charge * f for f in field_xyz]
    inverse = 1.0 / density
    vel = [(momentum[a] + 0.5 * force[a]) * inverse for a in range(3)]
    speed_sq = vel[0] * vel[0] + vel[1] * vel[1] + vel[2] * vel[2]
    work = vel[0] * force[0] + vel[1] * force[1] + vel[2] * force[2]
    base = (1.25 / 36.0 * density) * (1.0 - 1.5 * speed_sq) - (1.125 / 36.0) * work
    odd = [(3.75 / 36.0) * momentum[a] + (3.0 / 36.0) * force[a] for a in range(3)]
    even = [(5.625 / 36.0) * momentum[a] + (6.1875 / 36.0) * force[a] for a in range(3)]
    return base, vel, odd, even


def parts_of(q, base, vel, odd, even):
    axes = [(a, lattice_dirs[q][a]) for a in range(3) if lattice_dirs[q][a]]

    def along(v):
        out = v[axes[0][0]]
        for a, sign in axes[1:]:
            out = out + v[a] if sign > 0 else out - v[a]
        return out

    cu, odd_q, even_q = along(vel), along(odd), along(even)
    if len(axes) == 1:
        return (base + base) + 2.0 * (cu * even_q), odd_q + odd_q
    return base + cu * even_q, odd_q


def edges_kernel(
    pops_hbm,
    conc_hbm,
    flags_hbm,
    valence_hbm,
    diffusivity_hbm,
    field_hbm,
    even_msg,
    odd_msg,
    pops,
    conc,
    flags,
    table,
    valence,
    diffusivity,
    field,
    sems,
    *,
    chunks,
):
    small = [
        pltpu.make_async_copy(source, target, sems.at[i])
        for i, (source, target) in enumerate(
            (
                (flags_hbm, flags),
                (valence_hbm, valence),
                (field_hbm, field),
                (diffusivity_hbm, diffusivity),
            )
        )
    ]
    arrived = {}
    at = 0
    for c, count in enumerate(chunks):
        rows = pl.ds(32 * at, 32 * count)
        crows = pl.ds(128 * at, 128 * count)
        sem = sems.at[4 + c]
        pltpu.make_async_copy(conc_hbm.at[crows], conc.at[crows], sem).start()
        pltpu.make_async_copy(pops_hbm.at[:, rows], pops.at[pl.ds(0, DIRS), rows], sem).start()
        both = pops.at[:, rows]
        arrived[at] = pltpu.make_async_copy(both, both, sem)
        at += count
        if c == 0:
            for copy in small:
                copy.start()
    low = low_rows()
    for copy in small:
        copy.wait()
    val = [valence[s].astype(F32) for s in range(SPECIES)]
    field_xyz = [FORCE_GAIN * field[axis] for axis in range(3)]
    values = [jnp.full((8, LANES), f, F32) for f in field_xyz]
    for h in range(2):
        diff = jnp.where(low, diffusivity[2 * h], diffusivity[2 * h + 1])
        val_pair = jnp.where(low, val[2 * h], val[2 * h + 1])
        values += [
            val_pair,
            diff,
            diff * 0.01,
            diff * jnp.where(val_pair > 0, 0.5, 0.02),
            val_pair * field[2],
        ]
    for j, value in enumerate(values):
        table[pl.ds(8 * j, 8)] = value
    is_odd = lax.rem(lax.axis_index("lat"), 2) == 1
    for g in range(sum(chunks)):
        if g in arrived:
            arrived[g].wait()
        sent = {}
        for x, dirs in ((X_CELLS - 1, x_plus), (0, x_minus)):
            at = pl.ds(32 * g + x, 8, stride=4)
            p = [pops[q, at] for q in range(DIRS)]
            solid = flags[at] != 0
            terms = [
                val[s] * conc[pl.ds(128 * g + 4 * s + x, 8, stride=16)] for s in range(SPECIES)
            ]
            charge = (terms[0] + terms[1]) + (terms[2] + terms[3])
            found = moments(p, charge, field_xyz)
            for j, q in enumerate(dirs):
                first = q if q % 2 else q - 1
                shared, odd = parts_of(first, *found)
                relaxed = (shared + odd if q % 2 else shared - odd) - 0.25 * p[q]
                value = jnp.where(solid, p[q + 1 if q % 2 else q - 1], relaxed)
                step_y = lattice_dirs[q][1]
                if step_y:
                    value = pltpu.roll(value, step_y % LANES, axis=1)
                sent[x, j] = value
        for j in range(5):
            plus, minus = sent[X_CELLS - 1, j], sent[0, j]
            at = pl.ds(8 * sum(chunks) * j + 8 * g, 8)
            even_msg[at] = jnp.where(is_odd, minus, plus)
            odd_msg[at] = jnp.where(is_odd, plus, minus)


def write_faces(target, start, moved, level, tiles):
    def fill(dirs):
        for j, q in enumerate(dirs):
            rows = pl.ds(8 * tiles + 8, 4) if lattice_dirs[q][2] > 0 else pl.ds(4, 4)
            target[pl.ds(start + 4 * j, 4)] = moved[q, rows]
        target[pl.ds(start + 20, 4)] = jnp.zeros((4, LANES), F32)

    is_upper = bit(lax.axis_index("wall"), level) == 1
    pl.when(jnp.logical_not(is_upper))(functools.partial(fill, z_plus))
    pl.when(is_upper)(functools.partial(fill, z_minus))


def collide_kernel(pops, flags, mid, moved, pair_faces, *, tiles):
    def scatter(at):
        solid = flags[pl.ds(at, 8)] != 0
        base, *rest = [mid[j, pl.ds(at, 8)] for j in range(10)]
        p0 = pops[0, pl.ds(at, 8)]
        moved[0, pl.ds(8 + at, 8)] = jnp.where(solid, p0, 12.0 * base - 0.25 * p0)
        for q in range(1, DIRS, 2):
            shared, odd = parts_of(q, base, rest[:3], rest[3:6], rest[6:])
            ahead, behind = pops[q, pl.ds(at, 8)], pops[q + 1, pl.ds(at, 8)]
            for d, relaxed, bounced in (
                (q, (shared + odd) - 0.25 * ahead, behind),
                (q + 1, (shared - odd) - 0.25 * behind, ahead),
            ):
                step_x, step_y, step_z = lattice_dirs[d]
                value = jnp.where(solid, bounced, relaxed)
                if step_y:
                    value = pltpu.roll(value, step_y % LANES, axis=1)
                if step_x:
                    value = pltpu.roll(value, step_x % 8, axis=0)
                moved[d, pl.ds(8 + at + 4 * step_z, 8)] = value

    for k in range(tiles):
        scatter(8 * k)
    for d in z_plus + z_minus:
        at = 8 if lattice_dirs[d][2] > 0 else 8 * tiles + 4
        moved[d, pl.ds(at, 4)] = jnp.zeros((4, LANES), F32)
    write_faces(pair_faces, 0, moved, 0, tiles)


def reciprocal(x):
    return 1.0 / x


def eliminate_kernel(
    pops, conc, flags, table, mid, offset, edge, link, ends, *, rows
):
    low = low_rows()
    half = rows // 2
    field_xyz = [table[pl.ds(8 * a, 8)] for a in range(3)]
    val_pair = [table[pl.ds(8 * (3 + 5 * h), 8)] for h in range(2)]
    for k in range(half):
        at = 8 * k
        sums = []
        for z in range(2):
            part = val_pair[0] * conc[pl.ds(4 * at + 16 * z, 8)]
            part = part + val_pair[1] * conc[pl.ds(4 * at + 16 * z + 8, 8)]
            sums.append(part + pltpu.roll(part, 4, axis=0))
        charge = jnp.where(low, sums[0], sums[1])
        base, vel, odd, even = moments(
            [pops[q, pl.ds(at, 8)] for q in range(DIRS)], charge, field_xyz
        )
        for j, value in enumerate((base, *vel, *odd, *even)):
            mid[j, pl.ds(at, 8)] = value
    for h in range(2):
        diff, slow, membrane, pull = [table[pl.ds(8 * (4 + 5 * h + j), 8)] for j in range(4)]

        def coefficients(z):
            tile = pl.ds(8 * (z // 2), 8)
            vz, flag = mid[3, tile], flags[tile]
            mine = low if z % 2 == 0 else jnp.logical_not(low)
            vz = jnp.where(mine, vz, pltpu.roll(vz, 4, axis=0))
            flag = jnp.where(mine, flag, pltpu.roll(flag, 4, axis=0))
            spread = jnp.where(flag == 0, diff, jnp.where(flag == 1, slow, membrane))
            drift = spread * jnp.tanh(2.0 * vz + pull)
            lower = 0.5 * spread + 0.25 * drift
            upper = 0.5 * spread - 0.25 * drift
            here = conc[pl.ds(16 * z + 8 * h, 8)]
            rhs = here - spread * here
            if z > 0:
                rhs = rhs + lower * conc[pl.ds(16 * (z - 1) + 8 * h, 8)]
            if z < rows - 1:
                rhs = rhs + upper * conc[pl.ds(16 * (z + 1) + 8 * h, 8)]
            return 1.0 + spread, lower, upper, rhs

        state = {}
        for z_up in range(half):
            for side in range(2):
                z = z_up if side == 0 else rows - 1 - z_up
                main, lower, upper, rhs = coefficients(z)
                back, ahead = (lower, upper) if side == 0 else (upper, lower)
                if z_up == 0:
                    r = reciprocal(main)
                    d, e, k = rhs * r, back * r, ahead * r
                    first = (d, e, k)
                else:
                    d, e, k, first = state[side]
                    r = reciprocal(main - back * k)
                    d, e, k = (rhs + back * d) * r, (back * e) * r, ahead * r
                    first = (first[0] + first[2] * d, first[1] + first[2] * e, first[2] * k)
                state[side] = (d, e, k, first)
                at = pl.ds(16 * z + 8 * h, 8)
                offset[at] = d
                edge[at] = e
                link[at] = k
        (d0, e0, k0, first), (d1, e1, k1, last) = state[0], state[1]
        r = reciprocal(1.0 - k0 * k1)
        high = ((d1 + k1 * d0) * r, (k1 * e0) * r, e1 * r)
        below = ((d0 + k0 * d1) * r, e0 * r, (k0 * e1) * r)
        values = (
            conc[pl.ds(8 * h, 8)] + first[0] + first[2] * high[0],
            first[1] + first[2] * high[1],
            first[2] * high[2],
            conc[pl.ds(16 * (rows - 1) + 8 * h, 8)] + last[0] + last[2] * below[0],
            last[2] * below[1],
            last[1] + last[2] * below[2],
        )
        for j, value in enumerate(values):
            ends[pl.ds(16 * j + 8 * h, 8)] = value


def bit(wall, r):
    return lax.rem(lax.div(wall, 2**r), 2)


def read_ends(ref, h, n=6):
    return [ref[pl.ds(16 * j + 8 * h, 8)] for j in range(n)]


def ordered(own, got, is_upper):
    return (
        [jnp.where(is_upper, g, o) for o, g in zip(own, got)],
        [jnp.where(is_upper, o, g) for o, g in zip(own, got)],
    )


def merge(a, b):
    r = reciprocal(1.0 - a[5] * b[1])
    top_a = ((a[3] + a[5] * b[0]) * r, a[4] * r, (a[5] * b[2]) * r)
    low_b = ((b[0] + b[1] * a[3]) * r, (b[1] * a[4]) * r, b[2] * r)
    merged = (
        a[0] + a[2] * low_b[0],
        a[1] + a[2] * low_b[1],
        a[2] * low_b[2],
        b[3] + b[4] * top_a[0],
        b[4] * top_a[1],
        b[5] + b[4] * top_a[2],
    )
    return top_a, low_b, merged


def relay_kernel(own, got, moved, send, *, level, last, tiles):
    wall = lax.axis_index("wall")
    is_upper = bit(wall, level) == 1
    next_upper = bit(wall, level + 1) == 1
    for h in range(2):
        a, b = ordered(read_ends(own, h), read_ends(got, h), is_upper)
        values = merge(a, b)[2]
        if last:
            values = [
                jnp.where(next_upper, values[0], values[3]),
                jnp.where(next_upper, values[1], values[5]),
            ]
        for j, value in enumerate(values):
            send[pl.ds(16 * j + 8 * h, 8)] = value
    write_faces(send, 16 * len(values), moved, level + 1, tiles)


def faces_kernel(even_got, odd_got, *targets, tiles):
    wall, lat = lax.axis_index("wall"), lax.axis_index("lat")
    lats = lax.axis_size("lat")
    odd_lat = lax.rem(lat, 2) == 1

    def from_lat(q, odd_z, index):
        dirs = x_plus if q in x_plus else x_minus
        at = pl.ds(2 * tiles * dirs.index(q) + 2 * index + (1 if odd_z else 0), 1)
        use_even = odd_lat if q in x_plus else jnp.logical_not(odd_lat)
        exists = lat > 0 if q in x_plus else lat < lats - 1
        row = jnp.where(use_even, even_got[at], odd_got[at])
        return jnp.where(exists, row, 0.0)

    def fill(target, dirs):
        target[...] = jnp.zeros(target.shape, F32)
        for j, q in enumerate([q for q in dirs if lattice_dirs[q][0]]):
            up = lattice_dirs[q][2] > 0
            target[pl.ds(j, 1)] = from_lat(q, up, tiles - 1 if up else 0)

    for r, target in enumerate(targets):
        pl.when(bit(wall, r) == 0)(functools.partial(fill, target, z_plus))
        pl.when(bit(wall, r) == 1)(functools.partial(fill, target, z_minus))


def solve_ions(owns, gots, offset, edge, link, solved, write, *, rows):
    levels = len(owns)
    wall = lax.axis_index("wall")
    half = rows // 2
    inner = []
    for h in range(2):
        top = levels - 1
        go, xo = read_ends(owns[top], h, 2)
        gr, xr = read_ends(gots[top], h, 2)
        w = (gr + xr * go) * reciprocal(1.0 - xo * xr)
        is_upper = bit(wall, top) == 1
        w_low, w_high = jnp.where(is_upper, w, 0.0), jnp.where(is_upper, 0.0, w)
        for r in range(top - 1, -1, -1):
            is_upper = bit(wall, r) == 1
            a, b = ordered(read_ends(owns[r], h), read_ends(gots[r], h), is_upper)
            top_a, low_b, _ = merge(a, b)
            new_low = top_a[0] + top_a[1] * w_low + top_a[2] * w_high
            new_high = low_b[0] + low_b[1] * w_low + low_b[2] * w_high
            w_low, w_high = (
                jnp.where(is_upper, new_low, w_low),
                jnp.where(is_upper, w_high, new_high),
            )
        at0, at1 = pl.ds(16 * (half - 1) + 8 * h, 8), pl.ds(16 * half + 8 * h, 8)
        a0 = offset[at0] + edge[at0] * w_low
        a1 = offset[at1] + edge[at1] * w_high
        k0, k1 = link[at0], link[at1]
        r = reciprocal(1.0 - k0 * k1)
        u0, u1 = (a0 + k0 * a1) * r, (a1 + k1 * a0) * r
        solved[at0] = u0
        solved[at1] = u1
        inner.append([u0, u1, w_low, w_high])
    for i in range(1, half):
        for h in range(2):
            u0, u1, w_low, w_high = inner[h]
            at0 = pl.ds(16 * (half - 1 - i) + 8 * h, 8)
            at1 = pl.ds(16 * (half + i) + 8 * h, 8)
            u0 = (offset[at0] + edge[at0] * w_low) + link[at0] * u0
            u1 = (offset[at1] + edge[at1] * w_high) + link[at1] * u1
            solved[at0] = u0
            solved[at1] = u1
            inner[h] = [u0, u1, w_low, w_high]
        if i == half // 2 - 1:
            write(0, half - half // 2, 2 * (half // 2))
    write(1, 0, half - half // 2)
    write(2, half + half // 2, half - half // 2)


def outputs_kernel(*refs, rows, tiles, levels):
    it = iter(refs)
    owns = [next(it) for _ in range(levels)]
    gots = [next(it) for _ in range(levels)]
    offset, edge, link, moved, even_got, odd_got, _ = [next(it) for _ in range(7)]
    pops_out, conc_out, tops, patched, solved, sems = [next(it) for _ in range(6)]
    lat, lats = lax.axis_index("lat"), lax.axis_size("lat")
    odd_lat = lax.rem(lat, 2) == 1
    body = pl.ds(8, 8 * tiles)

    def start(source, target, sem):
        pltpu.make_async_copy(source, target, sems.at[sem]).start()

    for q in range(DIRS):
        if lattice_dirs[q][0] == 0:
            start(moved.at[q, body], pops_out.at[q], 0)
    order = {q: j for j, q in enumerate(x_plus + x_minus)}

    def fill(dirs, got, keep):
        for j, q in enumerate(dirs):
            for k in range(tiles + 2):
                patched[order[q], pl.ds(8 * k, 8)] = moved[q, pl.ds(8 * k, 8)]
            even_z = got[pl.ds(2 * tiles * j, tiles, stride=2)]
            odd_z = got[pl.ds(2 * tiles * j + 1, tiles, stride=2)]
            patched[order[q], pl.ds(out_odd(q), tiles, stride=8)] = jnp.where(keep, even_z, 0.0)
            patched[order[q], pl.ds(out_even(q), tiles, stride=8)] = jnp.where(keep, odd_z, 0.0)

    @pl.when(odd_lat)
    def _():
        fill(x_plus, even_got, lat > 0)
        fill(x_minus, odd_got, lat < lats - 1)

    @pl.when(jnp.logical_not(odd_lat))
    def _():
        fill(x_plus, odd_got, lat > 0)
        fill(x_minus, even_got, lat < lats - 1)

    for q in x_plus + x_minus:
        start(patched.at[order[q], body], pops_out.at[q], 0)
    for j, q in enumerate(z_plus + z_minus):
        at = pl.ds(8, 8) if lattice_dirs[q][2] > 0 else pl.ds(8 * tiles, 8)
        tops[pl.ds(8 * j, 8)] = patched[order[q], at] if q in order else moved[q, at]

    def write(_, begin, count):
        span = pl.ds(16 * begin, 16 * count)
        start(solved.at[span], conc_out.at[span], 1)

    solve_ions(owns, gots, offset, edge, link, solved, write, rows=rows)
    pltpu.make_async_copy(pops_out, pops_out, sems.at[0]).wait()
    pltpu.make_async_copy(solved, solved, sems.at[1]).wait()


def patch_kernel(*refs, tiles, levels):
    gots, faces = refs[:levels], refs[levels : 2 * levels]
    tops, _, pops_out, fixed, sem = refs[2 * levels :]
    wall = lax.axis_index("wall")
    for j in range(len(z_plus) + len(z_minus)):
        fixed[pl.ds(8 * j, 8)] = tops[pl.ds(8 * j, 8)]

    def put(r, lower):
        base = 0 if r == 0 else 32 if r == levels - 1 else 96
        row_of_x = 0
        for j, q in enumerate(z_plus if lower else z_minus):
            row = 8 * j if lower else 8 * (5 + j) + 4
            fixed[pl.ds(row, 4)] = faces[r][pl.ds(base + 4 * j, 4)]
            step_x = lattice_dirs[q][0]
            if step_x:
                row += 0 if step_x > 0 else 3
                fixed[pl.ds(row, 1)] = gots[r][pl.ds(row_of_x, 1)]
                row_of_x += 1

    for r in range(levels):
        rest = lax.rem(wall, 2 ** (r + 1))
        pl.when(rest == 2**r)(functools.partial(put, r, True))
        pl.when(rest == 2**r - 1)(functools.partial(put, r, False))
    for j, q in enumerate(z_plus + z_minus):
        at = pl.ds(0, 8) if lattice_dirs[q][2] > 0 else pl.ds(8 * tiles - 8, 8)
        pltpu.make_async_copy(fixed.at[pl.ds(8 * j, 8)], pops_out.at[q, at], sem).start()
    pltpu.make_async_copy(fixed, fixed, sem).wait()


def swaps(lats, walls):
    def pairs(partner):
        table = []
        for lat in range(lats):
            for wall in range(walls):
                to_lat, to_wall = partner(lat, wall)
                table.append((lat * walls + wall, to_lat * walls + to_wall))
        return table

    def odd_partner(lat, wall):
        if lat == 0 or lat == lats - 1:
            return lat, wall ^ 1
        return ((lat + 1) ^ 1) - 1, wall

    even = pairs(lambda lat, wall: (lat ^ 1, wall))
    odd = pairs(odd_partner)
    levels = []
    while 2 ** len(levels) < walls:
        flip = 2 ** (len(levels) + 1) - 1
        levels.append(pairs(lambda lat, wall: (lat, wall ^ flip)))
    return even, odd, levels


def per_device(
    populations, concentration, cell_flags, valence, diffusivity, applied_field, *, lats, walls
):
    rows, cells = populations.shape[1], populations.shape[1] * populations.shape[2]
    tiles = cells // 8
    chunks = [1] * (rows // 8)
    assert populations.shape[2] == X_CELLS and lats % 2 == 0 and walls >= 4
    even, odd, levels = swaps(lats, walls)
    assert 2 ** len(levels) == walls

    def move(x, table):
        return lax.ppermute(x, ("lat", "wall"), table)

    msg_rows = 2 * tiles * 5
    even_msg, odd_msg, pops, conc, flags, table = pl.pallas_call(
        functools.partial(edges_kernel, chunks=chunks),
        out_shape=(
            on_chip(msg_rows, LANES),
            on_chip(msg_rows, LANES),
            on_chip(DIRS + SPECIES, cells, LANES),
            on_chip(cells * SPECIES, LANES),
            on_chip(cells, LANES, dtype=jnp.int32),
            on_chip(104, LANES),
        ),
        in_specs=[ANY_SPEC] * 6,
        out_specs=(VMEM_SPEC,) * 6,
        scratch_shapes=[
            pltpu.SMEM((SPECIES,), jnp.int32),
            pltpu.SMEM((SPECIES,), F32),
            pltpu.SMEM((3,), F32),
            pltpu.SemaphoreType.DMA((4 + len(chunks),)),
        ],
        compiler_params=params(),
        cost_estimate=cost(2_000_000, 3_000_000),
        name="edges",
    )(
        *in_hbm(
            populations.reshape(DIRS, cells, LANES),
            concentration.reshape(cells * SPECIES, LANES),
            cell_flags.reshape(cells, LANES),
            valence,
            diffusivity,
            applied_field,
        )
    )
    odd_got = move(odd_msg, odd)
    even_got = move(even_msg, even)

    mid, offset, edge, link, ends = pl.pallas_call(
        functools.partial(eliminate_kernel, rows=rows),
        out_shape=(on_chip(10, cells, LANES),)
        + (on_chip(cells * SPECIES, LANES),) * 3
        + (on_chip(96, LANES),),
        in_specs=[VMEM_SPEC] * 4,
        out_specs=(VMEM_SPEC,) * 5,
        compiler_params=params(),
        cost_estimate=cost(5_000_000, 3_000_000),
        name="eliminate",
    )(*pin(pops, conc, flags, table))

    moved, pair_faces = pl.pallas_call(
        functools.partial(collide_kernel, tiles=tiles),
        out_shape=(on_chip(DIRS, cells + 16, LANES), on_chip(FACE_ROWS, LANES)),
        in_specs=[VMEM_SPEC] * 3,
        out_specs=(VMEM_SPEC,) * 2,
        compiler_params=params(),
        cost_estimate=cost(5_000_000, 3_000_000),
        name="collide",
    )(*pin(pops, flags, mid))

    depth = len(levels)
    pair_got = move(pair_faces, levels[0])
    owns, gots = [ends], [move(ends, levels[0])]
    for level in range(depth - 1):
        last = level == depth - 2
        sent = pl.pallas_call(
            functools.partial(relay_kernel, level=level, last=last, tiles=tiles),
            out_shape=on_chip((32 if last else 96) + FACE_ROWS, LANES),
            in_specs=[VMEM_SPEC] * 3,
            out_specs=VMEM_SPEC,
            compiler_params=params(),
            cost_estimate=cost(100_000, 200_000),
            name=f"relay{level}",
        )(*pin(owns[-1], gots[-1], moved))
        owns.append(sent)
        gots.append(move(sent, levels[level + 1]))

    faces = pl.pallas_call(
        functools.partial(faces_kernel, tiles=tiles),
        out_shape=(on_chip(8, LANES),) + (on_chip(8, LANES),) * (depth - 1),
        in_specs=[VMEM_SPEC] * 2,
        out_specs=(VMEM_SPEC,) * depth,
        compiler_params=params(),
        cost_estimate=cost(100_000, 200_000),
        name="faces",
    )(*pin(even_got, odd_got))
    face_gots = [move(face, table) for face, table in zip(faces, levels)]

    operands = pin(*owns, *gots, offset, edge, link, moved, even_got, odd_got, faces[-1])
    pops_out, new_conc, tops = pl.pallas_call(
        functools.partial(outputs_kernel, rows=rows, tiles=tiles, levels=depth),
        out_shape=(
            jax.ShapeDtypeStruct((DIRS, cells, LANES), F32),
            jax.ShapeDtypeStruct((cells * SPECIES, LANES), F32),
            on_chip(80, LANES),
        ),
        in_specs=[VMEM_SPEC] * len(operands),
        out_specs=(ANY_SPEC, ANY_SPEC, VMEM_SPEC),
        scratch_shapes=[
            pltpu.VMEM((10, cells + 16, LANES), F32),
            pltpu.VMEM((cells * SPECIES, LANES), F32),
            pltpu.SemaphoreType.DMA((2,)),
        ],
        compiler_params=params(),
        cost_estimate=cost(1_000_000, 2_500_000),
        name="outputs",
    )(*operands)

    new_pops = pl.pallas_call(
        functools.partial(patch_kernel, tiles=tiles, levels=depth),
        out_shape=jax.ShapeDtypeStruct((DIRS, cells, LANES), F32),
        in_specs=[VMEM_SPEC] * (2 * depth + 1) + [ANY_SPEC],
        out_specs=ANY_SPEC,
        input_output_aliases={2 * depth + 1: 0},
        scratch_shapes=[
            pltpu.VMEM((80, LANES), F32),
            pltpu.SemaphoreType.DMA,
        ],
        compiler_params=params(),
        cost_estimate=cost(10_000, 100_000),
        name="patch",
    )(*pin(*face_gots, pair_got, *gots[1:], tops), pops_out)
    return new_pops.reshape(populations.shape), new_conc.reshape(concentration.shape)


def solution(mesh):
    in_specs = (
        P(None, "wall", "lat", None),
        P("wall", None, "lat", None),
        P("wall", "lat", None),
        P(),
        P(),
        P(),
    )
    out_specs = (P(None, "wall", "lat", None), P("wall", None, "lat", None))
    return jax.shard_map(
        functools.partial(per_device, lats=mesh.shape["lat"], walls=mesh.shape["wall"]),
        mesh=mesh,
        in_specs=in_specs,
        out_specs=out_specs,
        check_vma=False,
    )
```
